32 devices in a mesh: img: 8 (over y, x, core), head: 4 (over z).
Axes of the slice: x: 2, y: 2, z: 4, core: 2. Of those that a mesh axis runs over, the one named last changes fastest.
Arguments:
- media: bfloat16 [64, 256, 1024], P('img'), may hold values from -6 to 6
- latents: bfloat16 [64, 64, 1024], P('img'), may hold values from -6 to 6
- counts: int32 [64], P('img'), may hold values from 32 to 256
- media_gain: float32 [1024], replicated, may hold values from 0.5 to 1.5
- media_bias: float32 [1024], replicated, may hold values from -1.5 to 1.5
- latent_gain: float32 [1024], replicated, may hold values from 0.5 to 1.5
- latent_bias: float32 [1024], replicated, may hold values from -1.5 to 1.5
- w_query: bfloat16 [1024, 512], P(None, 'head'), may hold values from -0.1875 to 0.1875
- w_key: bfloat16 [1024, 512], P(None, 'head'), may hold values from -0.1875 to 0.1875
- w_value: bfloat16 [1024, 512], P(None, 'head'), may hold values from -0.1875 to 0.1875
- w_out: bfloat16 [512, 1024], P('head'), may hold values from -2 to 2
- ff_gain: float32 [1024], replicated, may hold values from 0.5 to 1.5
- ff_bias: float32 [1024], replicated, may hold values from -1.5 to 1.5
- w_up: bfloat16 [4096, 1024], P(('img', 'head')), may hold values from -0.1875 to 0.1875
- w_down: bfloat16 [4096, 1024], P(('img', 'head')), may hold values from -0.09375 to 0.09375
- cotangent: bfloat16 [64, 64, 1024], P('img', 'head'), may hold values from -6 to 6
Outputs:
- latents_out: bfloat16 [64, 64, 1024], P('img', 'head')
- media_grad: bfloat16 [64, 256, 1024], P('img', 'head')
- latent_grad: bfloat16 [64, 64, 1024], P('img', 'head')
- media_gain_grad: float32 [1024], P(('img', 'head'))
- media_bias_grad: float32 [1024], P(('img', 'head'))
- latent_gain_grad: float32 [1024], P(('img', 'head'))
- latent_bias_grad: float32 [1024], P(('img', 'head'))
- w_query_grad: float32 [1024, 512], P('img', 'head')
- w_key_grad: float32 [1024, 512], P('img', 'head')
- w_value_grad: float32 [1024, 512], P('img', 'head')
- w_out_grad: float32 [512, 1024], P('head', 'img')
- ff_gain_grad: float32 [1024], P(('img', 'head'))
- ff_bias_grad: float32 [1024], P(('img', 'head'))
- w_up_grad: float32 [4096, 1024], P(('img', 'head'))
- w_down_grad: float32 [4096, 1024], P(('img', 'head'))
The draws below stay inside these ranges and needn't reach their ends.
Inputs may be any that keep to these rules, and one draw needn't show every extreme that they name: `counts`: patches of an image at or past its count are padding and are not keys.
All inputs are finite; a program needn't handle non-finite values.
Results may differ from the reference program's by a relative error of at most 0.019.
Values may be sent and summed in bfloat16 or wider, within the bound.
A program may use at most 192 MiB of HBM per device.

```python
import jax
import jax.numpy as jnp
from jax import lax

D = 1024
HEADS = 8
HS = 64
FF = 4096
LAT = 64
PATCHES = 256
IMG_DEV = 8
HD = 512
IMAGES = 64


def touch_ends(drawn, stream_key, least, largest):
    longest = drawn.shape.index(max(drawn.shape))
    spots = []
    for shift in (0, 1):
        where = [jax.random.randint(jax.random.fold_in(stream_key, axis), (), 0, length) for axis, length in enumerate(drawn.shape)]
        where[longest] = (where[longest] + shift) % drawn.shape[longest]
        spots.append(tuple(where))
    return drawn.at[spots[0]].set(least).at[spots[1]].set(largest)


def block_scale(key, extent, pieces, smallest, high):
    def one(dim, blocks):
        draws = jax.random.uniform(jax.random.fold_in(jax.random.fold_in(key, 6), dim), (blocks,), jnp.float32, smallest / len(pieces), high / len(pieces))
        return jnp.repeat(jnp.exp(draws), extent[dim] // blocks).reshape((-1,) + (1,) * (len(extent) - dim - 1))

    level = one(*pieces[0])
    for cut in pieces[1:]:
        level = level * one(*cut)
    return level


def gaussian(key, shape, width, reach, shards=(), kind=jnp.bfloat16):
    array = jax.random.normal(key, shape, jnp.float32) * width
    if len(shards) > 0:
        array = block_scale(key, shape, shards, -0.22, 0.18) * array
    return jnp.clip(array, min=-reach, max=reach).astype(kind)


def setup_inputs(seed: int = 0) -> dict:
    seeds = jax.random.split(jax.random.key(seed), 17)
    media = gaussian(seeds[0], (IMAGES, PATCHES, D), 1.0, 6.0, ((0, 8),))
    latents = gaussian(seeds[1], (IMAGES, LAT, D), 1.0, 6.0, ((0, 8),))
    counts = touch_ends(jax.random.randint(seeds[2], (IMAGES,), PATCHES // 8, PATCHES + 1), jax.random.fold_in(seeds[2], 1), PATCHES // 8, PATCHES).astype(jnp.int32)
    media_gain = jnp.clip(1.0 + 0.1 * jax.random.normal(seeds[3], (D,), jnp.float32), 0.5, 1.5)
    media_bias = gaussian(seeds[4], (D,), 0.3, 1.5, (), jnp.float32)
    latent_gain = jnp.clip(1.0 + 0.1 * jax.random.normal(seeds[5], (D,), jnp.float32), 0.5, 1.5)
    latent_bias = gaussian(seeds[6], (D,), 0.3, 1.5, (), jnp.float32)
    w_query = gaussian(seeds[7], (D, HD), D ** -0.5, 0.1875, ((1, 4),))
    w_key = gaussian(seeds[8], (D, HD), D ** -0.5, 0.1875, ((1, 4),))
    w_value = gaussian(seeds[9], (D, HD), D ** -0.5, 0.1875, ((1, 4),))
    w_out = gaussian(seeds[10], (HD, D), 8 ** -0.5, 2.0, ((0, 4),))
    ff_gain = jnp.clip(1.0 + 0.1 * jax.random.normal(seeds[11], (D,), jnp.float32), 0.5, 1.5)
    ff_bias = gaussian(seeds[12], (D,), 0.3, 1.5, (), jnp.float32)
    w_up = gaussian(seeds[13], (FF, D), D ** -0.5, 0.1875, ((0, 32),))
    w_down = gaussian(seeds[14], (FF, D), FF ** -0.5, 0.09375, ((0, 32),))
    cotangent = gaussian(seeds[15], (IMAGES, LAT, D), 1.0, 6.0, ((0, 8), (1, 4)))
    return dict(media=media, latents=latents, counts=counts, media_gain=media_gain, media_bias=media_bias, latent_gain=latent_gain, latent_bias=latent_bias, w_query=w_query, w_key=w_key, w_value=w_value, w_out=w_out, ff_gain=ff_gain, ff_bias=ff_bias, w_up=w_up, w_down=w_down, cotangent=cotangent)


PRECISE = lax.Precision.HIGHEST
EPSILON = 1e-05

@jax.custom_vjp
def low(v):
    return lax.optimization_barrier(v.astype(jnp.bfloat16)).astype(jnp.float32)

@jax.custom_vjp
def low_back(v):
    return v

def low_keep(v):
    return (low(v), None)

def low_pass(kept, grad):
    return (grad,)

def back_keep(v):
    return (v, None)

def back_low(kept, grad):
    return (low(grad),)
low.defvjp(low_keep, low_pass)
low_back.defvjp(back_keep, back_low)

def layer_norm(inputs, gain_vec, bias_vec):
    average = lax.optimization_barrier(jnp.mean(inputs, axis=-1, keepdims=True))
    centred = inputs - average
    variance = lax.optimization_barrier(jnp.mean(centred * centred, axis=-1, keepdims=True))
    return centred * lax.rsqrt(variance + EPSILON) * gain_vec + bias_vec

def layer(media_f, latents_f, count_vals, weights):
    media_gain, media_bias, latent_gain, latent_bias, w_query, w_key, w_value, w_out, ff_gain, ff_bias, w_up, w_down = weights
    group = media_f.shape[0]
    query_scale = HS ** (-0.5)
    media_n = low(layer_norm(media_f, media_gain, media_bias))
    latent_n = low(layer_norm(latents_f, latent_gain, latent_bias))
    keys_in = jnp.concatenate([media_n, latent_n], axis=1)
    query_proj = low_back(low(query_scale * jnp.einsum('gld,de->gle', latent_n, w_query, precision=PRECISE)))
    key_proj = low_back(low(jnp.einsum('gsd,de->gse', keys_in, w_key, precision=PRECISE)))
    value_proj = low_back(low(jnp.einsum('gsd,de->gse', keys_in, w_value, precision=PRECISE)))
    key_len = PATCHES + LAT
    query_heads = query_proj.reshape(group, LAT, HEADS, HS)
    key_heads = key_proj.reshape(group, key_len, HEADS, HS)
    value_heads = value_proj.reshape(group, key_len, HEADS, HS)
    scores = low_back(jnp.einsum('glhe,gshe->ghls', query_heads, key_heads, precision=PRECISE))
    positions = jnp.arange(key_len)
    is_valid = (positions[None, :] < count_vals[:, None]) | (positions[None, :] >= PATCHES)
    scores = jnp.where(is_valid[:, None, None, :], scores, -1e+30)
    probs = low(jax.nn.softmax(scores, axis=-1))
    attended = low_back(low(jnp.einsum('ghls,gshe->glhe', probs, value_heads, precision=PRECISE)))
    attended = attended.reshape(group, LAT, HEADS * HS)
    out_proj = low_back(jnp.einsum('gle,ed->gld', attended, w_out, precision=PRECISE))
    residual_mid = latents_f + out_proj
    ff_in = low(layer_norm(residual_mid, ff_gain, ff_bias))
    hidden = low_back(jnp.einsum('gld,fd->glf', ff_in, w_up, precision=PRECISE))
    activated = low(jax.nn.gelu(hidden, approximate=False))
    ff_out = low_back(jnp.einsum('glf,fd->gld', activated, w_down, precision=PRECISE))
    return residual_mid + ff_out

def reference(media, latents, counts, media_gain, media_bias, latent_gain, latent_bias, w_query, w_key, w_value, w_out, ff_gain, ff_bias, w_up, w_down, cotangent):
    groups = IMAGES // IMG_DEV
    weights = tuple((item.astype(jnp.float32) for item in (media_gain, media_bias, latent_gain, latent_bias, w_query, w_key, w_value, w_out, ff_gain, ff_bias, w_up, w_down)))
    media_f = media.astype(jnp.float32)
    latents_f = latents.astype(jnp.float32)

    def forward(media_in, latents_in, *params):

        def one_group(block):
            return layer(block[0], block[1], block[2], params)
        stacked = lax.map(jax.checkpoint(one_group), (media_in.reshape(groups, IMG_DEV, PATCHES, D), latents_in.reshape(groups, IMG_DEV, LAT, D), counts.reshape(groups, IMG_DEV)))
        return stacked.reshape(IMAGES, LAT, D)
    result, pullback = jax.vjp(forward, media_f, latents_f, *weights)
    grads = pullback(cotangent.astype(jnp.float32))
    return (result.astype(jnp.bfloat16), grads[0].astype(jnp.bfloat16), grads[1].astype(jnp.bfloat16), grads[2], grads[3], grads[4], grads[5], grads[6], grads[7], grads[8], grads[9], grads[10], grads[11], grads[12], grads[13])
```

```python
import math

import jax
import jax.numpy as jnp
from jax import lax
from jax.sharding import PartitionSpec as P

HS = 64


EPSILON = 1e-05


def layer_norm(inputs, gain_vec, bias_vec):
    average = jnp.mean(inputs, axis=-1, keepdims=True)
    centred = inputs - average
    variance = jnp.mean(centred * centred, axis=-1, keepdims=True)
    inv_std = lax.rsqrt(variance + EPSILON)
    normal_hat = centred * inv_std
    return (normal_hat * gain_vec + bias_vec, normal_hat, inv_std)


def norm_back(upstream, normal_hat, inv_std, gain_vec):
    scaled = upstream * gain_vec
    first = jnp.mean(scaled, axis=-1, keepdims=True)
    second = jnp.mean(scaled * normal_hat, axis=-1, keepdims=True)
    grad_input = inv_std * (scaled - first - normal_hat * second)
    row_axes = tuple(range(upstream.ndim - 1))
    return (
        grad_input,
        jnp.sum(upstream * normal_hat, axis=row_axes),
        jnp.sum(upstream, axis=row_axes),
    )


def gelu_parts(hidden):
    normal_cdf = 0.5 * (1.0 + lax.erf(hidden * (1.0 / math.sqrt(2.0))))
    density = jnp.exp(-0.5 * hidden * hidden) * (1.0 / math.sqrt(2.0 * math.pi))
    return (hidden * normal_cdf, normal_cdf + hidden * density)


def masked_scores(query_heads, key_heads, is_valid):
    scores = jnp.einsum(
        "glhe,gshe->ghls", query_heads, key_heads, preferred_element_type=jnp.float32
    )
    return jnp.where(is_valid[:, None, None, :], scores, -1e30)


def body(
    media,
    latents,
    counts,
    media_gain,
    media_bias,
    latent_gain,
    latent_bias,
    w_query,
    w_key,
    w_value,
    w_out,
    ff_gain,
    ff_bias,
    w_up,
    w_down,
    cotangent,
):
    images, patch_count, model_width = media.shape
    lat_count = latents.shape[1]
    head_parts = lax.axis_size("head")
    head_index = lax.axis_index("head")
    lat_rows = lat_count // head_parts
    patch_rows = patch_count // head_parts
    heads_here = w_query.shape[1] // HS
    query_scale = HS ** (-0.5)
    key_len = patch_count + lat_count
    media_f = media.astype(jnp.float32)
    latents_f = latents.astype(jnp.float32)
    media_norm, media_hat, media_std = layer_norm(media_f, media_gain, media_bias)
    latent_norm, latent_hat, latent_std = layer_norm(latents_f, latent_gain, latent_bias)
    media_n = media_norm.astype(jnp.bfloat16)
    latent_n = latent_norm.astype(jnp.bfloat16)
    keys_in = jnp.concatenate([media_n, latent_n], axis=1)
    query_proj = (
        query_scale
        * jnp.einsum("gld,de->gle", latent_n, w_query, preferred_element_type=jnp.float32)
    ).astype(jnp.bfloat16)
    key_proj = jnp.einsum("gsd,de->gse", keys_in, w_key, preferred_element_type=jnp.float32).astype(
        jnp.bfloat16
    )
    value_proj = jnp.einsum(
        "gsd,de->gse", keys_in, w_value, preferred_element_type=jnp.float32
    ).astype(jnp.bfloat16)
    query_heads = query_proj.reshape(images, lat_count, heads_here, HS)
    key_heads = key_proj.reshape(images, key_len, heads_here, HS)
    value_heads = value_proj.reshape(images, key_len, heads_here, HS)
    positions = jnp.arange(key_len)
    is_valid = (positions[None, :] < counts[:, None]) | (positions[None, :] >= patch_count)
    scores = masked_scores(query_heads, key_heads, is_valid)
    row_max = jnp.max(scores, axis=-1, keepdims=True)
    log_total = row_max + jnp.log(jnp.sum(jnp.exp(scores - row_max), axis=-1, keepdims=True))
    probs = jnp.exp(scores - log_total).astype(jnp.bfloat16)
    attended = jnp.einsum(
        "ghls,gshe->glhe", probs, value_heads, preferred_element_type=jnp.float32
    ).astype(jnp.bfloat16)
    attended = attended.reshape(images, lat_count, heads_here * HS)
    bf16 = jnp.bfloat16
    att_all = lax.all_gather(attended, "head", axis=2, tiled=True)
    w_out_all = lax.all_gather(w_out, "head", axis=0, tiled=True)
    cot_all = lax.all_gather(cotangent, "head", axis=1, tiled=True).reshape(-1, model_width)
    up_mat = lax.all_gather(w_up, "img", axis=0, tiled=True)
    down_mat = lax.all_gather(w_down, "img", axis=0, tiled=True)
    out_proj = jnp.einsum("gle,ed->gld", att_all, w_out_all, preferred_element_type=jnp.float32)
    mid_all = (latents_f + out_proj).reshape(-1, model_width)
    ff_norm, ff_hat, ff_std = layer_norm(mid_all, ff_gain, ff_bias)
    ff_in = ff_norm.astype(bf16)
    hidden = lax.dot_general(
        ff_in, up_mat, (((1,), (1,)), ((), ())), preferred_element_type=jnp.float32
    )
    activated, gelu_slope = gelu_parts(hidden)
    activated = activated.astype(bf16)
    ff_out = jnp.dot(activated, down_mat, preferred_element_type=jnp.float32)
    grad_act = lax.dot_general(
        cot_all, down_mat, (((1,), (1,)), ((), ())), preferred_element_type=jnp.float32
    )
    grad_hidden = (grad_act * gelu_slope).astype(bf16)
    grad_ff_in = jnp.dot(grad_hidden, up_mat, preferred_element_type=jnp.float32)
    grad_down = lax.dot_general(
        activated, cot_all, (((0,), (0,)), ((), ())), preferred_element_type=jnp.float32
    )
    grad_up = lax.dot_general(
        grad_hidden, ff_in, (((0,), (0,)), ((), ())), preferred_element_type=jnp.float32
    )
    ff_input_grad, grad_ff_gain, grad_ff_bias = norm_back(grad_ff_in, ff_hat, ff_std, ff_gain)
    mid_part = (cot_all.astype(jnp.float32) * (1.0 / head_parts) + ff_input_grad).astype(bf16)
    att_part = lax.dot_general(
        mid_part, w_out_all, (((1,), (1,)), ((), ())), preferred_element_type=jnp.float32
    ).astype(bf16)
    grad_attended = lax.psum_scatter(att_part, "head", scatter_dimension=1, tiled=True)
    pair = jnp.concatenate([ff_out.astype(bf16), mid_part], axis=1).reshape(
        images, lat_count, 2 * model_width
    )
    pair_sum = lax.psum_scatter(pair, "head", scatter_dimension=1, tiled=True).astype(jnp.float32)
    own_mid = lax.dynamic_slice_in_dim(
        mid_all.reshape(images, lat_count, model_width), head_index * lat_rows, lat_rows, 1
    )
    latents_out = (own_mid + pair_sum[..., :model_width]).astype(bf16)
    grad_mid = pair_sum[..., model_width:]
    grad_wout = jnp.einsum(
        "ne,nd->ed",
        att_all.reshape(-1, heads_here * HS * head_parts),
        mid_part,
        preferred_element_type=jnp.float32,
    ).astype(bf16)
    grad_attended = grad_attended.reshape(images, lat_count, heads_here, HS)
    scores_again = masked_scores(query_heads, key_heads, is_valid)
    probs_full = jnp.exp(scores_again - log_total)
    probs_low = probs_full.astype(jnp.bfloat16)
    grad_probs = jnp.einsum(
        "glhe,gshe->ghls", grad_attended, value_heads, preferred_element_type=jnp.float32
    )
    row_delta = jnp.sum(probs_full * grad_probs, axis=-1, keepdims=True)
    grad_scores = (probs_full * (grad_probs - row_delta)).astype(jnp.bfloat16)
    grad_value = jnp.einsum(
        "ghls,glhe->gshe", probs_low, grad_attended, preferred_element_type=jnp.float32
    ).astype(jnp.bfloat16)
    grad_key = jnp.einsum(
        "ghls,glhe->gshe", grad_scores, query_heads, preferred_element_type=jnp.float32
    ).astype(jnp.bfloat16)
    grad_query = (
        jnp.einsum(
            "ghls,gshe->glhe", grad_scores, key_heads, preferred_element_type=jnp.float32
        ).astype(jnp.bfloat16)
        * query_scale
    )
    grad_value = grad_value.reshape(images, key_len, heads_here * HS)
    grad_key = grad_key.reshape(images, key_len, heads_here * HS)
    grad_query = grad_query.reshape(images, lat_count, heads_here * HS)
    grad_wq = jnp.einsum("gld,gle->de", latent_n, grad_query, preferred_element_type=jnp.float32)
    grad_wk = jnp.einsum("gsd,gse->de", keys_in, grad_key, preferred_element_type=jnp.float32)
    grad_wv = jnp.einsum("gsd,gse->de", keys_in, grad_value, preferred_element_type=jnp.float32)
    wide = heads_here * HS
    own_grads = jnp.concatenate([grad_key, grad_value], axis=2)
    media_g = lax.all_to_all(own_grads[:, :patch_count], "head", 1, 2, tiled=True)
    latent_g = lax.all_to_all(
        jnp.concatenate([own_grads[:, patch_count:], grad_query], axis=2), "head", 1, 2, tiled=True
    )
    w_kv = lax.all_gather(jnp.concatenate([w_key, w_value], axis=1), "head", axis=1, tiled=True)
    w_kvq = lax.all_gather(
        jnp.concatenate([w_key, w_value, w_query], axis=1), "head", axis=1, tiled=True
    )
    grad_media_n = jnp.einsum("gse,de->gsd", media_g, w_kv, preferred_element_type=jnp.float32)
    grad_latent_n = jnp.einsum("gse,de->gsd", latent_g, w_kvq, preferred_element_type=jnp.float32)
    own_media_hat = lax.dynamic_slice_in_dim(media_hat, head_index * patch_rows, patch_rows, 1)
    own_media_std = lax.dynamic_slice_in_dim(media_std, head_index * patch_rows, patch_rows, 1)
    own_latent_hat = lax.dynamic_slice_in_dim(latent_hat, head_index * lat_rows, lat_rows, 1)
    own_latent_std = lax.dynamic_slice_in_dim(latent_std, head_index * lat_rows, lat_rows, 1)
    media_input_grad, grad_media_gain, grad_media_bias = norm_back(
        grad_media_n, own_media_hat, own_media_std, media_gain
    )
    latent_input_grad, grad_latent_gain, grad_latent_bias = norm_back(
        grad_latent_n, own_latent_hat, own_latent_std, latent_gain
    )
    media_grad = media_input_grad.astype(jnp.bfloat16)
    latent_grad = (grad_mid + latent_input_grad).astype(jnp.bfloat16)
    w_grad = jnp.concatenate([grad_wq, grad_wk, grad_wv], axis=1).astype(bf16)
    w_grad = lax.psum_scatter(w_grad, "img", scatter_dimension=0, tiled=True).astype(jnp.float32)
    wq_grad, wk_grad, wv_grad = (w_grad[:, k * wide : (k + 1) * wide] for k in range(3))
    wout_grad = lax.psum_scatter(grad_wout, "img", scatter_dimension=1, tiled=True)
    wout_grad = lax.psum_scatter(wout_grad, "head", scatter_dimension=0, tiled=True).astype(
        jnp.float32
    )
    ff_grads = jnp.concatenate([grad_up, grad_down], axis=1).astype(bf16)
    ff_grads = lax.psum_scatter(ff_grads, "img", scatter_dimension=0, tiled=True).astype(
        jnp.float32
    )
    up_grad, down_grad = ff_grads[:, :model_width], ff_grads[:, model_width:]
    vectors = jnp.stack(
        [
            grad_media_gain,
            grad_media_bias,
            grad_latent_gain,
            grad_latent_bias,
            grad_ff_gain,
            grad_ff_bias,
        ]
    )
    vectors = lax.psum(vectors, ("img", "head"))
    shard = model_width // (head_parts * lax.axis_size("img"))
    place = (lax.axis_index("img") * head_parts + head_index) * shard
    vectors = lax.dynamic_slice_in_dim(vectors, place, shard, 1)
    mgain_grad, mbias_grad, lgain_grad, lbias_grad, fgain_grad, fbias_grad = vectors
    return (
        latents_out,
        media_grad,
        latent_grad,
        mgain_grad,
        mbias_grad,
        lgain_grad,
        lbias_grad,
        wq_grad,
        wk_grad,
        wv_grad,
        wout_grad,
        fgain_grad,
        fbias_grad,
        up_grad,
        down_grad,
    )


def solution(mesh):
    return jax.shard_map(
        body,
        mesh=mesh,
        in_specs=(
            P("img", None, None),
            P("img", None, None),
            P("img"),
            P(),
            P(),
            P(),
            P(),
            P(None, "head"),
            P(None, "head"),
            P(None, "head"),
            P("head", None),
            P(),
            P(),
            P(("img", "head"), None),
            P(("img", "head"), None),
            P("img", "head", None),
        ),
        out_specs=(
            P("img", "head", None),
            P("img", "head", None),
            P("img", "head", None),
            P(("img", "head")),
            P(("img", "head")),
            P(("img", "head")),
            P(("img", "head")),
            P("img", "head"),
            P("img", "head"),
            P("img", "head"),
            P("head", "img"),
            P(("img", "head")),
            P(("img", "head")),
            P(("img", "head"), None),
            P(("img", "head"), None),
        ),
        check_vma=False,
    )
```

```python
import functools
import math

import jax
import jax.numpy as jnp
from jax import lax
from jax.experimental import pallas as pl
from jax.experimental.pallas import tpu as pltpu
from jax.sharding import PartitionSpec as P

HS = 64
EPSILON = 1e-05
LANES = 128
BF16 = jnp.bfloat16
F32 = jnp.float32
MESH = pl.DeviceIdType.MESH


def dot(a, b, dims):
    return lax.dot_general(a, b, (dims, ((), ())), preferred_element_type=F32)


NN = ((1,), (0,))
NT = ((1,), (1,))
TN = ((0,), (0,))


def normalize(x):
    width = x.shape[-1]
    centred = x - jnp.sum(x, axis=-1, keepdims=True) * (1.0 / width)
    variance = jnp.sum(centred * centred, axis=-1, keepdims=True) * (1.0 / width)
    inv_std = lax.rsqrt(variance + EPSILON)
    return centred * inv_std, inv_std


def norm_back(upstream, hat, inv_std, gain):
    width = upstream.shape[-1]
    scaled = upstream * gain
    first = jnp.sum(scaled, axis=-1, keepdims=True) * (1.0 / width)
    second = jnp.sum(scaled * hat, axis=-1, keepdims=True) * (1.0 / width)
    return inv_std * (scaled - first - hat * second)


def fold_rows(x):
    return jnp.sum(x.reshape(x.shape[0] // 8, 8, x.shape[1]), axis=0)


def gelu_parts(hidden):
    normal_cdf = 0.5 * (1.0 + lax.erf(hidden * (1.0 / math.sqrt(2.0))))
    density = jnp.exp(-0.5 * hidden * hidden) * (1.0 / math.sqrt(2.0 * math.pi))
    return (hidden * normal_cdf, normal_cdf + hidden * density)


def layout(ni, nh, media, latents, w_query, w_up):
    G, S, D = media.shape
    L = latents.shape[1]
    W = w_query.shape[1]
    FU = w_up.shape[0]
    z = dict(G=G, S=S, D=D, L=L, W=W, FU=FU, T=S + L, SR=S // nh, LR=L // nh)
    z.update(R=G * L, FH=ni * FU, RC=D // ni, NK=ni // 2, HN=W // HS)
    T, SR, LR, R, FH, RC, NK = (z[k] for k in ("T", "SR", "LR", "R", "FH", "RC", "NK"))
    vm = {
        "media_b": ((2, S, D), BF16),
        "media_o": ((G, SR, D), BF16),
        "lat": ((G, L, D), BF16),
        "keys": ((G * T, D), BF16),
        "lat_n": ((R, D), BF16),
        "wkv_o": ((D, 2 * W), BF16),
        "wq_o": ((D, W), BF16),
        "wkv_f": ((D, nh * 2 * W), BF16),
        "wq_f": ((D, nh * W), BF16),
        "wout_f": ((nh * W, D), BF16),
        "up_f": ((FH, D), BF16),
        "down_f": ((FH, D), BF16),
        "cot_f": ((G, L, D), BF16),
        "kv": ((G * T, 2 * W), BF16),
        "q": ((R, W), BF16),
        "probs": ((G * T, z["HN"] * L), F32),
        "att_f": ((G, L, nh * W), BF16),
        "mid_o": ((G, LR, D), F32),
        "hat": ((R, D), F32),
        "inv": ((R, LANES), F32),
        "ff_in": ((R, D), BF16),
        "act": ((R, FH), BF16),
        "slope": ((R, FH), F32),
        "gh": ((R, FH), BF16),
        "tmp": ((R // 2, max(D, FH)), F32),
        "ffo_p": ((G, L, D), BF16),
        "gm_p": ((G, L, D), BF16),
        "ga_p": ((G, L, nh * W), BF16),
        "ffo_r": ((nh, G, LR, D), BF16),
        "gm_r": ((nh, G, LR, D), BF16),
        "ga_r": ((nh, G, L, W), BF16),
        "gkv": ((G, T, 2 * W), BF16),
        "gq": ((G, L, W), BF16),
        "gkv_r": ((G, SR + LR, nh * 2 * W), BF16),
        "gq_r": ((G, LR, nh * W), BF16),
        "wu": ((FH, D), BF16),
        "wd": ((FH, D), BF16),
        "wo": ((D, nh * W), BF16),
        "wa": ((D, 3 * W), BF16),
        "wu1": ((NK * FU, D), BF16),
        "wd1": ((NK * FU, D), BF16),
        "wo1": ((NK * RC, nh * W), BF16),
        "wa1": ((NK * RC, 3 * W), BF16),
        "wu2": ((NK * FU, D), BF16),
        "wd2": ((NK * FU, D), BF16),
        "wo2": ((NK * RC, nh * W), BF16),
        "wa2": ((NK * RC, 3 * W), BF16),
        "wo_s": ((nh, RC, W), BF16),
        "wo_z": ((nh, RC, W), BF16),
        "glat": ((G, LR, D), F32),
        "vacc": ((6, 8, D), F32),
        "vec": ((8, D), F32),
        "vec_r": ((ni, 8, LANES), F32),
        "vec_t": ((8, LANES), F32),
        "vec_z": ((nh, 8, LANES), F32),
        "o_lat": ((G, LR, D), BF16),
        "o_mg": ((G, SR, D), BF16),
        "o_lg": ((G, LR, D), BF16),
        "o_up": ((FU, D), F32),
        "o_dn": ((FU, D), F32),
        "o_wa": ((RC, 3 * W), F32),
        "o_wo": ((RC, W), F32),
        "o_vec": ((8, LANES), F32),
    }
    z["vm"] = vm
    return z


RECV = (
    ("wout_z", 1), ("wout_p", 1), ("up_p", 1), ("up_x", 1), ("up_y", 1), ("dn_p", 1), ("dn_x", 1),
    ("dn_y", 1), ("kv_z", 1), ("kv_p", 1), ("kv_x", 1), ("kv_y", 1), ("cot", 1), ("att", 0),
    ("ga", 0), ("ffo", 1), ("gm", 1), ("gkv", 0), ("gq", 1), ("wu1", 1), ("wu2", 1), ("wd1", 1),
    ("wd2", 1), ("wo1", 1), ("wo2", 1), ("wo3", 1), ("wa1", 1), ("wa2", 1), ("vp", 1), ("vz", 1),
)
DONE = ("lat", "mg", "lg", "up", "dn", "wa", "wo", "vec")
LOCAL = ("m0", "m1", "w", "lat", "ff", "kvq", "mo") + DONE
INS = (
    "counts", "gm", "bm", "gl", "bl", "gf", "bf", "media", "latents", "w_query", "w_key", "w_value",
    "w_out", "w_up", "w_down", "cot",
)
SIZES = ("G", "S", "D", "L", "W", "FU", "T", "SR", "LR", "R", "FH", "RC", "NK", "HN")
OUTS = ("y_lat", "y_mg", "y_lg", "y_wa", "y_wo", "y_up", "y_dn", "y_vec")


def kernel(ni, nh, z, *refs):
    names = INS + OUTS + tuple(z["vm"]) + ("rsem", "ssem", "lsem")
    r = dict(zip(names, refs, strict=True))
    G, S, D, L, W, FU, T, SR, LR, R, FH, RC, NK, HN = (z[k] for k in SIZES)
    index, count = {}, 0
    for name, n in RECV:
        index[name] = count
        count += n if n else G
    me_i, me_h = lax.axis_index("img"), lax.axis_index("head")
    par, half = lax.rem(me_i, 2), lax.div(me_i, 2)
    mate = me_i + 1 - 2 * par
    counts = r["counts"]
    total_sent = {}

    def rsem(name, k=0):
        return r["rsem"].at[index[name] + k]

    def ssem(name):
        return r["ssem"].at[[n for n, _ in RECV].index(name)]

    def lsem(name):
        return r["lsem"].at[LOCAL.index(name)]

    def size(ref):
        return math.prod(ref.shape) * jnp.dtype(ref.dtype).itemsize

    def await_bytes(sem, nbytes):
        lanes = D
        while nbytes % (2 * lanes * 16):
            lanes //= 2
        assert lanes >= LANES and nbytes // (2 * lanes) <= G * T
        view = r["keys"].at[pl.ds(0, nbytes // (2 * lanes)), pl.ds(0, lanes)]
        pltpu.make_async_copy(view, view, sem).wait()

    def load(src, dst, name):
        pltpu.make_async_copy(src, dst, lsem(name)).start()

    def send(src, dst, name, img, head, k=0, times=1):
        pltpu.make_async_remote_copy(
            src_ref=src,
            dst_ref=dst,
            send_sem=ssem(name),
            recv_sem=rsem(name, k),
            device_id=(img, head),
            device_id_type=MESH,
        ).start()
        total_sent[name] = total_sent.get(name, 0) + size(src) * times

    def rows_of(i, n):
        return pl.ds(pl.multiple_of(i * n, n), n)

    heads = [lax.rem(me_h + d, nh) for d in range(1, nh)]

    def to_heads(f):
        for other in heads:
            f(other)

    def twin(k):
        return lax.rem(half + k, NK) * 2 + par

    def to_twins(f):
        def step(k, c):
            f(twin(k))
            return c

        lax.fori_loop(1, NK, step, 0)

    load(r["media"].at[0], r["media_b"].at[0], "m0")
    load(r["w_key"], r["wkv_o"].at[:, pl.ds(0, W)], "w")
    load(r["w_value"], r["wkv_o"].at[:, pl.ds(W, W)], "w")
    load(r["w_query"], r["wq_o"], "w")
    load(r["latents"], r["lat"], "lat")
    load(r["media"].at[1], r["media_b"].at[1], "m1")
    barrier = pltpu.get_barrier_semaphore()
    to_heads(
        lambda o: pl.semaphore_signal(
            barrier, inc=1, device_id=(me_i, o), device_id_type=MESH
        )
    )

    def greet(k, c):
        other = lax.rem(me_i + k, ni)
        pl.semaphore_signal(barrier, inc=1, device_id=(other, me_h), device_id_type=MESH)
        return c

    lax.fori_loop(1, ni, greet, 0)
    pl.semaphore_wait(barrier, nh - 1 + ni - 1)

    hw = W // 2
    wo_part = pl.ds(pl.multiple_of(me_h * W + par * hw, hw), hw)
    to_heads(
        lambda o: send(
            r["w_out"].at[rows_of(par, hw)], r["wout_f"].at[wo_part], "wout_z", me_i, o
        )
    )
    own_f = rows_of(me_i, FU)
    for src, dst, tag in (("w_up", "up_f", "up"), ("w_down", "down_f", "dn")):
        to_twins(
            lambda o, src=src, dst=dst, tag=tag: send(
                r[src], r[dst].at[own_f], tag + "_x", o, me_h, times=NK - 1
            )
        )
        send(r[src], r[dst].at[own_f], tag + "_p", mate, me_h)
    load(r["w_out"], r["wout_f"].at[rows_of(me_h, W)], "ff")
    load(r["w_up"], r["up_f"].at[own_f], "ff")
    load(r["w_down"], r["down_f"].at[own_f], "ff")
    load(r["cot"], r["cot_f"].at[:, rows_of(me_h, LR), :], "ff")
    own_kv = [pl.ds(pl.multiple_of(me_h * 2 * W + k * W, W), W) for k in range(2)]
    own_w = rows_of(me_h, W)
    own_c = rows_of(me_i, RC)
    load(r["w_key"].at[own_c], r["wkv_f"].at[own_c, own_kv[0]], "kvq")
    load(r["w_value"].at[own_c], r["wkv_f"].at[own_c, own_kv[1]], "kvq")
    load(r["w_query"].at[own_c], r["wq_f"].at[own_c, own_w], "kvq")
    load(r["media"].at[:, rows_of(me_h, SR), :], r["media_o"], "mo")

    gain_m, bias_m = r["gm"][...], r["bm"][...]
    gain_l, bias_l = r["gl"][...], r["bl"][...]
    gain_f, bias_f = r["gf"][...], r["bf"][...]
    NB = 32
    lane_head = lax.div(lax.broadcasted_iota(jnp.int32, (L, W), 1), HS)

    def spread(x):
        zero = jnp.zeros_like(x)
        return jnp.concatenate([jnp.where(lane_head == k, x, zero) for k in range(HN)], axis=0)

    def gather_diag(x):
        out = x[:L]
        for k in range(1, HN):
            out = jnp.where(lane_head == k, x[k * L : (k + 1) * L], out)
        return out

    await_bytes(lsem("w"), 3 * D * W * 2)
    await_bytes(lsem("lat"), G * L * D * 2)

    def relay(tag, buf, n):
        await_bytes(rsem(tag + "_x"), (NK - 1) * size(buf.at[rows_of(0, n)]))
        to_twins(
            lambda o: send(
                buf.at[rows_of(o, n)], buf.at[rows_of(o, n)], tag + "_y", mate, me_h, times=NK - 1
            )
        )

    def relay_wout():
        await_bytes(rsem("wout_z"), (nh - 1) * hw * D * 2)

        def pass_on(o):
            part = pl.ds(pl.multiple_of(o * W + par * hw, hw), hw)
            send(r["wout_f"].at[part], r["wout_f"].at[part], "wout_p", mate, me_h)

        to_heads(pass_on)

    def image(g, c):
        slot = lax.rem(g, 2)
        for k in range(2):

            @pl.when(slot == k)
            def _():
                await_bytes(lsem("m0" if k == 0 else "m1"), S * D * 2)

        def norm_media(b, c):
            x = r["media_b"][slot, pl.ds(pl.multiple_of(b * NB, NB), NB), :].astype(F32)
            hat, _ = normalize(x)
            at = pl.ds(pl.multiple_of(g * T + b * NB, NB), NB)
            r["keys"][at, :] = (hat * gain_m + bias_m).astype(BF16)
            return c

        lax.fori_loop(0, S // NB, norm_media, 0)

        def norm_latent(b, c):
            x = r["lat"][g, pl.ds(pl.multiple_of(b * NB, NB), NB), :].astype(F32)
            hat, _ = normalize(x)
            y = (hat * gain_l + bias_l).astype(BF16)
            r["keys"][pl.ds(pl.multiple_of(g * T + S + b * NB, NB), NB), :] = y
            r["lat_n"][pl.ds(pl.multiple_of(g * L + b * NB, NB), NB), :] = y
            return c

        lax.fori_loop(0, L // NB, norm_latent, 0)
        for k in range(2):

            @pl.when((slot == k) & (g + 2 < G))
            def _():
                load(r["media"].at[g + 2], r["media_b"].at[k], "m0" if k == 0 else "m1")

        rows = pl.ds(pl.multiple_of(g * T, T), T)
        lat_rows = pl.ds(pl.multiple_of(g * L, L), L)
        kv = dot(r["keys"][rows, :], r["wkv_o"][...], NN).astype(BF16)
        r["kv"][rows, :] = kv
        q = (dot(r["lat_n"][lat_rows, :], r["wq_o"][...], NN) * (HS**-0.5)).astype(BF16)
        r["q"][lat_rows, :] = q
        scores = dot(kv[:, :W], spread(q), NT)
        place = lax.broadcasted_iota(jnp.int32, scores.shape, 0)
        scores = jnp.where((place < counts[g]) | (place >= S), scores, -1e30)
        top = jnp.max(scores, axis=0, keepdims=True)
        total = jnp.sum(jnp.exp(scores - top), axis=0, keepdims=True)
        probs = jnp.exp(scores - (top + jnp.log(total)))
        r["probs"][rows, :] = probs
        att = gather_diag(dot(probs.astype(BF16), kv[:, W:], TN)).astype(BF16)
        r["att_f"][g, :, own_w] = att
        to_heads(
            lambda o: send(
                r["att_f"].at[g, :, own_w], r["att_f"].at[g, :, own_w], "att", me_i, o, g, times=G
            )
        )

        @pl.when(g == 3)
        def _():
            relay_wout()

        @pl.when(g == G - 2)
        def _():
            relay("up", r["up_f"], FU)

        return c

    lax.fori_loop(0, G, image, 0)
    own_l = rows_of(me_h, LR)
    to_heads(lambda o: send(r["cot"], r["cot_f"].at[:, own_l, :], "cot", me_i, o))

    def send_kvq(o):
        send(r["w_key"].at[own_c], r["wkv_f"].at[own_c, own_kv[0]], "kv_z", me_i, o)
        send(r["w_value"].at[own_c], r["wkv_f"].at[own_c, own_kv[1]], "kv_z", me_i, o)
        send(r["w_query"].at[own_c], r["wq_f"].at[own_c, own_w], "kv_z", me_i, o)

    to_heads(send_kvq)
    r["vacc"][...] = jnp.zeros_like(r["vacc"])

    CR = R // 2
    CG = G // 2
    await_bytes(lsem("ff"), (W + 2 * FU + G * LR) * D * 2)
    await_bytes(rsem("wout_p"), (nh - 1) * hw * D * 2)

    def ff_forward(b, c):
        for k in range(CG):
            await_bytes(rsem("att", b * CG + k), (nh - 1) * L * W * 2)
        at = pl.ds(pl.multiple_of(b * CR, CR), CR)
        att = r["att_f"][pl.ds(b * CG, CG), :, :].reshape(CR, nh * W)
        r["tmp"][:, :D] = dot(att, r["wout_f"][...], NN)

        def norm(k, c):
            here = pl.ds(pl.multiple_of(k * LR, LR), LR)
            row = pl.ds(pl.multiple_of(b * CR + k * LR, LR), LR)
            g, piece = b * CG + lax.div(k, nh), lax.rem(k, nh)
            x = r["tmp"][here, :D] + r["lat"][g, rows_of(piece, LR), :].astype(F32)
            hat, inv = normalize(x)

            @pl.when(piece == me_h)
            def _():
                r["mid_o"][g] = x

            r["hat"][row, :] = hat
            r["inv"][row, :] = jnp.broadcast_to(inv, (LR, LANES))
            r["ff_in"][row, :] = (hat * gain_f + bias_f).astype(BF16)
            return c

        lax.fori_loop(0, CR // LR, norm, 0)

        @pl.when(b == 0)
        def _():
            await_bytes(rsem("up_p"), FU * D * 2)
            await_bytes(rsem("up_y"), (NK - 1) * FU * D * 2)

        r["tmp"][:, :FH] = dot(r["ff_in"][at, :], r["up_f"][...], NT)

        def gelu(k, c):
            here = pl.ds(pl.multiple_of(k * 16, 16), 16)
            row = pl.ds(pl.multiple_of(b * CR + k * 16, 16), 16)
            value, slope = gelu_parts(r["tmp"][here, :FH])
            r["act"][row, :] = value.astype(BF16)
            r["slope"][row, :] = slope
            return c

        lax.fori_loop(0, CR // 16, gelu, 0)
        return c

    lax.fori_loop(0, 2, ff_forward, 0)
    relay("dn", r["down_f"], FU)
    await_bytes(rsem("dn_p"), FU * D * 2)
    await_bytes(rsem("dn_y"), (NK - 1) * FU * D * 2)

    await_bytes(rsem("cot"), (nh - 1) * G * LR * D * 2)

    def ff_backward(b, c):
        at = pl.ds(pl.multiple_of(b * CR, CR), CR)
        imgs = pl.ds(b * CG, CG)
        cot = r["cot_f"][imgs, :, :].reshape(CR, D)
        r["tmp"][:, :FH] = dot(cot, r["down_f"][...], NT)

        def slope(k, c):
            here = pl.ds(pl.multiple_of(k * 16, 16), 16)
            row = pl.ds(pl.multiple_of(b * CR + k * 16, 16), 16)
            r["gh"][row, :] = (r["tmp"][here, :FH] * r["slope"][row, :]).astype(BF16)
            return c

        lax.fori_loop(0, CR // 16, slope, 0)
        r["tmp"][:, :D] = dot(r["gh"][at, :], r["up_f"][...], NN)

        def norm(k, c):
            here = pl.ds(pl.multiple_of(k * LR, LR), LR)
            row = pl.ds(pl.multiple_of(b * CR + k * LR, LR), LR)
            g, piece = b * CG + lax.div(k, nh), lax.rem(k, nh)
            u = r["tmp"][here, :D]
            hat = r["hat"][row, :]
            grad = norm_back(u, hat, r["inv"][row, :1], gain_f)
            part = rows_of(piece, LR)
            cot = r["cot_f"][g, part, :].astype(F32) * (1.0 / nh)
            r["gm_p"][g, part, :] = (grad + cot).astype(BF16)
            r["vacc"][4] += fold_rows(u * hat)
            r["vacc"][5] += fold_rows(u)
            return c

        lax.fori_loop(0, CR // LR, norm, 0)
        ga = dot(r["gm_p"][imgs, :, :].reshape(CR, D), r["wout_f"][...], NT)
        r["ga_p"][imgs, :, :] = ga.astype(BF16).reshape(CG, L, nh * W)
        to_heads(
            lambda o: send(
                r["ga_p"].at[imgs, :, rows_of(o, W)], r["ga_r"].at[me_h, imgs], "ga", me_i, o, b,
                times=2,
            )
        )
        return c

    lax.fori_loop(0, 2, ff_backward, 0)

    def ff_out(b, c):
        at = pl.ds(pl.multiple_of(b * CR, CR), CR)
        out = dot(r["act"][at, :], r["down_f"][...], NN)
        r["ffo_p"][pl.ds(b * CG, CG), :, :] = out.astype(BF16).reshape(CG, L, D)
        return c

    lax.fori_loop(0, 2, ff_out, 0)

    def scatter_pair(buf, first, n, tag):
        def step(k, c):
            send(
                buf.at[rows_of(2 * k + 1 - par, n)], first.at[rows_of(k, n)], tag + "1", mate,
                me_h, times=NK,
            )
            return c

        lax.fori_loop(0, NK, step, 0)

    def scatter_twins(buf, first, second, n, tag):
        await_bytes(rsem(tag + "1"), size(first))

        def step(d, c):
            k = lax.rem(half + d, NK)
            mine, got = rows_of(2 * k + par, n), rows_of(k, n)
            both = buf[mine, :].astype(F32) + first[got, :].astype(F32)
            buf[mine, :] = both.astype(BF16)
            send(
                buf.at[mine], second.at[rows_of(half, n)], tag + "2", 2 * k + par, me_h,
                times=NK - 1,
            )
            return c

        lax.fori_loop(1, NK, step, 0)

    def scatter_sum(buf, first, second, n, tag, out):
        await_bytes(rsem(tag + "2"), size(second) // NK * (NK - 1))
        out[...] = buf[rows_of(me_i, n), :].astype(F32) + first[rows_of(half, n), :].astype(F32)

        def step(d, c):
            out[...] += second[rows_of(lax.rem(half + d, NK), n), :].astype(F32)
            return c

        lax.fori_loop(1, NK, step, 0)

    FT = 2 * LANES
    cot_all = r["cot_f"].reshape(R, D)
    gm_all = r["gm_p"].reshape(R, D)
    att_all = r["att_f"].reshape(R, nh * W)

    def down_grad(t, c):
        at = pl.ds(pl.multiple_of(t * FT, FT), FT)
        r["wd"][at, :] = dot(r["act"][:, at], cot_all[...], TN).astype(BF16)
        return c

    lax.fori_loop(0, FH // FT, down_grad, 0)
    scatter_pair(r["wd"], r["wd1"], FU, "wd")

    def up_grad(t, c):
        at = pl.ds(pl.multiple_of(t * FT, FT), FT)
        r["wu"][at, :] = dot(r["gh"][:, at], r["ff_in"][...], TN).astype(BF16)
        return c

    lax.fori_loop(0, FH // FT, up_grad, 0)
    scatter_pair(r["wu"], r["wu1"], FU, "wu")

    def out_grad(t, c):
        at = pl.ds(pl.multiple_of(t * FT, FT), FT)
        r["wo"][at, :] = dot(gm_all[:, at], att_all[...], TN).astype(BF16)
        return c

    lax.fori_loop(0, D // FT, out_grad, 0)
    scatter_pair(r["wo"], r["wo1"], RC, "wo")

    for b in range(2):
        await_bytes(rsem("ga", b), (nh - 1) * CG * L * W * 2)

    def image_back(g, c):
        rows = pl.ds(pl.multiple_of(g * T, T), T)
        lat_rows = pl.ds(pl.multiple_of(g * L, L), L)
        ga = r["ga_p"][g, :, own_w].astype(F32)
        for o in heads:
            ga = ga + r["ga_r"][o, g].astype(F32)
        ga = spread(ga.astype(BF16))
        q = spread(r["q"][lat_rows, :])
        key, value = r["kv"][rows, :W], r["kv"][rows, W:]
        probs = r["probs"][rows, :]
        grad_probs = dot(value, ga, NT)
        delta = jnp.sum(probs * grad_probs, axis=0, keepdims=True)
        grad_scores = (probs * (grad_probs - delta)).astype(BF16)
        grad_value = dot(probs.astype(BF16), ga, NN).astype(BF16)
        grad_key = dot(grad_scores, q, NN).astype(BF16)
        r["gkv"][g, :, :W] = grad_key
        r["gkv"][g, :, W:] = grad_value
        grad_query = gather_diag(dot(grad_scores, key, TN)).astype(BF16)
        r["gq"][g] = (grad_query.astype(F32) * (HS**-0.5)).astype(BF16)
        wide = rows_of(me_h, 2 * W)

        def out(o):
            send(
                r["gkv"].at[g, rows_of(o, SR), :], r["gkv_r"].at[g, pl.ds(0, SR), wide], "gkv",
                me_i, o, g, times=G,
            )
            lat_at = pl.ds(pl.multiple_of(S + o * LR, LR), LR)
            send(
                r["gkv"].at[g, lat_at, :], r["gkv_r"].at[g, pl.ds(SR, LR), wide], "gkv", me_i, o,
                g, times=G,
            )
            send(
                r["gq"].at[g, rows_of(o, LR), :], r["gq_r"].at[g, :, own_w], "gq", me_i, o,
                times=G,
            )

        to_heads(out)
        r["gkv_r"][g, :SR, wide] = r["gkv"][g, rows_of(me_h, SR), :]
        own_at = pl.ds(pl.multiple_of(S + me_h * LR, LR), LR)
        r["gkv_r"][g, SR:, wide] = r["gkv"][g, own_at, :]
        r["gq_r"][g, :, own_w] = r["gq"][g, own_l, :]
        return c

    lax.fori_loop(0, G, image_back, 0)
    to_heads(
        lambda o: send(r["ffo_p"].at[:, rows_of(o, LR), :], r["ffo_r"].at[me_h], "ffo", me_i, o)
    )
    to_heads(
        lambda o: send(r["gm_p"].at[:, rows_of(o, LR), :], r["gm_r"].at[me_h], "gm", me_i, o)
    )
    scatter_twins(r["wd"], r["wd1"], r["wd2"], FU, "wd")
    scatter_twins(r["wu"], r["wu1"], r["wu2"], FU, "wu")
    scatter_twins(r["wo"], r["wo1"], r["wo2"], RC, "wo")

    def share_kvq(o, tag, times):
        for buf in (r["wkv_f"], r["wq_f"]):
            send(buf.at[own_c], buf.at[own_c], tag, o, me_h, times=times)

    def relay_kvq(o):
        for buf in (r["wkv_f"], r["wq_f"]):
            send(buf.at[rows_of(o, RC)], buf.at[rows_of(o, RC)], "kv_y", mate, me_h, times=NK - 1)

    await_bytes(lsem("kvq"), 3 * RC * W * 2)
    await_bytes(rsem("kv_z"), (nh - 1) * 3 * RC * W * 2)
    to_twins(lambda o: share_kvq(o, "kv_x", NK - 1))
    share_kvq(mate, "kv_p", 1)

    gkv_all = r["gkv"].reshape(G * T, 2 * W)
    gq_all = r["gq"].reshape(R, W)

    def proj_grad(t, c):
        at = pl.ds(pl.multiple_of(t * FT, FT), FT)
        r["wa"][at, : 2 * W] = dot(r["keys"][:, at], gkv_all[...], TN).astype(BF16)
        r["wa"][at, 2 * W :] = dot(r["lat_n"][:, at], gq_all[...], TN).astype(BF16)
        return c

    lax.fori_loop(0, D // FT, proj_grad, 0)
    scatter_pair(r["wa"], r["wa1"], RC, "wa")
    await_bytes(rsem("kv_x"), (NK - 1) * 3 * nh * RC * W * 2)
    to_twins(relay_kvq)
    scatter_twins(r["wa"], r["wa1"], r["wa2"], RC, "wa")
    await_bytes(rsem("kv_p"), 3 * nh * RC * W * 2)
    await_bytes(rsem("kv_y"), (NK - 1) * 3 * nh * RC * W * 2)

    await_bytes(lsem("mo"), G * SR * D * 2)
    await_bytes(rsem("gq"), (nh - 1) * G * LR * W * 2)
    KR = SR + LR

    def own_rows(b, c):
        for k in range(2):
            await_bytes(rsem("gkv", 2 * b + k), (nh - 1) * KR * 2 * W * 2)
        two = pl.ds(2 * b, 2)
        wide = r["gkv_r"][two, :, :].reshape(2 * KR, nh * 2 * W)
        r["tmp"][: 2 * KR, :D] = dot(wide, r["wkv_f"][...], NT)
        query = dot(r["gq_r"][two, :, :].reshape(2 * LR, nh * W), r["wq_f"][...], NT)
        for k in range(2):
            at = pl.ds(k * KR + SR, LR)
            r["tmp"][at, :D] += query[k * LR : (k + 1) * LR]

        def rows(j, c):
            g = 2 * b + lax.div(j, SR // LR)
            piece = rows_of(lax.rem(j, SR // LR), LR)
            at = pl.ds(
                pl.multiple_of(lax.div(j, SR // LR) * KR + lax.rem(j, SR // LR) * LR, LR), LR
            )
            u = r["tmp"][at, :D]
            hat, inv = normalize(r["media_o"][g, piece, :].astype(F32))
            r["o_mg"][g, piece, :] = norm_back(u, hat, inv, gain_m).astype(BF16)
            r["vacc"][0] += fold_rows(u * hat)
            r["vacc"][1] += fold_rows(u)
            return c

        lax.fori_loop(0, 2 * SR // LR, rows, 0)
        for k in range(2):
            g = 2 * b + k
            u = r["tmp"][k * KR + SR : (k + 1) * KR, :D]
            hat, inv = normalize(r["lat"][g, own_l, :].astype(F32))
            r["glat"][g] = norm_back(u, hat, inv, gain_l)
            r["vacc"][2] += fold_rows(u * hat)
            r["vacc"][3] += fold_rows(u)
        pltpu.make_async_copy(r["o_mg"].at[two], r["y_mg"].at[two], lsem("mg")).start()
        return c

    lax.fori_loop(0, G // 2, own_rows, 0)

    for k in range(6):
        r["vec"][k : k + 1, :] = jnp.sum(r["vacc"][k], axis=0, keepdims=True)
    r["vec"][6:8, :] = jnp.zeros((2, D), F32)

    def block(i):
        return pl.ds(pl.multiple_of(lax.div(i * RC, LANES) * LANES, LANES), LANES)

    def vec_step(k, c):
        o = lax.rem(me_i + k, ni)
        send(r["vec"].at[:, block(o)], r["vec_r"].at[me_i], "vp", o, me_h, times=ni - 1)
        return c

    lax.fori_loop(1, ni, vec_step, 0)

    def put(name):
        pltpu.make_async_copy(r["o_" + name], r["y_" + name], lsem(name)).start()

    scatter_sum(r["wd"], r["wd1"], r["wd2"], FU, "wd", r["o_dn"])
    put("dn")
    scatter_sum(r["wu"], r["wu1"], r["wu2"], FU, "wu", r["o_up"])
    put("up")
    scatter_sum(r["wo"], r["wo1"], r["wo2"], RC, "wo", r["tmp"].at[:RC, : nh * W])
    for k in range(nh):
        r["wo_s"][k] = r["tmp"][:RC, k * W : (k + 1) * W].astype(BF16)
    to_heads(lambda o: send(r["wo_s"].at[o], r["wo_z"].at[me_h], "wo3", me_i, o))
    scatter_sum(r["wa"], r["wa1"], r["wa2"], RC, "wa", r["o_wa"])
    put("wa")
    await_bytes(rsem("vp"), (ni - 1) * 8 * LANES * 4)
    r["vec_t"][...] = r["vec"][:, block(me_i)]

    def vec_sum(k, c):
        r["vec_t"][...] += r["vec_r"][lax.rem(me_i + k, ni)]
        return c

    lax.fori_loop(1, ni, vec_sum, 0)
    to_heads(lambda o: send(r["vec_t"], r["vec_z"].at[me_h], "vz", me_i, o))
    await_bytes(rsem("wo3"), (nh - 1) * RC * W * 2)
    total = r["tmp"][:RC, own_w]
    for o in heads:
        total = total + r["wo_z"][o].astype(F32)
    r["o_wo"][...] = total
    put("wo")

    await_bytes(rsem("ffo"), (nh - 1) * G * LR * D * 2)

    def out_rows(g, c):
        out = r["mid_o"][g] + r["ffo_p"][g, own_l, :].astype(F32)
        for o in heads:
            out = out + r["ffo_r"][o, g].astype(F32)
        r["o_lat"][g] = out.astype(BF16)
        return c

    lax.fori_loop(0, G, out_rows, 0)
    put("lat")
    await_bytes(rsem("gm"), (nh - 1) * G * LR * D * 2)

    def grad_rows(g, c):
        out = r["glat"][g] + r["gm_p"][g, own_l, :].astype(F32)
        for o in heads:
            out = out + r["gm_r"][o, g].astype(F32)
        r["o_lg"][g] = out.astype(BF16)
        return c

    lax.fori_loop(0, G, grad_rows, 0)
    put("lg")
    await_bytes(rsem("vz"), (nh - 1) * 8 * LANES * 4)
    total = r["vec_t"][...]
    for o in heads:
        total = total + r["vec_z"][o]
    r["o_vec"][...] = total
    put("vec")

    for name, nbytes in total_sent.items():
        await_bytes(ssem(name), nbytes)
    for name in DONE:
        pltpu.make_async_copy(r["o_" + name], r["y_" + name], lsem(name)).wait()


def body(ni, nh, media, latents, counts, media_gain, media_bias, latent_gain, latent_bias, w_query,
         w_key, w_value, w_out, ff_gain, ff_bias, w_up, w_down, cotangent):
    z = layout(ni, nh, media, latents, w_query, w_up)
    G, D, W, SR, LR, FU, RC = (z[k] for k in ("G", "D", "W", "SR", "LR", "FU", "RC"))
    vm = pl.BlockSpec(memory_space=pltpu.VMEM)
    hbm = pl.BlockSpec(memory_space=pl.ANY)
    outs = (
        ((G, LR, D), BF16), ((G, SR, D), BF16), ((G, LR, D), BF16), ((RC, 3 * W), F32),
        ((RC, W), F32), ((FU, D), F32), ((FU, D), F32), ((8, LANES), F32),
    )
    n_recv = sum(n if n else G for _, n in RECV)
    rows = [v.reshape(1, D) for v in (media_gain, media_bias, latent_gain, latent_bias, ff_gain,
                                      ff_bias)]
    res = pl.pallas_call(
        functools.partial(kernel, ni, nh, z),
        out_shape=[jax.ShapeDtypeStruct(s, d) for s, d in outs],
        in_specs=[pl.BlockSpec(memory_space=pltpu.SMEM)] + [vm] * 6 + [hbm] * 9,
        out_specs=[hbm] * len(outs),
        scratch_shapes=[pltpu.VMEM(s, d) for s, d in z["vm"].values()]
        + [
            pltpu.SemaphoreType.DMA((n_recv,)),
            pltpu.SemaphoreType.DMA((len(RECV),)),
            pltpu.SemaphoreType.DMA((len(LOCAL),)),
        ],
        compiler_params=pltpu.CompilerParams(
            collective_id=0, has_side_effects=True, vmem_limit_bytes=67043328
        ),
        name="resampler",
    )(counts, *rows, media, latents, w_query, w_key, w_value, w_out, w_up, w_down, cotangent)
    lat_out, media_grad, lat_grad, wa, wo, up, down, vec = res
    place = lax.axis_index("img") * nh + lax.axis_index("head")
    share = D // (ni * nh)
    first = lax.rem(place * share, LANES)
    vec = lax.dynamic_slice(vec, (0, first), (8, share))
    wk, wv, wq = (wa[:, k * W : (k + 1) * W] for k in range(3))
    return (
        lat_out, media_grad, lat_grad, vec[0], vec[1], vec[2], vec[3], wq, wk, wv, wo.T, vec[4],
        vec[5], up, down,
    )


def solution(mesh):
    ni, nh = mesh.shape["img"], mesh.shape["head"]
    both = P(("img", "head"))
    rows = P("img", "head", None)
    return jax.shard_map(
        functools.partial(body, ni, nh),
        mesh=mesh,
        in_specs=(
            P("img", None, None), P("img", None, None), P("img"), P(), P(), P(), P(),
            P(None, "head"), P(None, "head"), P(None, "head"), P("head", None), P(), P(),
            P(("img", "head"), None), P(("img", "head"), None), rows,
        ),
        out_specs=(
            rows, rows, rows, both, both, both, both, P("img", "head"), P("img", "head"),
            P("img", "head"), P("head", "img"), both, both, P(("img", "head"), None),
            P(("img", "head"), None),
        ),
        check_vma=False,
    )
```

```python
import functools
import math
from types import SimpleNamespace

import jax
import jax.numpy as jnp
from jax import lax
from jax.experimental import pallas as pl
from jax.experimental.pallas import tpu as pltpu
from jax.sharding import PartitionSpec as P

HS = 64
EPSILON = 1e-05
LANES = 128
TILE = 16
BF16 = jnp.bfloat16
F32 = jnp.float32
MESH = pl.DeviceIdType.MESH
NN = ((1,), (0,))
NT = ((1,), (1,))
TN = ((0,), (0,))


def dot(a, b, dims):
    return lax.dot_general(a, b, (dims, ((), ())), preferred_element_type=F32)


def normalize(x):
    width = x.shape[-1]
    centred = x - jnp.sum(x, axis=-1, keepdims=True) * (1.0 / width)
    variance = jnp.sum(centred * centred, axis=-1, keepdims=True) * (1.0 / width)
    inv_std = lax.rsqrt(variance + EPSILON)
    return centred * inv_std, inv_std


def norm_back(upstream, hat, inv_std, gain):
    width = upstream.shape[-1]
    scaled = upstream * gain
    first = jnp.sum(scaled, axis=-1, keepdims=True) * (1.0 / width)
    second = jnp.sum(scaled * hat, axis=-1, keepdims=True) * (1.0 / width)
    return inv_std * (scaled - first - hat * second)


def fold_rows(x):
    return jnp.sum(x.reshape(x.shape[0] // 8, 8, x.shape[1]), axis=0)


def gelu_parts(hidden):
    normal_cdf = 0.5 * (1.0 + lax.erf(hidden * (1.0 / math.sqrt(2.0))))
    density = jnp.exp(-0.5 * hidden * hidden) * (1.0 / math.sqrt(2.0 * math.pi))
    return (hidden * normal_cdf, normal_cdf + hidden * density)


def sizes(ni, nh, media, latents, w_query, w_up):
    G, S, D = media.shape
    L, W, FU = latents.shape[1], w_query.shape[1], w_up.shape[0]
    Q = min(ni, W // TILE)
    return SimpleNamespace(
        ni=ni, nh=nh, G=G, S=S, D=D, L=L, W=W, FU=FU, T=S + L, SR=S // nh, LR=L // nh, R=G * L,
        FH=ni * FU, RC=D // ni, NK=ni // 2, HN=W // HS, Q=Q, QC=W // Q,
    )


def outputs(z):
    return dict(
        lat=((z.G, z.LR, z.D), BF16),
        mg=((z.G, z.SR, z.D), BF16),
        lg=((z.G, z.LR, z.D), BF16),
        wa=((z.RC, 3 * z.W), F32),
        wo=((z.RC, z.W), F32),
        up=((z.FU, z.D), F32),
        dn=((z.FU, z.D), F32),
        vec=((8, LANES), F32),
    )


def scratch(z):
    G, D, L, W, T, SR, LR, R, FH, RC, NK, FU, nh = (
        z.G, z.D, z.L, z.W, z.T, z.SR, z.LR, z.R, z.FH, z.RC, z.NK, z.FU, z.nh
    )
    return dict(
        media_b=((2, z.S, D), BF16),
        media_o=((G, SR, D), BF16),
        lat=((G, L, D), BF16),
        keys=((G * T, D), BF16),
        lat_n=((R, D), BF16),
        wkv_o=((D, 2 * W), BF16),
        wq_o=((D, W), BF16),
        wkv_f=((D, nh * 2 * W), BF16),
        wq_f=((D, nh * W), BF16),
        wout_f=((nh * W, D), BF16),
        up_f=((FH, D), BF16),
        down_f=((FH, D), BF16),
        cot_f=((G, L, D), BF16),
        kv=((G * T, 2 * W), BF16),
        q=((R, W), BF16),
        probs=((G * T, z.HN * L), F32),
        att_f=((G, L, nh * W), BF16),
        mid_o=((G, LR, D), F32),
        hat=((R, D), F32),
        inv=((R, LANES), F32),
        ff_in=((R, D), BF16),
        act=((R, FH), BF16),
        slope=((R, FH), F32),
        gh=((R, FH), BF16),
        tmp=((R // 2, max(D, FH)), F32),
        ffo_p=((G, L, D), BF16),
        gm_p=((G, L, D), BF16),
        ga_p=((G, L, nh * W), BF16),
        ffo_r=((nh + 1, G, LR, D), BF16),
        gm_r=((nh + 1, G, LR, D), BF16),
        ga_r=((nh, G, L, W), BF16),
        gkv=((G, T, 2 * W), BF16),
        gq=((G, L, W), BF16),
        gkv_r=((G, SR + LR, nh * 2 * W), BF16),
        gq_r=((G, LR, nh * W), BF16),
        wu=((FH, D), BF16),
        wd=((FH, D), BF16),
        wo=((D, nh * W), BF16),
        wa=((D, 3 * W), BF16),
        wu1=((NK * FU, D), BF16),
        wd1=((NK * FU, D), BF16),
        wo1=((NK * RC, nh * W), BF16),
        wa1=((NK * RC, 3 * W), BF16),
        wu2=((NK * FU, D), BF16),
        wd2=((NK * FU, D), BF16),
        wo2=((NK * RC, nh * W), BF16),
        wa2=((NK * RC, 3 * W), BF16),
        wo_s=((nh, RC, W), BF16),
        wo_z=((nh, RC, W), BF16),
        glat=((G, LR, D), F32),
        vacc=((6, 8, D), F32),
        vec=((8, D), F32),
        vec_r=((z.ni, 8, LANES), F32),
        vec_t=((8, LANES), F32),
        vec_z=((nh, 8, LANES), F32),
    )


def links(z):
    G, nh = z.G, z.nh
    return dict(
        wout_z=(1, 1), wout_x=(1, 1), up_p=(1, 1), up_x=(1, 1), up_y=(1, 1), dn_p=(1, 1),
        dn_x=(1, 1), dn_y=(1, 1), kv_z=(1, 1), kv_p=(1, 1), kv_x=(1, 1), kv_y=(1, 1),
        cot=(G * nh, 2 * nh), att=(G, 1), ga=(2, 1), ffo=(nh + 1, nh), gm=(nh + 1, nh), gkv=(G, 1),
        gq=(1, 1), wu1=(1, 1), wu2=(1, 1), wd1=(1, 1), wd2=(1, 1), wo1=(1, 1), wo2=(1, 1),
        wo3=(1, 1), wa1=(1, 1), wa2=(1, 1), vp=(1, 1), vz=(1, 1),
    )


LOADS = dict(m0=0, m1=1, w=2, lat=3, ff=4, kvq=5, mo=6)
INS = tuple(
    dict(
        counts=0, g_m=0, b_m=0, g_l=0, b_l=0, g_f=0, b_f=0, media=0, latents=0, w_query=0, w_key=0,
        w_value=0, w_out=0, w_up=0, w_down=0, cot=0,
    )
)


def kernel(z, *refs):
    outs, vmem = outputs(z), scratch(z)
    n_in, n_out = len(INS), len(outs)
    r = SimpleNamespace(
        **dict(zip(INS, refs[:n_in])),
        **dict(zip(vmem, refs[n_in + n_out :])),
    )
    dst = SimpleNamespace(**dict(zip(outs, refs[n_in : n_in + n_out])))
    out = SimpleNamespace(**dict(zip(outs, refs[n_in + n_out + len(vmem) :])))
    recv_sems, send_sems, load_sems, out_sems = refs[-4:]
    G, S, D, L, W, FU, T, SR, LR, R, FH, RC, NK, HN = (
        z.G, z.S, z.D, z.L, z.W, z.FU, z.T, z.SR, z.LR, z.R, z.FH, z.RC, z.NK, z.HN
    )
    ni, nh = z.ni, z.nh
    me_i, me_h = lax.axis_index("img"), lax.axis_index("head")
    par, half = lax.rem(me_i, 2), lax.div(me_i, 2)
    mate = me_i + 1 - 2 * par

    link, n_recv, n_send = {}, 0, 0
    for name, (a, b) in links(z).items():
        link[name] = SimpleNamespace(recv=n_recv, send=n_send, bytes=0)
        n_recv, n_send = n_recv + a, n_send + b
    link = SimpleNamespace(**link)
    ld = SimpleNamespace(**LOADS)

    def size(ref):
        return math.prod(ref.shape) * jnp.dtype(ref.dtype).itemsize

    def await_bytes(sem, nbytes):
        lanes = D
        while nbytes % (2 * lanes * TILE):
            lanes //= 2
        assert lanes >= LANES and nbytes // (2 * lanes) <= G * T
        view = r.keys.at[pl.ds(0, nbytes // (2 * lanes)), pl.ds(0, lanes)]
        pltpu.make_async_copy(view, view, sem).wait()

    def load(src, dst, k):
        pltpu.make_async_copy(src, dst, load_sems.at[k]).start()

    def loaded(k, nbytes):
        await_bytes(load_sems.at[k], nbytes)

    def arrived(to, nbytes, k=0):
        await_bytes(recv_sems.at[to.recv + k], nbytes)

    def push(src, dst, to, img, head, k=0, s=0):
        pltpu.make_async_remote_copy(
            src_ref=src,
            dst_ref=dst,
            send_sem=send_sems.at[to.send + s],
            recv_sem=recv_sems.at[to.recv + k],
            device_id=(img, head),
            device_id_type=MESH,
        ).start()

    def send(src, dst, to, img, head, k=0, times=1):
        push(src, dst, to, img, head, k)
        to.bytes += size(src) * times

    def rows_of(i, n):
        return pl.ds(pl.multiple_of(i * n, n), n)

    def at_rows(start, n, unit):
        return pl.ds(pl.multiple_of(start, unit), n)

    heads = [lax.rem(me_h + d, nh) for d in range(1, nh)]

    def to_heads(f):
        for other in heads:
            f(other)

    def to_twins(f):
        def step(k, c):
            f(lax.rem(half + k, NK) * 2 + par)
            return c

        lax.fori_loop(1, NK, step, 0)

    def repeat(n, f):
        def step(k, c):
            f(k)
            return c

        lax.fori_loop(0, n, step, 0)

    load(r.media.at[0], r.media_b.at[0], ld.m0)
    load(r.w_key, r.wkv_o.at[:, pl.ds(0, W)], ld.w)
    load(r.w_value, r.wkv_o.at[:, pl.ds(W, W)], ld.w)
    load(r.w_query, r.wq_o, ld.w)
    load(r.latents, r.lat, ld.lat)
    load(r.media.at[1], r.media_b.at[1], ld.m1)
    barrier = pltpu.get_barrier_semaphore()
    to_heads(
        lambda o: pl.semaphore_signal(
            barrier, inc=1, device_id=(me_i, o), device_id_type=MESH
        )
    )
    repeat(
        ni - 1,
        lambda k: pl.semaphore_signal(
            barrier, inc=1, device_id=(lax.rem(me_i + 1 + k, ni), me_h), device_id_type=MESH
        ),
    )
    pl.semaphore_wait(barrier, nh - 1 + ni - 1)

    Q, QC = z.Q, z.QC
    share = lax.rem(me_i, Q)
    first = me_i - share
    wo_part = at_rows(me_h * W + share * QC, QC, QC)
    to_heads(
        lambda o: send(r.w_out.at[rows_of(share, QC)], r.wout_f.at[wo_part], link.wout_z, me_i, o)
    )
    own_f = rows_of(me_i, FU)

    def spread_rows(src, buf, twins, pair):
        to_twins(lambda o: send(src, buf.at[own_f], twins, o, me_h, times=NK - 1))
        send(src, buf.at[own_f], pair, mate, me_h)

    spread_rows(r.w_up, r.up_f, link.up_x, link.up_p)
    load(r.w_out, r.wout_f.at[rows_of(me_h, W)], ld.ff)
    load(r.w_up, r.up_f.at[own_f], ld.ff)
    load(r.w_down, r.down_f.at[own_f], ld.ff)
    own_l = rows_of(me_h, LR)
    load(r.cot, r.cot_f.at[:, own_l, :], ld.ff)
    own_kv = [at_rows(me_h * 2 * W + k * W, W, W) for k in range(2)]
    own_w = rows_of(me_h, W)
    own_c = rows_of(me_i, RC)
    load(r.w_key.at[own_c], r.wkv_f.at[own_c, own_kv[0]], ld.kvq)
    load(r.w_value.at[own_c], r.wkv_f.at[own_c, own_kv[1]], ld.kvq)
    load(r.w_query.at[own_c], r.wq_f.at[own_c, own_w], ld.kvq)
    load(r.media.at[:, rows_of(me_h, SR), :], r.media_o, ld.mo)

    gain_m, bias_m = r.g_m[...], r.b_m[...]
    gain_l, bias_l = r.g_l[...], r.b_l[...]
    gain_f, bias_f = r.g_f[...], r.b_f[...]
    NB = 32
    lane_head = lax.div(lax.broadcasted_iota(jnp.int32, (L, W), 1), HS)

    def spread(x):
        zero = jnp.zeros_like(x)
        return jnp.concatenate([jnp.where(lane_head == k, x, zero) for k in range(HN)], axis=0)

    def gather_diag(x):
        out = x[:L]
        for k in range(1, HN):
            out = jnp.where(lane_head == k, x[k * L : (k + 1) * L], out)
        return out

    loaded(ld.w, 3 * D * W * 2)
    loaded(ld.lat, G * L * D * 2)

    def cot_push(g, source, way):
        part = rows_of(source, LR)
        view = r.cot_f.at[g, part, :]
        return lambda src, s: push(src, view, link.cot, me_i, me_h + way, g * nh + source, s)

    def cot_start(g):
        for s, way in enumerate((1, -1)):

            @pl.when((me_h + way >= 0) & (me_h + way < nh))
            def _():
                cot_push(g, me_h, way)(r.cot.at[g], s)

    def cot_pass(g, d):
        for s, way in enumerate((1, -1)):
            source, onto = me_h - way * d, me_h + way

            @pl.when((source >= 0) & (source < nh))
            def _():
                arrived(link.cot, LR * D * 2, g * nh + source)

            if d < nh - 1:

                @pl.when((source >= 0) & (source < nh) & (onto >= 0) & (onto < nh))
                def _():
                    cot_push(g, source, way)(r.cot_f.at[g, rows_of(source, LR), :], 2 * d + s)

    def cot_step(g):
        if isinstance(g, int):
            for d in range(1, nh):
                if 0 <= g - d < G:
                    cot_pass(g - d, d)
            return
        cot_start(g)
        for d in range(1, nh):

            @pl.when(g >= d)
            def _():
                cot_pass(g - d, d)

    def relay(twins, onto, buf, n):
        arrived(twins, (NK - 1) * size(buf.at[rows_of(0, n)]))
        to_twins(
            lambda o: send(
                buf.at[rows_of(o, n)], buf.at[rows_of(o, n)], onto, mate, me_h, times=NK - 1
            )
        )

    def share_wout():
        arrived(link.wout_z, (nh - 1) * QC * D * 2)

        def one(k):
            other = first + lax.rem(share + 1 + k, Q)

            def part(o):
                at = r.wout_f.at[at_rows(o * W + share * QC, QC, QC)]
                send(at, at, link.wout_x, other, me_h, times=Q - 1)

            to_heads(part)

        repeat(Q - 1, one)
        spread_rows(r.w_down, r.down_f, link.dn_x, link.dn_p)

    def image(g):
        slot = lax.rem(g, 2)
        for k, sem in enumerate((ld.m0, ld.m1)):

            @pl.when(slot == k)
            def _():
                loaded(sem, S * D * 2)

        def norm_media(b):
            hat, _ = normalize(r.media_b[slot, rows_of(b, NB), :].astype(F32))
            r.keys[at_rows(g * T + b * NB, NB, NB), :] = (hat * gain_m + bias_m).astype(BF16)

        repeat(S // NB, norm_media)

        def norm_latent(b):
            hat, _ = normalize(r.lat[g, rows_of(b, NB), :].astype(F32))
            y = (hat * gain_l + bias_l).astype(BF16)
            r.keys[at_rows(g * T + S + b * NB, NB, NB), :] = y
            r.lat_n[at_rows(g * L + b * NB, NB, NB), :] = y

        repeat(L // NB, norm_latent)
        for k, sem in enumerate((ld.m0, ld.m1)):

            @pl.when((slot == k) & (g + 2 < G))
            def _():
                load(r.media.at[g + 2], r.media_b.at[k], sem)

        rows, lat_rows = rows_of(g, T), rows_of(g, L)
        kv = dot(r.keys[rows, :], r.wkv_o[...], NN).astype(BF16)
        r.kv[rows, :] = kv
        q = (dot(r.lat_n[lat_rows, :], r.wq_o[...], NN) * (HS**-0.5)).astype(BF16)
        r.q[lat_rows, :] = q
        scores = dot(kv[:, :W], spread(q), NT)
        place = lax.broadcasted_iota(jnp.int32, scores.shape, 0)
        scores = jnp.where((place < r.counts[g]) | (place >= S), scores, -1e30)
        top = jnp.max(scores, axis=0, keepdims=True)
        total = jnp.sum(jnp.exp(scores - top), axis=0, keepdims=True)
        probs = jnp.exp(scores - (top + jnp.log(total)))
        r.probs[rows, :] = probs
        att = gather_diag(dot(probs.astype(BF16), kv[:, W:], TN)).astype(BF16)
        r.att_f[g, :, own_w] = att
        own_att = r.att_f.at[g, :, own_w]
        to_heads(lambda o: send(own_att, own_att, link.att, me_i, o, g, times=G))
        cot_step(g)

        @pl.when(g == 1)
        def _():
            share_wout()

        @pl.when(g == G - 2)
        def _():
            relay(link.up_x, link.up_y, r.up_f, FU)

    repeat(G, image)
    cot_step(G)

    def send_kvq(o):
        send(r.w_key.at[own_c], r.wkv_f.at[own_c, own_kv[0]], link.kv_z, me_i, o)
        send(r.w_value.at[own_c], r.wkv_f.at[own_c, own_kv[1]], link.kv_z, me_i, o)
        send(r.w_query.at[own_c], r.wq_f.at[own_c, own_w], link.kv_z, me_i, o)

    to_heads(send_kvq)
    r.vacc[...] = jnp.zeros_like(r.vacc)

    CR, CG = R // 2, G // 2
    loaded(ld.ff, (W + 2 * FU + G * LR) * D * 2)
    arrived(link.wout_x, (Q - 1) * (nh - 1) * QC * D * 2)

    def ff_forward(b):
        for k in range(CG):
            arrived(link.att, (nh - 1) * L * W * 2, b * CG + k)
        at = rows_of(b, CR)
        att = r.att_f[pl.ds(b * CG, CG), :, :].reshape(CR, nh * W)
        r.tmp[:, :D] = dot(att, r.wout_f[...], NN)

        def norm(k):
            row = at_rows(b * CR + k * LR, LR, LR)
            g, piece = b * CG + lax.div(k, nh), lax.rem(k, nh)
            x = r.tmp[rows_of(k, LR), :D] + r.lat[g, rows_of(piece, LR), :].astype(F32)
            hat, inv = normalize(x)

            @pl.when(piece == me_h)
            def _():
                r.mid_o[g] = x

            r.hat[row, :] = hat
            r.inv[row, :] = jnp.broadcast_to(inv, (LR, LANES))
            r.ff_in[row, :] = (hat * gain_f + bias_f).astype(BF16)

        repeat(CR // LR, norm)
        for k in range(1, min(nh - 1, 3)):

            @pl.when(b == k - 1)
            def _():
                cot_step(G + k)

        @pl.when(b == 0)
        def _():
            arrived(link.up_p, FU * D * 2)
            arrived(link.up_y, (NK - 1) * FU * D * 2)

        r.tmp[:, :FH] = dot(r.ff_in[at, :], r.up_f[...], NT)

        def gelu(k):
            row = at_rows(b * CR + k * TILE, TILE, TILE)
            value, slope = gelu_parts(r.tmp[rows_of(k, TILE), :FH])
            r.act[row, :] = value.astype(BF16)
            r.slope[row, :] = slope

        repeat(CR // TILE, gelu)

    repeat(2, ff_forward)
    for k in range(3, nh - 1):
        cot_step(G + k)
    relay(link.dn_x, link.dn_y, r.down_f, FU)
    arrived(link.dn_p, FU * D * 2)
    arrived(link.dn_y, (NK - 1) * FU * D * 2)

    def ff_backward(b):
        at, imgs = rows_of(b, CR), pl.ds(b * CG, CG)
        r.tmp[:, :FH] = dot(r.cot_f[imgs, :, :].reshape(CR, D), r.down_f[...], NT)

        def slope(k):
            row = at_rows(b * CR + k * TILE, TILE, TILE)
            r.gh[row, :] = (r.tmp[rows_of(k, TILE), :FH] * r.slope[row, :]).astype(BF16)

        repeat(CR // TILE, slope)
        r.tmp[:, :D] = dot(r.gh[at, :], r.up_f[...], NN)

        def norm(k):
            row = at_rows(b * CR + k * LR, LR, LR)
            g, part = b * CG + lax.div(k, nh), rows_of(lax.rem(k, nh), LR)
            u, hat = r.tmp[rows_of(k, LR), :D], r.hat[row, :]
            grad = norm_back(u, hat, r.inv[row, :1], gain_f)
            cot = r.cot_f[g, part, :].astype(F32) * (1.0 / nh)
            r.gm_p[g, part, :] = (grad + cot).astype(BF16)
            r.vacc[4] += fold_rows(u * hat)
            r.vacc[5] += fold_rows(u)

        repeat(CR // LR, norm)
        ga = dot(r.gm_p[imgs, :, :].reshape(CR, D), r.wout_f[...], NT)
        r.ga_p[imgs, :, :] = ga.astype(BF16).reshape(CG, L, nh * W)
        to_heads(
            lambda o: send(
                r.ga_p.at[imgs, :, rows_of(o, W)], r.ga_r.at[me_h, imgs], link.ga, me_i, o, b,
                times=2,
            )
        )

    repeat(2, ff_backward)

    def share_kvq(o, to, times):
        for buf in (r.wkv_f, r.wq_f):
            send(buf.at[own_c], buf.at[own_c], to, o, me_h, times=times)

    def relay_kvq(o):
        for buf in (r.wkv_f, r.wq_f):
            at = buf.at[rows_of(o, RC)]
            send(at, at, link.kv_y, mate, me_h, times=NK - 1)

    loaded(ld.kvq, 3 * RC * W * 2)
    arrived(link.kv_z, (nh - 1) * 3 * RC * W * 2)
    to_twins(lambda o: share_kvq(o, link.kv_x, NK - 1))
    share_kvq(mate, link.kv_p, 1)

    def ff_out(b):
        out = dot(r.act[rows_of(b, CR), :], r.down_f[...], NN)
        r.ffo_p[pl.ds(b * CG, CG), :, :] = out.astype(BF16).reshape(CG, L, D)

    repeat(2, ff_out)

    def scatter_pair(buf, got, n, to):
        repeat(
            NK,
            lambda k: send(
                buf.at[rows_of(2 * k + 1 - par, n)], got.at[rows_of(k, n)], to, mate, me_h, times=NK
            ),
        )

    def scatter_twins(buf, got, got2, n, to, to2):
        arrived(to, size(got))

        def step(d, c):
            k = lax.rem(half + d, NK)
            mine = rows_of(2 * k + par, n)
            both = buf[mine, :].astype(F32) + got[rows_of(k, n), :].astype(F32)
            buf[mine, :] = both.astype(BF16)
            send(
                buf.at[mine], got2.at[rows_of(half, n)], to2, 2 * k + par, me_h, times=NK - 1
            )
            return c

        lax.fori_loop(1, NK, step, 0)

    def scatter_sum(buf, got, got2, n, to2, total):
        arrived(to2, size(got2) // NK * (NK - 1))
        total[...] = buf[rows_of(me_i, n), :].astype(F32) + got[rows_of(half, n), :].astype(F32)

        def step(d, c):
            total[...] += got2[rows_of(lax.rem(half + d, NK), n), :].astype(F32)
            return c

        lax.fori_loop(1, NK, step, 0)

    FT = 2 * LANES

    def down_grad(t):
        at = rows_of(t, FT)
        r.wd[at, :] = dot(r.act[:, at], r.cot_f[...].reshape(R, D), TN).astype(BF16)

    repeat(FH // FT, down_grad)
    scatter_pair(r.wd, r.wd1, FU, link.wd1)

    def up_grad(t):
        at = rows_of(t, FT)
        r.wu[at, :] = dot(r.gh[:, at], r.ff_in[...], TN).astype(BF16)

    repeat(FH // FT, up_grad)
    scatter_pair(r.wu, r.wu1, FU, link.wu1)

    def out_grad(t):
        at = rows_of(t, FT)
        left = r.gm_p[:, :, at].reshape(R, FT)
        r.wo[at, :] = dot(left, r.att_f[...].reshape(R, nh * W), TN).astype(BF16)

    repeat(D // FT, out_grad)
    scatter_pair(r.wo, r.wo1, RC, link.wo1)

    for b in range(2):
        arrived(link.ga, (nh - 1) * CG * L * W * 2, b)
    wide = rows_of(me_h, 2 * W)

    def image_back(g):
        rows, lat_rows = rows_of(g, T), rows_of(g, L)
        ga = r.ga_p[g, :, own_w].astype(F32)
        for o in heads:
            ga = ga + r.ga_r[o, g].astype(F32)
        ga = spread(ga.astype(BF16))
        q = spread(r.q[lat_rows, :])
        key, value = r.kv[rows, :W], r.kv[rows, W:]
        probs = r.probs[rows, :]
        grad_probs = dot(value, ga, NT)
        delta = jnp.sum(probs * grad_probs, axis=0, keepdims=True)
        grad_scores = (probs * (grad_probs - delta)).astype(BF16)
        r.gkv[g, :, W:] = dot(probs.astype(BF16), ga, NN).astype(BF16)
        r.gkv[g, :, :W] = dot(grad_scores, q, NN).astype(BF16)
        grad_query = gather_diag(dot(grad_scores, key, TN)).astype(BF16)
        r.gq[g] = (grad_query.astype(F32) * (HS**-0.5)).astype(BF16)

        def go(o):
            part = r.gkv_r.at[g, pl.ds(0, SR), wide]
            send(r.gkv.at[g, rows_of(o, SR), :], part, link.gkv, me_i, o, g, times=G)
            part = r.gkv_r.at[g, pl.ds(SR, LR), wide]
            at = at_rows(S + o * LR, LR, LR)
            send(r.gkv.at[g, at, :], part, link.gkv, me_i, o, g, times=G)
            part = r.gq_r.at[g, :, own_w]
            send(r.gq.at[g, rows_of(o, LR), :], part, link.gq, me_i, o, times=G)

        to_heads(go)
        r.gkv_r[g, :SR, wide] = r.gkv[g, rows_of(me_h, SR), :]
        r.gkv_r[g, SR:, wide] = r.gkv[g, at_rows(S + me_h * LR, LR, LR), :]
        r.gq_r[g, :, own_w] = r.gq[g, own_l, :]

    repeat(G, image_back)

    BLOCK = G * LR * D * 2

    def line_push(part, got, to, o, way):
        onto = me_h + way
        slot = o if way < 0 else jnp.where(o == onto, nh, o)
        push(part.at[:, rows_of(o, LR), :], got.at[slot], to, me_i, onto, slot, o)

    def line_start(part, got, to):
        @pl.when(me_h == nh - 1)
        def _():
            for o in range(nh - 1):
                line_push(part, got, to, o, -1)
            got[nh - 1] = jnp.zeros((G, LR, D), BF16)

        @pl.when(me_h == 0)
        def _():
            for o in range(nh - 1, 0, -1):
                line_push(part, got, to, o, 1)
            got[nh] = jnp.zeros((G, LR, D), BF16)

    def line_pass(part, got, to, k):
        for o, way in ((k, -1), (nh - 1 - k, 1)):
            ahead = (o < me_h) & (me_h < nh - 1) if way < 0 else (o > me_h) & (me_h > 0)

            @pl.when(ahead)
            def _():
                arrived(to, BLOCK, o)

                def add(g):
                    at = rows_of(o, LR)
                    both = part[g, at, :].astype(F32) + got[o, g].astype(F32)
                    part[g, at, :] = both.astype(BF16)

                repeat(G, add)
                line_push(part, got, to, o, way)

    def line_end(part, got, to, base, total):
        @pl.when(me_h < nh - 1)
        def _():
            arrived(to, BLOCK, me_h)

        @pl.when(me_h > 0)
        def _():
            arrived(to, BLOCK, nh)

        def add(g):
            x = base[g] + part[g, own_l, :].astype(F32)
            x = x + got[me_h, g].astype(F32) + got[nh, g].astype(F32)
            total[g] = x.astype(BF16)

        repeat(G, add)

    line_start(r.ffo_p, r.ffo_r, link.ffo)
    line_start(r.gm_p, r.gm_r, link.gm)
    scatter_twins(r.wd, r.wd1, r.wd2, FU, link.wd1, link.wd2)
    scatter_twins(r.wu, r.wu1, r.wu2, FU, link.wu1, link.wu2)
    scatter_twins(r.wo, r.wo1, r.wo2, RC, link.wo1, link.wo2)

    def proj_grad(t):
        at = rows_of(t, FT)
        left = r.gkv[...].reshape(G * T, 2 * W)
        r.wa[at, : 2 * W] = dot(r.keys[:, at], left, TN).astype(BF16)
        r.wa[at, 2 * W :] = dot(r.lat_n[:, at], r.gq[...].reshape(R, W), TN).astype(BF16)

    repeat(D // FT, proj_grad)
    scatter_pair(r.wa, r.wa1, RC, link.wa1)
    arrived(link.kv_x, (NK - 1) * 3 * nh * RC * W * 2)
    to_twins(relay_kvq)
    scatter_twins(r.wa, r.wa1, r.wa2, RC, link.wa1, link.wa2)
    arrived(link.kv_p, 3 * nh * RC * W * 2)
    arrived(link.kv_y, (NK - 1) * 3 * nh * RC * W * 2)

    loaded(ld.mo, G * SR * D * 2)
    arrived(link.gq, (nh - 1) * G * LR * W * 2)
    KR = SR + LR

    def put(k, at=slice(None)):
        name = list(outs)[k]
        a, b = getattr(out, name).at[at], getattr(dst, name).at[at]
        pltpu.make_async_copy(a, b, out_sems.at[k]).start()

    def own_rows(b):
        for k in range(2):
            arrived(link.gkv, (nh - 1) * KR * 2 * W * 2, 2 * b + k)
        two = pl.ds(2 * b, 2)
        left = r.gkv_r[two, :, :].reshape(2 * KR, nh * 2 * W)
        r.tmp[: 2 * KR, :D] = dot(left, r.wkv_f[...], NT)
        query = dot(r.gq_r[two, :, :].reshape(2 * LR, nh * W), r.wq_f[...], NT)
        for k in range(2):
            r.tmp[pl.ds(k * KR + SR, LR), :D] += query[k * LR : (k + 1) * LR]

        def rows(j):
            k, i = lax.div(j, SR // LR), lax.rem(j, SR // LR)
            g, piece = 2 * b + k, rows_of(i, LR)
            u = r.tmp[at_rows(k * KR + i * LR, LR, LR), :D]
            hat, inv = normalize(r.media_o[g, piece, :].astype(F32))
            out.mg[g, piece, :] = norm_back(u, hat, inv, gain_m).astype(BF16)
            r.vacc[0] += fold_rows(u * hat)
            r.vacc[1] += fold_rows(u)

        repeat(2 * SR // LR, rows)
        for k in range(2):
            g = 2 * b + k
            u = r.tmp[k * KR + SR : (k + 1) * KR, :D]
            hat, inv = normalize(r.lat[g, own_l, :].astype(F32))
            r.glat[g] = norm_back(u, hat, inv, gain_l)
            r.vacc[2] += fold_rows(u * hat)
            r.vacc[3] += fold_rows(u)
        put(1, two)

    repeat(G // 2, own_rows)

    for k in range(6):
        r.vec[k : k + 1, :] = jnp.sum(r.vacc[k], axis=0, keepdims=True)
    r.vec[6:8, :] = jnp.zeros((2, D), F32)

    def block(i):
        return at_rows(lax.div(i * RC, LANES) * LANES, LANES, LANES)

    def vec_step(k):
        o = lax.rem(me_i + 1 + k, ni)
        send(r.vec.at[:, block(o)], r.vec_r.at[me_i], link.vp, o, me_h, times=ni - 1)

    repeat(ni - 1, vec_step)

    line_pass(r.ffo_p, r.ffo_r, link.ffo, 0)
    scatter_sum(r.wd, r.wd1, r.wd2, FU, link.wd2, out.dn)
    line_pass(r.ffo_p, r.ffo_r, link.ffo, 1)
    scatter_sum(r.wu, r.wu1, r.wu2, FU, link.wu2, out.up)
    for k in range(2, nh - 2):
        line_pass(r.ffo_p, r.ffo_r, link.ffo, k)
    scatter_sum(r.wo, r.wo1, r.wo2, RC, link.wo2, r.tmp.at[:RC, : nh * W])
    for k in range(nh):
        r.wo_s[k] = r.tmp[:RC, k * W : (k + 1) * W].astype(BF16)
    to_heads(lambda o: send(r.wo_s.at[o], r.wo_z.at[me_h], link.wo3, me_i, o))
    scatter_sum(r.wa, r.wa1, r.wa2, RC, link.wa2, out.wa)
    arrived(link.vp, (ni - 1) * 8 * LANES * 4)
    r.vec_t[...] = r.vec[:, block(me_i)]

    def vec_sum(k):
        r.vec_t[...] += r.vec_r[lax.rem(me_i + 1 + k, ni)]

    repeat(ni - 1, vec_sum)
    to_heads(lambda o: send(r.vec_t, r.vec_z.at[me_h], link.vz, me_i, o))
    for k in range(nh - 2):
        line_pass(r.gm_p, r.gm_r, link.gm, k)
    line_end(r.ffo_p, r.ffo_r, link.ffo, r.mid_o, out.lat)
    arrived(link.wo3, (nh - 1) * RC * W * 2)
    total = r.tmp[:RC, own_w]
    for o in heads:
        total = total + r.wo_z[o].astype(F32)
    out.wo[...] = total
    arrived(link.vz, (nh - 1) * 8 * LANES * 4)
    total = r.vec_t[...]
    for o in heads:
        total = total + r.vec_z[o]
    out.vec[...] = total
    for k in range(len(outs)):
        if k not in (1, 2):
            put(k)
    line_end(r.gm_p, r.gm_r, link.gm, r.glat, out.lg)
    put(2)

    for to in vars(link).values():
        if to.bytes:
            await_bytes(send_sems.at[to.send], to.bytes)
    for d in range(nh - 1):
        for s, way in enumerate((1, -1)):
            source, onto = me_h - way * d, me_h + way

            @pl.when((source >= 0) & (source < nh) & (onto >= 0) & (onto < nh))
            def _():
                await_bytes(send_sems.at[link.cot.send + 2 * d + s], BLOCK)

    for to in (link.ffo, link.gm):
        for o in range(nh):

            @pl.when(me_h != o)
            def _():
                await_bytes(send_sems.at[to.send + o], BLOCK)

    for k, name in enumerate(outs):
        pltpu.make_async_copy(getattr(out, name), getattr(dst, name), out_sems.at[k]).wait()


def finish(z, *refs):
    n = len(outputs(z)) - 1
    src, dst, buf, turned, in_sems, out_sems = (
        refs[:n], refs[n : n + 9], refs[n + 9 : 2 * n + 9], refs[-3], refs[-2], refs[-1]
    )
    W = z.W
    loads = [pltpu.make_async_copy(src[k], buf[k], in_sems.at[k]) for k in range(n)]
    for copy in loads:
        copy.start()
    stores = []

    def store(ref, k):
        stores.append(pltpu.make_async_copy(ref, dst[k], out_sems.at[k]))
        stores[-1].start()

    lat, mg, lg, wa, wo, up, dn = range(7)
    loads[mg].wait()
    store(buf[mg], 1)
    loads[up].wait()
    store(buf[up], 7)
    loads[dn].wait()
    store(buf[dn], 8)
    loads[lat].wait()
    store(buf[lat], 0)
    loads[lg].wait()
    store(buf[lg], 2)
    loads[wa].wait()
    store(buf[wa].at[:, pl.ds(2 * W, W)], 3)
    store(buf[wa].at[:, pl.ds(0, W)], 4)
    store(buf[wa].at[:, pl.ds(W, W)], 5)
    loads[wo].wait()
    turned[...] = buf[wo][...].T
    store(turned, 6)
    for copy in stores:
        copy.wait()


def body(ni, nh, media, latents, counts, media_gain, media_bias, latent_gain, latent_bias, w_query,
         w_key, w_value, w_out, ff_gain, ff_bias, w_up, w_down, cotangent):
    z = sizes(ni, nh, media, latents, w_query, w_up)
    D, W, RC = z.D, z.W, z.RC
    vm = pl.BlockSpec(memory_space=pltpu.VMEM)
    hbm = pl.BlockSpec(memory_space=pl.ANY)
    dma = pltpu.SemaphoreType.DMA
    outs = list(outputs(z).values())
    rows = [
        v.reshape(1, D)
        for v in (media_gain, media_bias, latent_gain, latent_bias, ff_gain, ff_bias)
    ]
    counted = links(z).values()
    res = pl.pallas_call(
        functools.partial(kernel, z),
        out_shape=[jax.ShapeDtypeStruct(s, d) for s, d in outs],
        in_specs=[pl.BlockSpec(memory_space=pltpu.SMEM)] + [vm] * 6 + [hbm] * 9,
        out_specs=[hbm] * len(outs),
        scratch_shapes=[pltpu.VMEM(s, d) for s, d in (*scratch(z).values(), *outs)]
        + [
            dma((sum(a for a, _ in counted),)),
            dma((sum(b for _, b in counted),)),
            dma((len(LOADS),)),
            dma((len(outs),)),
        ],
        compiler_params=pltpu.CompilerParams(
            collective_id=0, has_side_effects=True, vmem_limit_bytes=67043328
        ),
    )(counts, *rows, media, latents, w_query, w_key, w_value, w_out, w_up, w_down, cotangent)
    last = outs[:3] + [((RC, W), F32)] * 3 + [((W, RC), F32)] + outs[5:7]
    res2 = pl.pallas_call(
        functools.partial(finish, z),
        out_shape=[jax.ShapeDtypeStruct(s, d) for s, d in last],
        in_specs=[hbm] * 7,
        out_specs=[hbm] * 9,
        scratch_shapes=[pltpu.VMEM(s, d) for s, d in outs[:7]]
        + [pltpu.VMEM((W, RC), F32), dma((7,)), dma((9,))],
    )(*res[:7])
    lat_out, media_grad, lat_grad, wq, wk, wv, wo, up, down = res2
    share = D // (ni * nh)
    place = lax.axis_index("img") * nh + lax.axis_index("head")
    vec = lax.dynamic_slice(res[7], (0, lax.rem(place * share, LANES)), (8, share))
    return (
        lat_out, media_grad, lat_grad, vec[0], vec[1], vec[2], vec[3], wq, wk, wv, wo, vec[4],
        vec[5], up, down,
    )


def solution(mesh):
    ni, nh = mesh.shape["img"], mesh.shape["head"]
    both = P(("img", "head"))
    rows = P("img", "head", None)
    return jax.shard_map(
        functools.partial(body, ni, nh),
        mesh=mesh,
        in_specs=(
            P("img", None, None), P("img", None, None), P("img"), P(), P(), P(), P(),
            P(None, "head"), P(None, "head"), P(None, "head"), P("head", None), P(), P(),
            P(("img", "head"), None), P(("img", "head"), None), rows,
        ),
        out_specs=(
            rows, rows, rows, both, both, both, both, P("img", "head"), P("img", "head"),
            P("img", "head"), P("head", "img"), both, both, P(("img", "head"), None),
            P(("img", "head"), None),
        ),
        check_vma=False,
    )
```

```python
import functools
import math
from types import SimpleNamespace

import jax
import jax.numpy as jnp
from jax import lax
from jax.experimental import pallas as pl
from jax.experimental.pallas import tpu as pltpu
from jax.sharding import PartitionSpec as P

HS = 64
EPSILON = 1e-05
LANES = 128
TILE = 16
SIDE = 16
BF16 = jnp.bfloat16
F32 = jnp.float32
MESH = pl.DeviceIdType.MESH
NN = ((1,), (0,))
NT = ((1,), (1,))
TN = ((0,), (0,))


def dot(a, b, dims):
    return lax.dot_general(a, b, (dims, ((), ())), preferred_element_type=F32)


def fold_rows(x):
    return jnp.sum(x.reshape(x.shape[0] // 8, 8, x.shape[1]), axis=0)


def gelu_parts(hidden):
    normal_cdf = 0.5 * (1.0 + lax.erf(hidden * (1.0 / math.sqrt(2.0))))
    density = jnp.exp(-0.5 * hidden * hidden) * (1.0 / math.sqrt(2.0 * math.pi))
    return (hidden * normal_cdf, normal_cdf + hidden * density)


def sizes(ni, nh, media, latents, w_query, w_up):
    G, S, D = media.shape
    L, W, FU = latents.shape[1], w_query.shape[1], w_up.shape[0]
    Q = min(ni, W // TILE)
    return SimpleNamespace(
        ni=ni, nh=nh, G=G, S=S, D=D, L=L, W=W, FU=FU, T=S + L, SR=S // nh, LR=L // nh, R=G * L,
        FH=ni * FU, RC=D // ni, NK=ni // 2, HN=W // HS, Q=Q, QC=W // Q,
    )


def outputs(z):
    return dict(
        lat=((z.G, z.LR, z.D), BF16),
        mg=((z.G, z.SR, z.D), BF16),
        lg=((z.G, z.LR, z.D), BF16),
        wa=((z.RC, 3 * z.W), F32),
        wo=((z.RC, z.W), F32),
        up=((z.FU, z.D), F32),
        dn=((z.FU, z.D), F32),
        vec=((8, LANES), F32),
    )


def scratch(z):
    G, D, L, W, T, SR, LR, R, FH, RC, NK, FU, nh = (
        z.G, z.D, z.L, z.W, z.T, z.SR, z.LR, z.R, z.FH, z.RC, z.NK, z.FU, z.nh
    )
    return dict(
        media_b=((2, z.S, D), BF16),
        media_o=((G, SR, D), BF16),
        lat=((G, L, D), BF16),
        keys=((G * T, D), BF16),
        lat_n=((R, D), BF16),
        wkv_o=((D, 2 * W), BF16),
        wq_o=((D, W), BF16),
        wkv_f=((D, nh * 2 * W), BF16),
        wq_f=((D, nh * W), BF16),
        wout_f=((nh * W, D), BF16),
        up_f=((FH, D), BF16),
        down_f=((FH, D), BF16),
        cot_f=((G, L, D), BF16),
        kv=((G * T, 2 * W), BF16),
        q=((R, W), BF16),
        probs=((G * T, z.HN * L), F32),
        att_f=((G, L, nh * W), BF16),
        mid_o=((G, LR, D), F32),
        hat=((R, D), F32),
        inv=((R, LANES), F32),
        ff_in=((R, D), BF16),
        act=((R, FH), BF16),
        slope=((R, FH), F32),
        gh=((R, FH), BF16),
        tmp=((R // 2, max(D, FH)), F32),
        ffo_p=((G, L, D), BF16),
        gm_p=((G, L, D), BF16),
        ga_p=((G, L, nh * W), BF16),
        ffo_r=((nh + 1, G, LR, D), BF16),
        gm_r=((nh + 1, G, LR, D), BF16),
        ga_r=((nh, G, L, W), BF16),
        gkv=((G, T, 2 * W), BF16),
        gq=((G, L, W), BF16),
        gkv_r=((G, SR + LR, nh * 2 * W), BF16),
        gq_r=((G, LR, nh * W), BF16),
        wu=((FH, D), BF16),
        wd=((FH, D), BF16),
        wo=((D, nh * W), BF16),
        wa=((D, 3 * W), BF16),
        wu1=((NK * FU, D), BF16),
        wd1=((NK * FU, D), BF16),
        wo1=((NK * RC, nh * W), BF16),
        wa1=((NK * RC, 3 * W), BF16),
        wu2=((NK * FU, D), BF16),
        wd2=((NK * FU, D), BF16),
        wo2=((NK * RC, nh * W), BF16),
        wa2=((NK * RC, 3 * W), BF16),
        wo_s=((nh, RC, W), BF16),
        wo_z=((nh, RC, W), BF16),
        glat=((G, LR, D), F32),
        hat_m=((G * SR // TILE, TILE, D), F32),
        inv_m=((G * SR // TILE, TILE, LANES), F32),
        hat_l=((G * LR // TILE, TILE, D), F32),
        inv_l=((G * LR // TILE, TILE, LANES), F32),
        vacc=((6, 8, D), F32),
        vec=((8, D), F32),
        vec_r=((z.ni, 8, LANES), F32),
        vec_t=((8, LANES), F32),
        vec_z=((nh, 8, LANES), F32),
    )


def links(z):
    G, nh = z.G, z.nh
    return dict(
        wout_z=(1, 1), wout_x=(1, 1), up_p=(1, 1), up_x=(1, 1), up_y=(1, 1), dn_p=(1, 1),
        dn_x=(1, 1), dn_y=(1, 1), kv_z=(1, 1), kv_p=(1, 1), kv_x=(1, 1), kv_y=(1, 1),
        cot=(G * nh, 2 * nh), att=(G, 1), ga=(2, 1), ffo=(nh + 1, nh), gm=(nh + 1, nh), gkv=(G, 1),
        gq=(1, 1), wu1=(1, 1), wu2=(1, 1), wd1=(1, 1), wd2=(1, 1), wo1=(1, 1), wo2=(1, 1),
        wo3=(1, 1), wa1=(1, 1), wa2=(1, 1), vp=(1, 1), vz=(1, 1),
    )


LOADS = dict(m0=0, m1=1, w=2, lat=3, ff=4, kvq=5, mo=6)
INS = tuple(
    dict(
        counts=0, g_m=0, b_m=0, g_l=0, b_l=0, g_f=0, b_f=0, media=0, latents=0, w_query=0, w_key=0,
        w_value=0, w_out=0, w_up=0, w_down=0, cot=0,
    )
)


def kernel(z, *refs):
    outs, vmem = outputs(z), scratch(z)
    n_in, n_out = len(INS), len(outs)
    r = SimpleNamespace(
        **dict(zip(INS, refs[:n_in])),
        **dict(zip(vmem, refs[n_in + n_out :])),
    )
    dst = SimpleNamespace(**dict(zip(outs, refs[n_in : n_in + n_out])))
    out = SimpleNamespace(**dict(zip(outs, refs[n_in + n_out + len(vmem) :])))
    recv_sems, send_sems, load_sems, out_sems = refs[-4:]
    G, S, D, L, W, FU, T, SR, LR, R, FH, RC, NK, HN = (
        z.G, z.S, z.D, z.L, z.W, z.FU, z.T, z.SR, z.LR, z.R, z.FH, z.RC, z.NK, z.HN
    )
    ni, nh = z.ni, z.nh
    me_i, me_h = lax.axis_index("img"), lax.axis_index("head")
    par, half = lax.rem(me_i, 2), lax.div(me_i, 2)
    mate = me_i + 1 - 2 * par

    link, n_recv, n_send = {}, 0, 0
    for name, (a, b) in links(z).items():
        link[name] = SimpleNamespace(recv=n_recv, send=n_send, bytes=0)
        n_recv, n_send = n_recv + a, n_send + b
    link = SimpleNamespace(**link)
    ld = SimpleNamespace(**LOADS)

    def size(ref):
        return math.prod(ref.shape) * jnp.dtype(ref.dtype).itemsize

    def await_bytes(sem, nbytes):
        lanes = D
        while nbytes % (2 * lanes * TILE):
            lanes //= 2
        assert lanes >= LANES and nbytes // (2 * lanes) <= G * T
        view = r.keys.at[pl.ds(0, nbytes // (2 * lanes)), pl.ds(0, lanes)]
        pltpu.make_async_copy(view, view, sem).wait()

    def load(src, dst, k):
        pltpu.make_async_copy(src, dst, load_sems.at[k]).start()

    def loaded(k, nbytes):
        await_bytes(load_sems.at[k], nbytes)

    def arrived(to, nbytes, k=0):
        await_bytes(recv_sems.at[to.recv + k], nbytes)

    def push(src, dst, to, img, head, k=0, s=0):
        pltpu.make_async_remote_copy(
            src_ref=src,
            dst_ref=dst,
            send_sem=send_sems.at[to.send + s],
            recv_sem=recv_sems.at[to.recv + k],
            device_id=(img, head),
            device_id_type=MESH,
        ).start()

    def send(src, dst, to, img, head, k=0, times=1):
        push(src, dst, to, img, head, k)
        to.bytes += size(src) * times

    def rows_of(i, n):
        return pl.ds(pl.multiple_of(i * n, n), n)

    def at_rows(start, n, unit):
        return pl.ds(pl.multiple_of(start, unit), n)

    heads = [lax.rem(me_h + d, nh) for d in range(1, nh)]

    def to_heads(f):
        for other in heads:
            f(other)

    def to_twins(f):
        def step(k, c):
            f(lax.rem(half + k, NK) * 2 + par)
            return c

        lax.fori_loop(1, NK, step, 0)

    def repeat(n, f):
        if n == 1:
            return f(0)

        def step(k, c):
            f(k)
            return c

        lax.fori_loop(0, n, step, 0)

    load(r.media.at[0], r.media_b.at[0], ld.m0)
    load(r.w_key, r.wkv_o.at[:, pl.ds(0, W)], ld.w)
    load(r.w_value, r.wkv_o.at[:, pl.ds(W, W)], ld.w)
    load(r.w_query, r.wq_o, ld.w)
    load(r.latents, r.lat, ld.lat)
    load(r.media.at[1], r.media_b.at[1], ld.m1)
    barrier = pltpu.get_barrier_semaphore()
    to_heads(
        lambda o: pl.semaphore_signal(
            barrier, inc=1, device_id=(me_i, o), device_id_type=MESH
        )
    )
    repeat(
        ni - 1,
        lambda k: pl.semaphore_signal(
            barrier, inc=1, device_id=(lax.rem(me_i + 1 + k, ni), me_h), device_id_type=MESH
        ),
    )
    pl.semaphore_wait(barrier, nh - 1 + ni - 1)

    Q, QC = z.Q, z.QC
    share = lax.rem(me_i, Q)
    first = me_i - share
    wo_part = at_rows(me_h * W + share * QC, QC, QC)
    to_heads(
        lambda o: send(r.w_out.at[rows_of(share, QC)], r.wout_f.at[wo_part], link.wout_z, me_i, o)
    )
    own_f = rows_of(me_i, FU)

    def spread_rows(src, buf, twins, pair):
        to_twins(lambda o: send(src, buf.at[own_f], twins, o, me_h, times=NK - 1))
        send(src, buf.at[own_f], pair, mate, me_h)

    spread_rows(r.w_up, r.up_f, link.up_x, link.up_p)
    load(r.w_out, r.wout_f.at[rows_of(me_h, W)], ld.ff)
    load(r.w_up, r.up_f.at[own_f], ld.ff)
    load(r.w_down, r.down_f.at[own_f], ld.ff)
    own_l = rows_of(me_h, LR)
    load(r.cot, r.cot_f.at[:, own_l, :], ld.ff)
    own_kv = [at_rows(me_h * 2 * W + k * W, W, W) for k in range(2)]
    own_w = rows_of(me_h, W)
    own_c = rows_of(me_i, RC)
    load(r.w_key.at[own_c], r.wkv_f.at[own_c, own_kv[0]], ld.kvq)
    load(r.w_value.at[own_c], r.wkv_f.at[own_c, own_kv[1]], ld.kvq)
    load(r.w_query.at[own_c], r.wq_f.at[own_c, own_w], ld.kvq)
    load(r.media.at[:, rows_of(me_h, SR), :], r.media_o, ld.mo)

    gain_m, bias_m = r.g_m[...], r.b_m[...]
    gain_l, bias_l = r.g_l[...], r.b_l[...]
    gain_f, bias_f = r.g_f[...], r.b_f[...]

    def normalize_rows(read, write, n):
        side = min(n // TILE, SIDE)

        def step(b):
            ks = [b * side + j for j in range(side)]
            mean = [jnp.sum(read(k), axis=-1, keepdims=True) * (1.0 / D) for k in ks]
            var = [
                jnp.sum(jnp.square(read(k) - m), axis=-1, keepdims=True) * (1.0 / D)
                for k, m in zip(ks, mean)
            ]
            inv = [lax.rsqrt(v + EPSILON) for v in var]
            for k, m, i in zip(ks, mean, inv):
                write(k, (read(k) - m) * i, i)

        repeat(n // TILE // side, step)

    def norm_back_rows(read, write, n, gain, k_gain):
        side = min(n // TILE, SIDE)

        def step(b):
            ks = [b * side + j for j in range(side)]
            means = []
            for k in ks:
                u, hat, _ = read(k)
                u = u * gain
                means.append(
                    [jnp.sum(v, axis=-1, keepdims=True) * (1.0 / D) for v in (u, u * hat)]
                )
            gains = biases = jnp.zeros((8, D), F32)
            for k, (one, two) in zip(ks, means):
                u, hat, inv = read(k)
                write(k, inv * (u * gain - one - hat * two))
                gains, biases = gains + fold_rows(u * hat), biases + fold_rows(u)
            r.vacc[k_gain] += gains
            r.vacc[k_gain + 1] += biases

        repeat(n // TILE // side, step)

    lane_head = lax.div(lax.broadcasted_iota(jnp.int32, (L, W), 1), HS)

    def spread(x):
        zero = jnp.zeros_like(x)
        return jnp.concatenate([jnp.where(lane_head == k, x, zero) for k in range(HN)], axis=0)

    def gather_diag(x):
        out = x[:L]
        for k in range(1, HN):
            out = jnp.where(lane_head == k, x[k * L : (k + 1) * L], out)
        return out

    loaded(ld.w, 3 * D * W * 2)
    loaded(ld.lat, G * L * D * 2)

    def cot_push(g, source, way):
        part = rows_of(source, LR)
        view = r.cot_f.at[g, part, :]
        return lambda src, s: push(src, view, link.cot, me_i, me_h + way, g * nh + source, s)

    def cot_start(g):
        for s, way in enumerate((1, -1)):

            @pl.when((me_h + way >= 0) & (me_h + way < nh))
            def _():
                cot_push(g, me_h, way)(r.cot.at[g], s)

    def cot_pass(g, d):
        for s, way in enumerate((1, -1)):
            source, onto = me_h - way * d, me_h + way

            @pl.when((source >= 0) & (source < nh))
            def _():
                arrived(link.cot, LR * D * 2, g * nh + source)

            if d < nh - 1:

                @pl.when((source >= 0) & (source < nh) & (onto >= 0) & (onto < nh))
                def _():
                    cot_push(g, source, way)(r.cot_f.at[g, rows_of(source, LR), :], 2 * d + s)

    def cot_step(g):
        if isinstance(g, int):
            for d in range(1, nh):
                if 0 <= g - d < G:
                    cot_pass(g - d, d)
            return
        cot_start(g)
        for d in range(1, nh):

            @pl.when(g >= d)
            def _():
                cot_pass(g - d, d)

    def relay(twins, onto, buf, n):
        arrived(twins, (NK - 1) * size(buf.at[rows_of(0, n)]))
        to_twins(
            lambda o: send(
                buf.at[rows_of(o, n)], buf.at[rows_of(o, n)], onto, mate, me_h, times=NK - 1
            )
        )

    def share_wout():
        arrived(link.wout_z, (nh - 1) * QC * D * 2)

        def one(k):
            other = first + lax.rem(share + 1 + k, Q)

            def part(o):
                at = r.wout_f.at[at_rows(o * W + share * QC, QC, QC)]
                send(at, at, link.wout_x, other, me_h, times=Q - 1)

            to_heads(part)

        repeat(Q - 1, one)
        spread_rows(r.w_down, r.down_f, link.dn_x, link.dn_p)

    def image(g):
        slot = lax.rem(g, 2)
        for k, sem in enumerate((ld.m0, ld.m1)):

            @pl.when(slot == k)
            def _():
                loaded(sem, S * D * 2)

        def put_media(k, hat, _):
            r.keys[at_rows(g * T + k * TILE, TILE, TILE), :] = (hat * gain_m + bias_m).astype(BF16)

        def put_latent(k, hat, _):
            y = (hat * gain_l + bias_l).astype(BF16)
            r.keys[at_rows(g * T + S + k * TILE, TILE, TILE), :] = y
            r.lat_n[at_rows(g * L + k * TILE, TILE, TILE), :] = y

        normalize_rows(lambda k: r.media_b[slot, rows_of(k, TILE), :].astype(F32), put_media, S)
        normalize_rows(lambda k: r.lat[g, rows_of(k, TILE), :].astype(F32), put_latent, L)
        for k, sem in enumerate((ld.m0, ld.m1)):

            @pl.when((slot == k) & (g + 2 < G))
            def _():
                load(r.media.at[g + 2], r.media_b.at[k], sem)

        rows, lat_rows = rows_of(g, T), rows_of(g, L)
        kv = dot(r.keys[rows, :], r.wkv_o[...], NN).astype(BF16)
        r.kv[rows, :] = kv
        q = (dot(r.lat_n[lat_rows, :], r.wq_o[...], NN) * (HS**-0.5)).astype(BF16)
        r.q[lat_rows, :] = q
        scores = dot(kv[:, :W], spread(q), NT)
        place = lax.broadcasted_iota(jnp.int32, scores.shape, 0)
        scores = jnp.where((place < r.counts[g]) | (place >= S), scores, -1e30)
        top = jnp.max(scores, axis=0, keepdims=True)
        total = jnp.sum(jnp.exp(scores - top), axis=0, keepdims=True)
        probs = jnp.exp(scores - (top + jnp.log(total)))
        r.probs[rows, :] = probs
        att = gather_diag(dot(probs.astype(BF16), kv[:, W:], TN)).astype(BF16)
        r.att_f[g, :, own_w] = att
        own_att = r.att_f.at[g, :, own_w]
        to_heads(lambda o: send(own_att, own_att, link.att, me_i, o, g, times=G))
        cot_step(g)

        @pl.when(g == 1)
        def _():
            share_wout()

        @pl.when(g == G - 2)
        def _():
            relay(link.up_x, link.up_y, r.up_f, FU)

    repeat(G, image)
    cot_step(G)

    def send_kvq(o):
        send(r.w_key.at[own_c], r.wkv_f.at[own_c, own_kv[0]], link.kv_z, me_i, o)
        send(r.w_value.at[own_c], r.wkv_f.at[own_c, own_kv[1]], link.kv_z, me_i, o)
        send(r.w_query.at[own_c], r.wq_f.at[own_c, own_w], link.kv_z, me_i, o)

    to_heads(send_kvq)
    r.vacc[...] = jnp.zeros_like(r.vacc)

    CR, CG = R // 2, G // 2
    loaded(ld.ff, (W + 2 * FU + G * LR) * D * 2)
    arrived(link.wout_x, (Q - 1) * (nh - 1) * QC * D * 2)

    def ff_forward(b):
        for k in range(CG):
            arrived(link.att, (nh - 1) * L * W * 2, b * CG + k)
        at = rows_of(b, CR)
        imgs = pl.ds(b * CG, CG)
        att = r.att_f[imgs, :, :].reshape(CR, nh * W)
        base = r.lat[imgs, :, :].reshape(CR, D).astype(F32)
        r.tmp[:, :D] = dot(att, r.wout_f[...], NN) + base
        for k in range(nh):

            @pl.when(me_h == k)
            def _():
                r.mid_o[imgs] = r.tmp[:, :D].reshape(CG, nh, LR, D)[:, k]

        def put_norm(k, hat, inv):
            row = at_rows(b * CR + k * TILE, TILE, TILE)
            r.hat[row, :] = hat
            r.inv[row, :] = jnp.broadcast_to(inv, (TILE, LANES))
            r.ff_in[row, :] = (hat * gain_f + bias_f).astype(BF16)

        normalize_rows(lambda k: r.tmp[rows_of(k, TILE), :D], put_norm, CR)
        for k in range(1, min(nh - 1, 3)):

            @pl.when(b == k - 1)
            def _():
                cot_step(G + k)

        @pl.when(b == 0)
        def _():
            arrived(link.up_p, FU * D * 2)
            arrived(link.up_y, (NK - 1) * FU * D * 2)

        r.tmp[:, :FH] = dot(r.ff_in[at, :], r.up_f[...], NT)

        def gelu(k):
            row = at_rows(b * CR + k * TILE, TILE, TILE)
            value, slope = gelu_parts(r.tmp[rows_of(k, TILE), :FH])
            r.act[row, :] = value.astype(BF16)
            r.slope[row, :] = slope

        repeat(CR // TILE, gelu)

    repeat(2, ff_forward)
    for k in range(3, nh - 1):
        cot_step(G + k)
    relay(link.dn_x, link.dn_y, r.down_f, FU)
    arrived(link.dn_p, FU * D * 2)
    arrived(link.dn_y, (NK - 1) * FU * D * 2)

    def ff_backward(b):
        at, imgs = rows_of(b, CR), pl.ds(b * CG, CG)
        r.tmp[:, :FH] = dot(r.cot_f[imgs, :, :].reshape(CR, D), r.down_f[...], NT)

        def slope(k):
            row = at_rows(b * CR + k * TILE, TILE, TILE)
            r.gh[row, :] = (r.tmp[rows_of(k, TILE), :FH] * r.slope[row, :]).astype(BF16)

        repeat(CR // TILE, slope)
        r.tmp[:, :D] = dot(r.gh[at, :], r.up_f[...], NN)

        def read(k):
            row = at_rows(b * CR + k * TILE, TILE, TILE)
            return r.tmp[rows_of(k, TILE), :D], r.hat[row, :], r.inv[row, :1]

        def write(k, grad):
            g, part = b * CG + k * TILE // L, rows_of(k % (L // TILE), TILE)
            cot = r.cot_f[g, part, :].astype(F32) * (1.0 / nh)
            r.gm_p[g, part, :] = (grad + cot).astype(BF16)

        norm_back_rows(read, write, CR, gain_f, 4)
        ga = dot(r.gm_p[imgs, :, :].reshape(CR, D), r.wout_f[...], NT)
        r.ga_p[imgs, :, :] = ga.astype(BF16).reshape(CG, L, nh * W)
        to_heads(
            lambda o: send(
                r.ga_p.at[imgs, :, rows_of(o, W)], r.ga_r.at[me_h, imgs], link.ga, me_i, o, b,
                times=2,
            )
        )

    repeat(2, ff_backward)

    def share_kvq(o, to, times):
        for buf in (r.wkv_f, r.wq_f):
            send(buf.at[own_c], buf.at[own_c], to, o, me_h, times=times)

    def relay_kvq(o):
        for buf in (r.wkv_f, r.wq_f):
            at = buf.at[rows_of(o, RC)]
            send(at, at, link.kv_y, mate, me_h, times=NK - 1)

    loaded(ld.kvq, 3 * RC * W * 2)
    arrived(link.kv_z, (nh - 1) * 3 * RC * W * 2)
    to_twins(lambda o: share_kvq(o, link.kv_x, NK - 1))
    share_kvq(mate, link.kv_p, 1)

    def ff_out(b):
        out = dot(r.act[rows_of(b, CR), :], r.down_f[...], NN)
        r.ffo_p[pl.ds(b * CG, CG), :, :] = out.astype(BF16).reshape(CG, L, D)

    repeat(2, ff_out)

    def scatter_pair(buf, got, n, to):
        repeat(
            NK,
            lambda k: send(
                buf.at[rows_of(2 * k + 1 - par, n)], got.at[rows_of(k, n)], to, mate, me_h, times=NK
            ),
        )

    def scatter_twins(buf, got, got2, n, to, to2):
        arrived(to, size(got))

        def step(d, c):
            k = lax.rem(half + d, NK)
            mine = rows_of(2 * k + par, n)
            both = buf[mine, :].astype(F32) + got[rows_of(k, n), :].astype(F32)
            buf[mine, :] = both.astype(BF16)
            send(
                buf.at[mine], got2.at[rows_of(half, n)], to2, 2 * k + par, me_h, times=NK - 1
            )
            return c

        lax.fori_loop(1, NK, step, 0)

    def scatter_sum(buf, got, got2, n, to2, total):
        arrived(to2, size(got2) // NK * (NK - 1))
        total[...] = buf[rows_of(me_i, n), :].astype(F32) + got[rows_of(half, n), :].astype(F32)

        def step(d, c):
            total[...] += got2[rows_of(lax.rem(half + d, NK), n), :].astype(F32)
            return c

        lax.fori_loop(1, NK, step, 0)

    FT = 2 * LANES

    def down_grad(t):
        at = rows_of(t, FT)
        r.wd[at, :] = dot(r.act[:, at], r.cot_f[...].reshape(R, D), TN).astype(BF16)

    repeat(FH // FT, down_grad)
    scatter_pair(r.wd, r.wd1, FU, link.wd1)

    def up_grad(t):
        at = rows_of(t, FT)
        r.wu[at, :] = dot(r.gh[:, at], r.ff_in[...], TN).astype(BF16)

    repeat(FH // FT, up_grad)
    scatter_pair(r.wu, r.wu1, FU, link.wu1)

    def out_grad(t):
        at = rows_of(t, FT)
        left = r.gm_p[:, :, at].reshape(R, FT)
        r.wo[at, :] = dot(left, r.att_f[...].reshape(R, nh * W), TN).astype(BF16)

    repeat(D // FT, out_grad)
    scatter_pair(r.wo, r.wo1, RC, link.wo1)

    loaded(ld.mo, G * SR * D * 2)

    def keep(hats, invs):
        def put(k, hat, inv):
            hats[k] = hat
            invs[k] = jnp.broadcast_to(inv, (TILE, LANES))

        return put

    NM, NL = SR // TILE, LR // TILE
    normalize_rows(
        lambda k: r.media_o[k // NM, rows_of(k % NM, TILE), :].astype(F32),
        keep(r.hat_m, r.inv_m), G * SR,
    )
    normalize_rows(
        lambda k: r.lat[k // NL, at_rows(me_h * LR + (k % NL) * TILE, TILE, TILE), :].astype(F32),
        keep(r.hat_l, r.inv_l), G * LR,
    )

    for b in range(2):
        arrived(link.ga, (nh - 1) * CG * L * W * 2, b)
    wide = rows_of(me_h, 2 * W)

    def image_back(g):
        rows, lat_rows = rows_of(g, T), rows_of(g, L)
        ga = r.ga_p[g, :, own_w].astype(F32)
        for o in heads:
            ga = ga + r.ga_r[o, g].astype(F32)
        ga = spread(ga.astype(BF16))
        q = spread(r.q[lat_rows, :])
        key, value = r.kv[rows, :W], r.kv[rows, W:]
        probs = r.probs[rows, :]
        grad_probs = dot(value, ga, NT)
        delta = jnp.sum(probs * grad_probs, axis=0, keepdims=True)
        grad_scores = (probs * (grad_probs - delta)).astype(BF16)
        r.gkv[g, :, W:] = dot(probs.astype(BF16), ga, NN).astype(BF16)
        r.gkv[g, :, :W] = dot(grad_scores, q, NN).astype(BF16)
        grad_query = gather_diag(dot(grad_scores, key, TN)).astype(BF16)
        r.gq[g] = (grad_query.astype(F32) * (HS**-0.5)).astype(BF16)

        def go(o):
            part = r.gkv_r.at[g, pl.ds(0, SR), wide]
            send(r.gkv.at[g, rows_of(o, SR), :], part, link.gkv, me_i, o, g, times=G)
            part = r.gkv_r.at[g, pl.ds(SR, LR), wide]
            at = at_rows(S + o * LR, LR, LR)
            send(r.gkv.at[g, at, :], part, link.gkv, me_i, o, g, times=G)
            part = r.gq_r.at[g, :, own_w]
            send(r.gq.at[g, rows_of(o, LR), :], part, link.gq, me_i, o, times=G)

        to_heads(go)
        r.gkv_r[g, :SR, wide] = r.gkv[g, rows_of(me_h, SR), :]
        r.gkv_r[g, SR:, wide] = r.gkv[g, at_rows(S + me_h * LR, LR, LR), :]
        r.gq_r[g, :, own_w] = r.gq[g, own_l, :]

    repeat(G, image_back)

    BLOCK = G * LR * D * 2

    def line_push(part, got, to, o, way):
        onto = me_h + way
        slot = o if way < 0 else jnp.where(o == onto, nh, o)
        push(part.at[:, rows_of(o, LR), :], got.at[slot], to, me_i, onto, slot, o)

    def line_start(part, got, to):
        @pl.when(me_h == nh - 1)
        def _():
            for o in range(nh - 1):
                line_push(part, got, to, o, -1)
            got[nh - 1] = jnp.zeros((G, LR, D), BF16)

        @pl.when(me_h == 0)
        def _():
            for o in range(nh - 1, 0, -1):
                line_push(part, got, to, o, 1)
            got[nh] = jnp.zeros((G, LR, D), BF16)

    def line_pass(part, got, to, k):
        for o, way in ((k, -1), (nh - 1 - k, 1)):
            ahead = (o < me_h) & (me_h < nh - 1) if way < 0 else (o > me_h) & (me_h > 0)

            @pl.when(ahead)
            def _():
                arrived(to, BLOCK, o)

                def add(g):
                    at = rows_of(o, LR)
                    both = part[g, at, :].astype(F32) + got[o, g].astype(F32)
                    part[g, at, :] = both.astype(BF16)

                repeat(G, add)
                line_push(part, got, to, o, way)

    def line_end(part, got, to, base, total):
        @pl.when(me_h < nh - 1)
        def _():
            arrived(to, BLOCK, me_h)

        @pl.when(me_h > 0)
        def _():
            arrived(to, BLOCK, nh)

        def add(g):
            x = base[g] + part[g, own_l, :].astype(F32)
            x = x + got[me_h, g].astype(F32) + got[nh, g].astype(F32)
            total[g] = x.astype(BF16)

        repeat(G, add)

    line_start(r.ffo_p, r.ffo_r, link.ffo)
    line_start(r.gm_p, r.gm_r, link.gm)
    scatter_twins(r.wd, r.wd1, r.wd2, FU, link.wd1, link.wd2)
    scatter_twins(r.wu, r.wu1, r.wu2, FU, link.wu1, link.wu2)
    scatter_twins(r.wo, r.wo1, r.wo2, RC, link.wo1, link.wo2)

    def proj_grad(t):
        at = rows_of(t, FT)
        left = r.gkv[...].reshape(G * T, 2 * W)
        r.wa[at, : 2 * W] = dot(r.keys[:, at], left, TN).astype(BF16)
        r.wa[at, 2 * W :] = dot(r.lat_n[:, at], r.gq[...].reshape(R, W), TN).astype(BF16)

    repeat(D // FT, proj_grad)
    scatter_pair(r.wa, r.wa1, RC, link.wa1)
    arrived(link.kv_x, (NK - 1) * 3 * nh * RC * W * 2)
    to_twins(relay_kvq)
    scatter_twins(r.wa, r.wa1, r.wa2, RC, link.wa1, link.wa2)
    arrived(link.kv_p, 3 * nh * RC * W * 2)
    arrived(link.kv_y, (NK - 1) * 3 * nh * RC * W * 2)

    arrived(link.gq, (nh - 1) * G * LR * W * 2)
    KR = SR + LR

    def put(k, at=slice(None)):
        name = list(outs)[k]
        a, b = getattr(out, name).at[at], getattr(dst, name).at[at]
        pltpu.make_async_copy(a, b, out_sems.at[k]).start()

    def own_rows(b):
        for k in range(2):
            arrived(link.gkv, (nh - 1) * KR * 2 * W * 2, 2 * b + k)
        two = pl.ds(2 * b, 2)
        left = r.gkv_r[two, :, :].reshape(2 * KR, nh * 2 * W)
        r.tmp[: 2 * KR, :D] = dot(left, r.wkv_f[...], NT)
        query = dot(r.gq_r[two, :, :].reshape(2 * LR, nh * W), r.wq_f[...], NT)
        for k in range(2):
            r.tmp[pl.ds(k * KR + SR, LR), :D] += query[k * LR : (k + 1) * LR]

        def read_media(j):
            k = j // NM
            u = r.tmp[at_rows(k * KR + (j % NM) * TILE, TILE, TILE), :D]
            return u, r.hat_m[b * 2 * NM + j], r.inv_m[b * 2 * NM + j][:, :1]

        def write_media(j, grad):
            out.mg[2 * b + j // NM, rows_of(j % NM, TILE), :] = grad.astype(BF16)

        norm_back_rows(read_media, write_media, 2 * SR, gain_m, 0)
        def read_latent(j):
            at = at_rows((j // NL) * KR + SR + (j % NL) * TILE, TILE, TILE)
            return r.tmp[at, :D], r.hat_l[b * 2 * NL + j], r.inv_l[b * 2 * NL + j][:, :1]

        def write_latent(j, grad):
            r.glat[2 * b + j // NL, rows_of(j % NL, TILE), :] = grad

        norm_back_rows(read_latent, write_latent, 2 * LR, gain_l, 2)
        put(1, two)

    repeat(G // 2, own_rows)

    for k in range(6):
        r.vec[k : k + 1, :] = jnp.sum(r.vacc[k], axis=0, keepdims=True)
    r.vec[6:8, :] = jnp.zeros((2, D), F32)

    def block(i):
        return at_rows(lax.div(i * RC, LANES) * LANES, LANES, LANES)

    def vec_step(k):
        o = lax.rem(me_i + 1 + k, ni)
        send(r.vec.at[:, block(o)], r.vec_r.at[me_i], link.vp, o, me_h, times=ni - 1)

    repeat(ni - 1, vec_step)

    line_pass(r.ffo_p, r.ffo_r, link.ffo, 0)
    scatter_sum(r.wd, r.wd1, r.wd2, FU, link.wd2, out.dn)
    line_pass(r.ffo_p, r.ffo_r, link.ffo, 1)
    scatter_sum(r.wu, r.wu1, r.wu2, FU, link.wu2, out.up)
    for k in range(2, nh - 2):
        line_pass(r.ffo_p, r.ffo_r, link.ffo, k)
    scatter_sum(r.wo, r.wo1, r.wo2, RC, link.wo2, r.tmp.at[:RC, : nh * W])
    for k in range(nh):
        r.wo_s[k] = r.tmp[:RC, k * W : (k + 1) * W].astype(BF16)
    to_heads(lambda o: send(r.wo_s.at[o], r.wo_z.at[me_h], link.wo3, me_i, o))
    scatter_sum(r.wa, r.wa1, r.wa2, RC, link.wa2, out.wa)
    arrived(link.vp, (ni - 1) * 8 * LANES * 4)
    r.vec_t[...] = r.vec[:, block(me_i)]

    def vec_sum(k):
        r.vec_t[...] += r.vec_r[lax.rem(me_i + 1 + k, ni)]

    repeat(ni - 1, vec_sum)
    to_heads(lambda o: send(r.vec_t, r.vec_z.at[me_h], link.vz, me_i, o))
    for k in range(nh - 2):
        line_pass(r.gm_p, r.gm_r, link.gm, k)
    line_end(r.ffo_p, r.ffo_r, link.ffo, r.mid_o, out.lat)
    arrived(link.wo3, (nh - 1) * RC * W * 2)
    total = r.tmp[:RC, own_w]
    for o in heads:
        total = total + r.wo_z[o].astype(F32)
    out.wo[...] = total
    arrived(link.vz, (nh - 1) * 8 * LANES * 4)
    total = r.vec_t[...]
    for o in heads:
        total = total + r.vec_z[o]
    out.vec[...] = total
    for k in range(len(outs)):
        if k not in (1, 2):
            put(k)
    line_end(r.gm_p, r.gm_r, link.gm, r.glat, out.lg)
    put(2)

    for to in vars(link).values():
        if to.bytes:
            await_bytes(send_sems.at[to.send], to.bytes)
    for d in range(nh - 1):
        for s, way in enumerate((1, -1)):
            source, onto = me_h - way * d, me_h + way

            @pl.when((source >= 0) & (source < nh) & (onto >= 0) & (onto < nh))
            def _():
                await_bytes(send_sems.at[link.cot.send + 2 * d + s], BLOCK)

    for to in (link.ffo, link.gm):
        for o in range(nh):

            @pl.when(me_h != o)
            def _():
                await_bytes(send_sems.at[to.send + o], BLOCK)

    for k, name in enumerate(outs):
        pltpu.make_async_copy(getattr(out, name), getattr(dst, name), out_sems.at[k]).wait()


def finish(z, *refs):
    n = len(outputs(z)) - 1
    src, dst, buf, turned, in_sems, out_sems = (
        refs[:n], refs[n : n + 9], refs[n + 9 : 2 * n + 9], refs[-3], refs[-2], refs[-1]
    )
    W = z.W
    loads = [pltpu.make_async_copy(src[k], buf[k], in_sems.at[k]) for k in range(n)]
    for copy in loads:
        copy.start()
    stores = []

    def store(ref, k):
        stores.append(pltpu.make_async_copy(ref, dst[k], out_sems.at[k]))
        stores[-1].start()

    lat, mg, lg, wa, wo, up, dn = range(7)
    loads[mg].wait()
    store(buf[mg], 1)
    loads[up].wait()
    store(buf[up], 7)
    loads[dn].wait()
    store(buf[dn], 8)
    loads[lat].wait()
    store(buf[lat], 0)
    loads[lg].wait()
    store(buf[lg], 2)
    loads[wa].wait()
    store(buf[wa].at[:, pl.ds(2 * W, W)], 3)
    store(buf[wa].at[:, pl.ds(0, W)], 4)
    store(buf[wa].at[:, pl.ds(W, W)], 5)
    loads[wo].wait()
    turned[...] = buf[wo][...].T
    store(turned, 6)
    for copy in stores:
        copy.wait()


def body(ni, nh, media, latents, counts, media_gain, media_bias, latent_gain, latent_bias, w_query,
         w_key, w_value, w_out, ff_gain, ff_bias, w_up, w_down, cotangent):
    z = sizes(ni, nh, media, latents, w_query, w_up)
    D, W, RC = z.D, z.W, z.RC
    vm = pl.BlockSpec(memory_space=pltpu.VMEM)
    hbm = pl.BlockSpec(memory_space=pl.ANY)
    dma = pltpu.SemaphoreType.DMA
    outs = list(outputs(z).values())
    rows = [
        v.reshape(1, D)
        for v in (media_gain, media_bias, latent_gain, latent_bias, ff_gain, ff_bias)
    ]
    counted = links(z).values()
    res = pl.pallas_call(
        functools.partial(kernel, z),
        out_shape=[jax.ShapeDtypeStruct(s, d) for s, d in outs],
        in_specs=[pl.BlockSpec(memory_space=pltpu.SMEM)] + [vm] * 6 + [hbm] * 9,
        out_specs=[hbm] * len(outs),
        scratch_shapes=[pltpu.VMEM(s, d) for s, d in (*scratch(z).values(), *outs)]
        + [
            dma((sum(a for a, _ in counted),)),
            dma((sum(b for _, b in counted),)),
            dma((len(LOADS),)),
            dma((len(outs),)),
        ],
        compiler_params=pltpu.CompilerParams(
            collective_id=0, has_side_effects=True, vmem_limit_bytes=67043328
        ),
    )(counts, *rows, media, latents, w_query, w_key, w_value, w_out, w_up, w_down, cotangent)
    last = outs[:3] + [((RC, W), F32)] * 3 + [((W, RC), F32)] + outs[5:7]
    res2 = pl.pallas_call(
        functools.partial(finish, z),
        out_shape=[jax.ShapeDtypeStruct(s, d) for s, d in last],
        in_specs=[hbm] * 7,
        out_specs=[hbm] * 9,
        scratch_shapes=[pltpu.VMEM(s, d) for s, d in outs[:7]]
        + [pltpu.VMEM((W, RC), F32), dma((7,)), dma((9,))],
    )(*res[:7])
    lat_out, media_grad, lat_grad, wq, wk, wv, wo, up, down = res2
    share = D // (ni * nh)
    place = lax.axis_index("img") * nh + lax.axis_index("head")
    vec = lax.dynamic_slice(res[7], (0, lax.rem(place * share, LANES)), (8, share))
    return (
        lat_out, media_grad, lat_grad, vec[0], vec[1], vec[2], vec[3], wq, wk, wv, wo, vec[4],
        vec[5], up, down,
    )


def solution(mesh):
    ni, nh = mesh.shape["img"], mesh.shape["head"]
    both = P(("img", "head"))
    rows = P("img", "head", None)
    return jax.shard_map(
        functools.partial(body, ni, nh),
        mesh=mesh,
        in_specs=(
            P("img", None, None), P("img", None, None), P("img"), P(), P(), P(), P(),
            P(None, "head"), P(None, "head"), P(None, "head"), P("head", None), P(), P(),
            P(("img", "head"), None), P(("img", "head"), None), rows,
        ),
        out_specs=(
            rows, rows, rows, both, both, both, both, P("img", "head"), P("img", "head"),
            P("img", "head"), P("head", "img"), both, both, P(("img", "head"), None),
            P(("img", "head"), None),
        ),
        check_vma=False,
    )
```

```python
import functools
import math
from types import SimpleNamespace

import jax
import jax.numpy as jnp
from jax import lax
from jax.experimental import pallas as pl
from jax.experimental.pallas import tpu as pltpu
from jax.sharding import PartitionSpec as P

HS = 64
EPSILON = 1e-05
LANES = 128
TILE = 16
SIDE = 16
BF16 = jnp.bfloat16
F32 = jnp.float32
MESH = pl.DeviceIdType.MESH
NN = ((1,), (0,))
NT = ((1,), (1,))
TN = ((0,), (0,))


def dot(a, b, dims):
    return lax.dot_general(a, b, (dims, ((), ())), preferred_element_type=F32)


def fold_rows(x):
    return jnp.sum(x.reshape(x.shape[0] // 8, 8, x.shape[1]), axis=0)


def gelu_parts(hidden):
    normal_cdf = 0.5 * (1.0 + lax.erf(hidden * (1.0 / math.sqrt(2.0))))
    density = jnp.exp(-0.5 * hidden * hidden) * (1.0 / math.sqrt(2.0 * math.pi))
    return (hidden * normal_cdf, normal_cdf + hidden * density)


def sizes(ni, nh, media, latents, w_query, w_up):
    G, S, D = media.shape
    L, W, FU = latents.shape[1], w_query.shape[1], w_up.shape[0]
    Q = min(ni, W // TILE)
    return SimpleNamespace(
        ni=ni, nh=nh, G=G, S=S, D=D, L=L, W=W, FU=FU, T=S + L, SR=S // nh, LR=L // nh, R=G * L,
        FH=ni * FU, RC=D // ni, NK=ni // 2, NH=nh // 2, HN=W // HS, Q=Q, QC=W // Q,
    )


def outputs(z):
    return dict(
        lat=((z.G, z.LR, z.D), BF16),
        mg=((z.G, z.SR, z.D), BF16),
        lg=((z.G, z.LR, z.D), BF16),
        wa=((z.RC, 3 * z.W), F32),
        wo=((z.RC, z.W), F32),
        up=((z.FU, z.D), F32),
        dn=((z.FU, z.D), F32),
        vec=((8, LANES), F32),
    )


def scratch(z):
    G, D, L, W, T, SR, LR, R, FH, RC, NK, NH, FU, nh = (
        z.G, z.D, z.L, z.W, z.T, z.SR, z.LR, z.R, z.FH, z.RC, z.NK, z.NH, z.FU, z.nh
    )
    return dict(
        media_b=((2, z.S, D), BF16),
        media_o=((G, SR, D), BF16),
        lat=((G, L, D), BF16),
        keys=((G * T, D), BF16),
        lat_n=((R, D), BF16),
        wkv_o=((D, 2 * W), BF16),
        wq_o=((D, W), BF16),
        wkv_f=((D, nh * 2 * W), BF16),
        wq_f=((D, nh * W), BF16),
        wout_f=((nh * W, D), BF16),
        up_f=((FH, D), BF16),
        down_f=((FH, D), BF16),
        cot_f=((G, L, D), BF16),
        kv=((G * T, 2 * W), BF16),
        q=((R, W), BF16),
        probs=((G * T, z.HN * L), F32),
        att_f=((G, L, nh * W), BF16),
        mid_o=((G, LR, D), F32),
        hat=((R, D), F32),
        inv=((R, LANES), F32),
        ff_in=((R, D), BF16),
        act=((R, FH), BF16),
        slope=((R, FH), F32),
        gh=((R, FH), BF16),
        tmp=((R // 2, max(D, FH)), F32),
        ffo_p=((G, L, D), BF16),
        gm_p=((G, L, D), BF16),
        ga_p=((G, L, nh * W), BF16),
        ffo1=((NH, G, LR, D), BF16),
        ffo2=((NH, G, LR, D), BF16),
        gm1=((NH, G, LR, D), BF16),
        gm2=((NH, G, LR, D), BF16),
        ga1=((NH, G, L, W), BF16),
        ga2=((NH, G, L, W), BF16),
        ga_f=((nh, G, L, W), BF16),
        lse=((nh, G, z.HN * L), F32),
        delta=((nh, G, z.HN * L), F32),
        keys_o=((G * (SR + LR), D), BF16),
        kv_h=((G * (SR + LR), 2 * W), BF16),
        q_h=((R, W), BF16),
        gkv=((G, T, 2 * W), BF16),
        gq=((G, L, W), BF16),
        gkv_r=((G, SR + LR, nh * 2 * W), BF16),
        gq_r=((G, LR, nh * W), BF16),
        wu=((FH, D), BF16),
        wd=((FH, D), BF16),
        wo=((D, nh * W), BF16),
        wa=((D, 3 * W), BF16),
        wu1=((NK * FU, D), BF16),
        wd1=((NK * FU, D), BF16),
        wo1=((NK * RC, nh * W), BF16),
        wa1=((NK * RC, 3 * W), BF16),
        wu2=((NK * FU, D), BF16),
        wd2=((NK * FU, D), BF16),
        wo2=((NK * RC, nh * W), BF16),
        wa2=((NK * RC, 3 * W), BF16),
        wo_s=((nh, RC, W), BF16),
        wo_z=((nh, RC, W), BF16),
        glat=((G, LR, D), F32),
        hat_m=((G * SR // TILE, TILE, D), F32),
        inv_m=((G * SR // TILE, TILE, LANES), F32),
        hat_l=((G * LR // TILE, TILE, D), F32),
        inv_l=((G * LR // TILE, TILE, LANES), F32),
        vacc=((6, 8, D), F32),
        vec=((8, D), F32),
        vec_r=((z.ni, 8, LANES), F32),
        vec_t=((8, LANES), F32),
        vec_z=((nh, 8, LANES), F32),
    )


def links(z):
    G = z.G
    one = (1, 1)
    return dict(
        wout_z=one, wout_x=one, up_p=one, up_x=one, up_y=one, dn_p=one, dn_x=one, dn_y=one,
        kvq_t=one, kvq_m=one, kvq_y=one, kv_p=one, kv_x=one, kv_y=one,
        cot_t=one, cot_m=one, cot_y=one, att_t=(G, 1), att_m=(G, 1), att_y=(G, 1), lse=one,
        delta=one, ga1=(2, 1), ga2=(2, 1), ga_t=one, ga_m=one, ga_y=one, gq=one,
        ffo1=one, ffo2=one, gm1=one, gm2=one,
        wu1=one, wu2=one, wd1=one, wd2=one, wo1=one, wo2=one, wo3=one, wa1=one, wa2=one,
        vp=one, vz=one,
    )


LOADS = dict(m0=0, m1=1, w=2, lat=3, ff=4, kvq=5, mo=6)
INS = tuple(
    dict(
        counts=0, g_m=0, b_m=0, g_l=0, b_l=0, g_f=0, b_f=0, media=0, latents=0, w_query=0, w_key=0,
        w_value=0, w_out=0, w_up=0, w_down=0, cot=0,
    )
)


def kernel(z, *refs):
    outs, vmem = outputs(z), scratch(z)
    n_in, n_out = len(INS), len(outs)
    r = SimpleNamespace(
        **dict(zip(INS, refs[:n_in])),
        **dict(zip(vmem, refs[n_in + n_out :])),
    )
    dst = SimpleNamespace(**dict(zip(outs, refs[n_in : n_in + n_out])))
    out = SimpleNamespace(**dict(zip(outs, refs[n_in + n_out + len(vmem) :])))
    recv_sems, send_sems, load_sems, out_sems = refs[-4:]
    G, S, D, L, W, FU, T, SR, LR, R, FH, RC, NK, NH, HN = (
        z.G, z.S, z.D, z.L, z.W, z.FU, z.T, z.SR, z.LR, z.R, z.FH, z.RC, z.NK, z.NH, z.HN
    )
    ni, nh = z.ni, z.nh
    me_i, me_h = lax.axis_index("img"), lax.axis_index("head")
    par, half = lax.rem(me_i, 2), lax.div(me_i, 2)
    mate = me_i + 1 - 2 * par
    par_h, half_h = lax.rem(me_h, 2), lax.div(me_h, 2)
    mate_h = me_h + 1 - 2 * par_h
    halves_h = [lax.rem(half_h + k, NH) for k in range(1, NH)]
    twins_h = [2 * k + par_h for k in halves_h]

    link, n_recv, n_send = {}, 0, 0
    for name, (a, b) in links(z).items():
        link[name] = SimpleNamespace(recv=n_recv, send=n_send, bytes=0)
        n_recv, n_send = n_recv + a, n_send + b
    link = SimpleNamespace(**link)
    ld = SimpleNamespace(**LOADS)

    def size(ref):
        return math.prod(ref.shape) * jnp.dtype(ref.dtype).itemsize

    def await_bytes(sem, nbytes):
        lanes = D
        while nbytes % (2 * lanes * TILE):
            lanes //= 2
        assert lanes >= LANES and nbytes // (2 * lanes) <= G * T
        view = r.keys.at[pl.ds(0, nbytes // (2 * lanes)), pl.ds(0, lanes)]
        pltpu.make_async_copy(view, view, sem).wait()

    def load(src, dst, k):
        pltpu.make_async_copy(src, dst, load_sems.at[k]).start()

    def loaded(k, nbytes):
        await_bytes(load_sems.at[k], nbytes)

    def arrived(to, nbytes, k=0):
        await_bytes(recv_sems.at[to.recv + k], nbytes)

    def push(src, dst, to, img, head, k=0, s=0):
        pltpu.make_async_remote_copy(
            src_ref=src,
            dst_ref=dst,
            send_sem=send_sems.at[to.send + s],
            recv_sem=recv_sems.at[to.recv + k],
            device_id=(img, head),
            device_id_type=MESH,
        ).start()

    def send(src, dst, to, img, head, k=0, times=1):
        push(src, dst, to, img, head, k)
        to.bytes += size(src) * times

    def rows_of(i, n):
        return pl.ds(pl.multiple_of(i * n, n), n)

    def at_rows(start, n, unit):
        return pl.ds(pl.multiple_of(start, unit), n)

    heads = [lax.rem(me_h + d, nh) for d in range(1, nh)]

    def to_heads(f):
        for other in heads:
            f(other)

    def to_twins(f):
        def step(k, c):
            f(lax.rem(half + k, NK) * 2 + par)
            return c

        lax.fori_loop(1, NK, step, 0)

    def head_spread(view, src, twins, pair, k=0, times=1):
        for o in twins_h:
            send(src, view(me_h), twins, me_i, o, k, times)
        send(src, view(me_h), pair, me_i, mate_h, k, times)

    def head_relay(view, twins, onto, k=0, times=1):
        arrived(twins, (NH - 1) * size(view(0)), k)
        for o in twins_h:
            send(view(o), view(o), onto, me_i, mate_h, k, times)

    def head_landed(view, pair, onto, k=0):
        arrived(pair, size(view(0)), k)
        arrived(onto, (NH - 1) * size(view(0)), k)

    def head_pair(view, got, to, k=0, times=1):
        for p in range(NH):
            send(view(2 * p + 1 - par_h), got(p), to, me_i, mate_h, k, times)

    def repeat(n, f):
        if n == 1:
            return f(0)

        def step(k, c):
            f(k)
            return c

        lax.fori_loop(0, n, step, 0)

    load(r.media.at[0], r.media_b.at[0], ld.m0)
    load(r.w_key, r.wkv_o.at[:, pl.ds(0, W)], ld.w)
    load(r.w_value, r.wkv_o.at[:, pl.ds(W, W)], ld.w)
    load(r.w_query, r.wq_o, ld.w)
    load(r.latents, r.lat, ld.lat)
    load(r.media.at[1], r.media_b.at[1], ld.m1)
    barrier = pltpu.get_barrier_semaphore()
    to_heads(
        lambda o: pl.semaphore_signal(
            barrier, inc=1, device_id=(me_i, o), device_id_type=MESH
        )
    )
    repeat(
        ni - 1,
        lambda k: pl.semaphore_signal(
            barrier, inc=1, device_id=(lax.rem(me_i + 1 + k, ni), me_h), device_id_type=MESH
        ),
    )
    pl.semaphore_wait(barrier, nh - 1 + ni - 1)

    Q, QC = z.Q, z.QC
    share = lax.rem(me_i, Q)
    first = me_i - share
    wo_part = at_rows(me_h * W + share * QC, QC, QC)
    to_heads(
        lambda o: send(r.w_out.at[rows_of(share, QC)], r.wout_f.at[wo_part], link.wout_z, me_i, o)
    )
    own_f = rows_of(me_i, FU)
    own_l = rows_of(me_h, LR)

    def cot_at(o):
        return r.cot_f.at[:, rows_of(o, LR), :]

    head_spread(cot_at, r.cot, link.cot_t, link.cot_m)

    def spread_rows(src, buf, twins, pair):
        to_twins(lambda o: send(src, buf.at[own_f], twins, o, me_h, times=NK - 1))
        send(src, buf.at[own_f], pair, mate, me_h)

    spread_rows(r.w_up, r.up_f, link.up_x, link.up_p)
    load(r.w_out, r.wout_f.at[rows_of(me_h, W)], ld.ff)
    load(r.w_up, r.up_f.at[own_f], ld.ff)
    load(r.w_down, r.down_f.at[own_f], ld.ff)
    load(r.cot, r.cot_f.at[:, own_l, :], ld.ff)
    own_kv = [at_rows(me_h * 2 * W + k * W, W, W) for k in range(2)]
    own_w = rows_of(me_h, W)
    own_c = rows_of(me_i, RC)
    load(r.w_key.at[own_c], r.wkv_f.at[own_c, own_kv[0]], ld.kvq)
    load(r.w_value.at[own_c], r.wkv_f.at[own_c, own_kv[1]], ld.kvq)
    load(r.w_query.at[own_c], r.wq_f.at[own_c, own_w], ld.kvq)
    load(r.media.at[:, rows_of(me_h, SR), :], r.media_o, ld.mo)

    gain_m, bias_m = r.g_m[...], r.b_m[...]
    gain_l, bias_l = r.g_l[...], r.b_l[...]
    gain_f, bias_f = r.g_f[...], r.b_f[...]

    def normalize_rows(read, write, n):
        side = min(n // TILE, SIDE)

        def step(b):
            ks = [b * side + j for j in range(side)]
            mean = [jnp.sum(read(k), axis=-1, keepdims=True) * (1.0 / D) for k in ks]
            var = [
                jnp.sum(jnp.square(read(k) - m), axis=-1, keepdims=True) * (1.0 / D)
                for k, m in zip(ks, mean)
            ]
            inv = [lax.rsqrt(v + EPSILON) for v in var]
            for k, m, i in zip(ks, mean, inv):
                write(k, (read(k) - m) * i, i)

        repeat(n // TILE // side, step)

    def norm_back_rows(read, write, n, gain, k_gain):
        side = min(n // TILE, SIDE)

        def step(b):
            ks = [b * side + j for j in range(side)]
            means = []
            for k in ks:
                u, hat, _ = read(k)
                u = u * gain
                means.append(
                    [jnp.sum(v, axis=-1, keepdims=True) * (1.0 / D) for v in (u, u * hat)]
                )
            gains = biases = jnp.zeros((8, D), F32)
            for k, (one, two) in zip(ks, means):
                u, hat, inv = read(k)
                write(k, inv * (u * gain - one - hat * two))
                gains, biases = gains + fold_rows(u * hat), biases + fold_rows(u)
            r.vacc[k_gain] += gains
            r.vacc[k_gain + 1] += biases

        repeat(n // TILE // side, step)

    lane_head = lax.div(lax.broadcasted_iota(jnp.int32, (L, W), 1), HS)

    def spread(x):
        zero = jnp.zeros_like(x)
        return jnp.concatenate([jnp.where(lane_head == k, x, zero) for k in range(HN)], axis=0)

    def gather_diag(x):
        out = x[:L]
        for k in range(1, HN):
            out = jnp.where(lane_head == k, x[k * L : (k + 1) * L], out)
        return out

    loaded(ld.w, 3 * D * W * 2)
    loaded(ld.lat, G * L * D * 2)

    def row_of(g, n):
        return lax.broadcasted_iota(jnp.int32, (G, n), 0) == g

    def put_row(ref, g, x):
        ref[...] = jnp.where(row_of(g, x.shape[1]), x, ref[...])

    def to_all(ref, to):
        to_heads(lambda o: send(ref.at[me_h], ref.at[me_h], to, me_i, o))

    def kv_at(k):
        return lambda o: r.wkv_f.at[own_c, at_rows(o * 2 * W + k * W, W, W)]

    def kvq_views():
        return (
            (r.w_key, kv_at(0)), (r.w_value, kv_at(1)),
            (r.w_query, lambda o: r.wq_f.at[own_c, rows_of(o, W)]),
        )

    def att_at(g):
        return lambda o: r.att_f.at[g, :, rows_of(o, W)]

    def ga_at(o):
        return r.ga_f.at[o]

    r.lse[me_h] = r.delta[me_h] = jnp.zeros((G, HN * L), F32)

    def relay(twins, onto, buf, n):
        arrived(twins, (NK - 1) * size(buf.at[rows_of(0, n)]))
        to_twins(
            lambda o: send(
                buf.at[rows_of(o, n)], buf.at[rows_of(o, n)], onto, mate, me_h, times=NK - 1
            )
        )

    def share_wout():
        arrived(link.wout_z, (nh - 1) * QC * D * 2)

        def one(k):
            other = first + lax.rem(share + 1 + k, Q)

            def part(o):
                at = r.wout_f.at[at_rows(o * W + share * QC, QC, QC)]
                send(at, at, link.wout_x, other, me_h, times=Q - 1)

            to_heads(part)

        repeat(Q - 1, one)
        spread_rows(r.w_down, r.down_f, link.dn_x, link.dn_p)

    def image(g):
        slot = lax.rem(g, 2)
        for k, sem in enumerate((ld.m0, ld.m1)):

            @pl.when(slot == k)
            def _():
                loaded(sem, S * D * 2)

        def put_media(k, hat, _):
            r.keys[at_rows(g * T + k * TILE, TILE, TILE), :] = (hat * gain_m + bias_m).astype(BF16)

        def put_latent(k, hat, _):
            y = (hat * gain_l + bias_l).astype(BF16)
            r.keys[at_rows(g * T + S + k * TILE, TILE, TILE), :] = y
            r.lat_n[at_rows(g * L + k * TILE, TILE, TILE), :] = y

        normalize_rows(lambda k: r.media_b[slot, rows_of(k, TILE), :].astype(F32), put_media, S)
        normalize_rows(lambda k: r.lat[g, rows_of(k, TILE), :].astype(F32), put_latent, L)
        for k, sem in enumerate((ld.m0, ld.m1)):

            @pl.when((slot == k) & (g + 2 < G))
            def _():
                load(r.media.at[g + 2], r.media_b.at[k], sem)

        rows, lat_rows = rows_of(g, T), rows_of(g, L)
        kv = dot(r.keys[rows, :], r.wkv_o[...], NN).astype(BF16)
        r.kv[rows, :] = kv
        q = (dot(r.lat_n[lat_rows, :], r.wq_o[...], NN) * (HS**-0.5)).astype(BF16)
        r.q[lat_rows, :] = q
        scores = dot(kv[:, :W], spread(q), NT)
        place = lax.broadcasted_iota(jnp.int32, scores.shape, 0)
        scores = jnp.where((place < r.counts[g]) | (place >= S), scores, -1e30)
        top = jnp.max(scores, axis=0, keepdims=True)
        total = jnp.sum(jnp.exp(scores - top), axis=0, keepdims=True)
        lse = top + jnp.log(total)
        put_row(r.lse.at[me_h], g, lse)
        probs = jnp.exp(scores - lse)
        r.probs[rows, :] = probs
        att = gather_diag(dot(probs.astype(BF16), kv[:, W:], TN)).astype(BF16)
        r.att_f[g, :, own_w] = att
        head_spread(att_at(g), r.att_f.at[g, :, own_w], link.att_t, link.att_m, g, G)

        @pl.when(g >= 2)
        def _():
            head_relay(att_at(g - 2), link.att_t, link.att_y, g - 2, G - 2)

        @pl.when(g == 1)
        def _():
            share_wout()

        @pl.when(g == 2)
        def _():
            for w, view in kvq_views():
                head_spread(view, w.at[own_c], link.kvq_t, link.kvq_m)

        @pl.when(g == G // 2)
        def _():
            head_relay(cot_at, link.cot_t, link.cot_y)

        @pl.when(g == G - 2)
        def _():
            relay(link.up_x, link.up_y, r.up_f, FU)

    repeat(G, image)
    for g in (G - 2, G - 1):
        head_relay(att_at(g), link.att_t, link.att_y, g)
    to_all(r.lse, link.lse)
    arrived(link.kvq_t, (NH - 1) * 3 * RC * W * 2)
    for _, view in kvq_views():
        for o in twins_h:
            send(view(o), view(o), link.kvq_y, me_i, mate_h)
    r.vacc[...] = jnp.zeros_like(r.vacc)

    CR, CG = R // 2, G // 2
    loaded(ld.ff, (W + 2 * FU + G * LR) * D * 2)
    arrived(link.wout_x, (Q - 1) * (nh - 1) * QC * D * 2)

    def ff_forward(b):
        for k in range(CG):
            head_landed(att_at(b * CG + k), link.att_m, link.att_y, b * CG + k)
        at = rows_of(b, CR)
        imgs = pl.ds(b * CG, CG)
        att = r.att_f[imgs, :, :].reshape(CR, nh * W)
        base = r.lat[imgs, :, :].reshape(CR, D).astype(F32)
        r.tmp[:, :D] = dot(att, r.wout_f[...], NN) + base
        for k in range(nh):

            @pl.when(me_h == k)
            def _():
                r.mid_o[imgs] = r.tmp[:, :D].reshape(CG, nh, LR, D)[:, k]

        def put_norm(k, hat, inv):
            row = at_rows(b * CR + k * TILE, TILE, TILE)
            r.hat[row, :] = hat
            r.inv[row, :] = jnp.broadcast_to(inv, (TILE, LANES))
            r.ff_in[row, :] = (hat * gain_f + bias_f).astype(BF16)

        normalize_rows(lambda k: r.tmp[rows_of(k, TILE), :D], put_norm, CR)

        @pl.when(b == 0)
        def _():
            arrived(link.up_p, FU * D * 2)
            arrived(link.up_y, (NK - 1) * FU * D * 2)

        r.tmp[:, :FH] = dot(r.ff_in[at, :], r.up_f[...], NT)

        def gelu(k):
            row = at_rows(b * CR + k * TILE, TILE, TILE)
            value, slope = gelu_parts(r.tmp[rows_of(k, TILE), :FH])
            r.act[row, :] = value.astype(BF16)
            r.slope[row, :] = slope

        repeat(CR // TILE, gelu)

    repeat(2, ff_forward)
    relay(link.dn_x, link.dn_y, r.down_f, FU)
    arrived(link.dn_p, FU * D * 2)
    arrived(link.dn_y, (NK - 1) * FU * D * 2)

    def share_kvq(o, to, times):
        for buf in (r.wkv_f, r.wq_f):
            send(buf.at[own_c], buf.at[own_c], to, o, me_h, times=times)

    def relay_kvq(o):
        for buf in (r.wkv_f, r.wq_f):
            at = buf.at[rows_of(o, RC)]
            send(at, at, link.kv_y, mate, me_h, times=NK - 1)

    loaded(ld.kvq, 3 * RC * W * 2)
    arrived(link.kvq_m, 3 * RC * W * 2)
    arrived(link.kvq_y, (NH - 1) * 3 * RC * W * 2)
    to_twins(lambda o: share_kvq(o, link.kv_x, NK - 1))
    share_kvq(mate, link.kv_p, 1)
    head_landed(cot_at, link.cot_m, link.cot_y)

    def ff_backward(b):
        at, imgs = rows_of(b, CR), pl.ds(b * CG, CG)
        r.tmp[:, :FH] = dot(r.cot_f[imgs, :, :].reshape(CR, D), r.down_f[...], NT)

        def slope(k):
            row = at_rows(b * CR + k * TILE, TILE, TILE)
            r.gh[row, :] = (r.tmp[rows_of(k, TILE), :FH] * r.slope[row, :]).astype(BF16)

        repeat(CR // TILE, slope)
        r.tmp[:, :D] = dot(r.gh[at, :], r.up_f[...], NN)

        def read(k):
            row = at_rows(b * CR + k * TILE, TILE, TILE)
            return r.tmp[rows_of(k, TILE), :D], r.hat[row, :], r.inv[row, :1]

        def write(k, grad):
            g, part = b * CG + k * TILE // L, rows_of(k % (L // TILE), TILE)
            cot = r.cot_f[g, part, :].astype(F32) * (1.0 / nh)
            r.gm_p[g, part, :] = (grad + cot).astype(BF16)

        norm_back_rows(read, write, CR, gain_f, 4)
        ga = dot(r.gm_p[imgs, :, :].reshape(CR, D), r.wout_f[...], NT)
        r.ga_p[imgs, :, :] = ga.astype(BF16).reshape(CG, L, nh * W)
        head_pair(
            lambda o: r.ga_p.at[imgs, :, rows_of(o, W)], lambda p: r.ga1.at[p, imgs], link.ga1, b, 2
        )

    repeat(2, ff_backward)

    def ff_out(b):
        out = dot(r.act[rows_of(b, CR), :], r.down_f[...], NN)
        r.ffo_p[pl.ds(b * CG, CG), :, :] = out.astype(BF16).reshape(CG, L, D)

    def ga_twins(b):
        imgs = pl.ds(b * CG, CG)
        arrived(link.ga1, NH * CG * L * W * 2, b)
        for k, o in zip(halves_h, twins_h):
            at = rows_of(o, W)
            both = r.ga_p[imgs, :, at].astype(F32) + r.ga1[k, imgs].astype(F32)
            r.ga_p[imgs, :, at] = both.astype(BF16)
            send(r.ga_p.at[imgs, :, at], r.ga2.at[half_h, imgs], link.ga2, me_i, o, b)

    def ga_sum(b):
        imgs = pl.ds(b * CG, CG)
        arrived(link.ga2, (NH - 1) * CG * L * W * 2, b)
        total = r.ga_p[imgs, :, own_w].astype(F32) + r.ga1[half_h, imgs].astype(F32)
        for k in halves_h:
            total = total + r.ga2[k, imgs].astype(F32)
        r.ga_f[me_h, imgs] = total.astype(BF16)

    def rows_at(part):
        return lambda o: part.at[:, rows_of(o, LR), :]

    def rows_pair(part, got, to):
        head_pair(rows_at(part), lambda p: got.at[p], to)

    def rows_twins(part, got, got2, to, to2):
        arrived(to, size(got))
        for k, o in zip(halves_h, twins_h):
            at = rows_of(o, LR)

            def add(g):
                both = part[g, at, :].astype(F32) + got[k, g].astype(F32)
                part[g, at, :] = both.astype(BF16)

            repeat(G, add)
            send(part.at[:, at, :], got2.at[half_h], to2, me_i, o)

    def rows_sum(part, got, got2, to2, base, total):
        arrived(to2, size(got2) // NH * (NH - 1))

        def add(g):
            x = base[g] + part[g, own_l, :].astype(F32) + got[half_h, g].astype(F32)
            for k in halves_h:
                x = x + got2[k, g].astype(F32)
            total[g] = x.astype(BF16)

        repeat(G, add)

    for b in range(2):
        ff_out(b)
        ga_twins(b)
    rows_pair(r.ffo_p, r.ffo1, link.ffo1)

    def scatter_pair(buf, got, n, to):
        repeat(
            NK,
            lambda k: send(
                buf.at[rows_of(2 * k + 1 - par, n)], got.at[rows_of(k, n)], to, mate, me_h, times=NK
            ),
        )

    def scatter_twins(buf, got, got2, n, to, to2):
        arrived(to, size(got))

        def step(d, c):
            k = lax.rem(half + d, NK)
            mine = rows_of(2 * k + par, n)
            both = buf[mine, :].astype(F32) + got[rows_of(k, n), :].astype(F32)
            buf[mine, :] = both.astype(BF16)
            send(
                buf.at[mine], got2.at[rows_of(half, n)], to2, 2 * k + par, me_h, times=NK - 1
            )
            return c

        lax.fori_loop(1, NK, step, 0)

    def scatter_sum(buf, got, got2, n, to2, total):
        arrived(to2, size(got2) // NK * (NK - 1))
        total[...] = buf[rows_of(me_i, n), :].astype(F32) + got[rows_of(half, n), :].astype(F32)

        def step(d, c):
            total[...] += got2[rows_of(lax.rem(half + d, NK), n), :].astype(F32)
            return c

        lax.fori_loop(1, NK, step, 0)

    FT = 2 * LANES

    def down_grad(t):
        at = rows_of(t, FT)
        r.wd[at, :] = dot(r.act[:, at], r.cot_f[...].reshape(R, D), TN).astype(BF16)

    repeat(FH // FT, down_grad)
    scatter_pair(r.wd, r.wd1, FU, link.wd1)
    for b in range(2):
        ga_sum(b)
    head_spread(ga_at, r.ga_f.at[me_h], link.ga_t, link.ga_m)

    def up_grad(t):
        at = rows_of(t, FT)
        r.wu[at, :] = dot(r.gh[:, at], r.ff_in[...], TN).astype(BF16)

    repeat(FH // FT, up_grad)
    scatter_pair(r.wu, r.wu1, FU, link.wu1)
    rows_pair(r.gm_p, r.gm1, link.gm1)
    head_relay(ga_at, link.ga_t, link.ga_y)

    def out_grad(t):
        at = rows_of(t, FT)
        left = r.gm_p[:, :, at].reshape(R, FT)
        r.wo[at, :] = dot(left, r.att_f[...].reshape(R, nh * W), TN).astype(BF16)

    repeat(D // FT, out_grad)
    scatter_pair(r.wo, r.wo1, RC, link.wo1)
    scatter_twins(r.wd, r.wd1, r.wd2, FU, link.wd1, link.wd2)
    rows_twins(r.ffo_p, r.ffo1, r.ffo2, link.ffo1, link.ffo2)

    loaded(ld.mo, G * SR * D * 2)

    def keep(hats, invs):
        def put(k, hat, inv):
            hats[k] = hat
            invs[k] = jnp.broadcast_to(inv, (TILE, LANES))

        return put

    NM, NL = SR // TILE, LR // TILE
    normalize_rows(
        lambda k: r.media_o[k // NM, rows_of(k % NM, TILE), :].astype(F32),
        keep(r.hat_m, r.inv_m), G * SR,
    )
    normalize_rows(
        lambda k: r.lat[k // NL, at_rows(me_h * LR + (k % NL) * TILE, TILE, TILE), :].astype(F32),
        keep(r.hat_l, r.inv_l), G * LR,
    )

    def image_back(g):
        rows, lat_rows = rows_of(g, T), rows_of(g, L)
        ga = spread(r.ga_f[me_h, g])
        q = spread(r.q[lat_rows, :])
        key, value = r.kv[rows, :W], r.kv[rows, W:]
        probs = r.probs[rows, :]
        grad_probs = dot(value, ga, NT)
        delta = jnp.sum(probs * grad_probs, axis=0, keepdims=True)
        put_row(r.delta.at[me_h], g, delta)
        grad_scores = (probs * (grad_probs - delta)).astype(BF16)
        r.gkv[g, :, W:] = dot(probs.astype(BF16), ga, NN).astype(BF16)
        r.gkv[g, :, :W] = dot(grad_scores, q, NN).astype(BF16)
        grad_query = gather_diag(dot(grad_scores, key, TN)).astype(BF16)
        r.gq[g] = (grad_query.astype(F32) * (HS**-0.5)).astype(BF16)

    repeat(G, image_back)
    to_all(r.delta, link.delta)
    to_heads(
        lambda o: send(r.gq.at[:, rows_of(o, LR), :], r.gq_r.at[:, :, own_w], link.gq, me_i, o)
    )
    r.gq_r[:, :, own_w] = r.gq[:, own_l, :]
    scatter_twins(r.wu, r.wu1, r.wu2, FU, link.wu1, link.wu2)
    scatter_twins(r.wo, r.wo1, r.wo2, RC, link.wo1, link.wo2)
    rows_twins(r.gm_p, r.gm1, r.gm2, link.gm1, link.gm2)

    def proj_grad(t):
        at = rows_of(t, FT)
        left = r.gkv[...].reshape(G * T, 2 * W)
        r.wa[at, : 2 * W] = dot(r.keys[:, at], left, TN).astype(BF16)
        r.wa[at, 2 * W :] = dot(r.lat_n[:, at], r.gq[...].reshape(R, W), TN).astype(BF16)

    repeat(D // FT, proj_grad)
    scatter_pair(r.wa, r.wa1, RC, link.wa1)
    arrived(link.kv_x, (NK - 1) * 3 * nh * RC * W * 2)
    to_twins(relay_kvq)
    scatter_twins(r.wa, r.wa1, r.wa2, RC, link.wa1, link.wa2)
    arrived(link.kv_p, 3 * nh * RC * W * 2)
    arrived(link.kv_y, (NK - 1) * 3 * nh * RC * W * 2)

    KR = SR + LR

    def take_rows(g):
        at = at_rows(g * KR, SR, LR)
        r.keys_o[at, :] = r.keys[at_rows(g * T + me_h * SR, SR, SR), :]
        at = at_rows(g * KR + SR, LR, LR)
        r.keys_o[at, :] = r.keys[at_rows(g * T + S + me_h * LR, LR, LR), :]

    repeat(G, take_rows)
    arrived(link.lse, (nh - 1) * G * HN * L * 4)
    arrived(link.delta, (nh - 1) * G * HN * L * 4)
    head_landed(ga_at, link.ga_m, link.ga_y)

    def heads_back(o):
        wide = rows_of(o, 2 * W)
        r.kv_h[...] = dot(r.keys_o[...], r.wkv_f[:, wide], NN).astype(BF16)
        q_all = dot(r.lat_n[...], r.wq_f[:, rows_of(o, W)], NN) * (HS**-0.5)
        r.q_h[...] = q_all.astype(BF16)
        for g in range(G):
            rows = pl.ds(g * KR, KR)
            ga = spread(r.ga_f[o, g])
            q = spread(r.q_h[g * L : (g + 1) * L, :])
            key, value = r.kv_h[rows, :W], r.kv_h[rows, W:]
            scores = dot(key, q, NT)
            place = lax.broadcasted_iota(jnp.int32, scores.shape, 0)
            valid = (place + me_h * SR < r.counts[g]) | (place >= SR)
            probs = jnp.exp(jnp.where(valid, scores, -1e30) - r.lse[o, g : g + 1, :])
            grad_probs = dot(value, ga, NT)
            grad_scores = (probs * (grad_probs - r.delta[o, g : g + 1, :])).astype(BF16)
            grad_value = dot(probs.astype(BF16), ga, NN)
            grad_key = dot(grad_scores, q, NN)
            both = jnp.concatenate([grad_key, grad_value], axis=1)
            r.gkv_r[g, :, wide] = both.astype(BF16)

    repeat(nh, heads_back)

    arrived(link.gq, (nh - 1) * G * LR * W * 2)

    def put(k, at=slice(None)):
        name = list(outs)[k]
        a, b = getattr(out, name).at[at], getattr(dst, name).at[at]
        pltpu.make_async_copy(a, b, out_sems.at[k]).start()

    def own_rows(b):
        two = pl.ds(2 * b, 2)
        left = r.gkv_r[two, :, :].reshape(2 * KR, nh * 2 * W)
        r.tmp[: 2 * KR, :D] = dot(left, r.wkv_f[...], NT)
        query = dot(r.gq_r[two, :, :].reshape(2 * LR, nh * W), r.wq_f[...], NT)
        for k in range(2):
            r.tmp[pl.ds(k * KR + SR, LR), :D] += query[k * LR : (k + 1) * LR]

        def read_media(j):
            k = j // NM
            u = r.tmp[at_rows(k * KR + (j % NM) * TILE, TILE, TILE), :D]
            return u, r.hat_m[b * 2 * NM + j], r.inv_m[b * 2 * NM + j][:, :1]

        def write_media(j, grad):
            out.mg[2 * b + j // NM, rows_of(j % NM, TILE), :] = grad.astype(BF16)

        norm_back_rows(read_media, write_media, 2 * SR, gain_m, 0)
        def read_latent(j):
            at = at_rows((j // NL) * KR + SR + (j % NL) * TILE, TILE, TILE)
            return r.tmp[at, :D], r.hat_l[b * 2 * NL + j], r.inv_l[b * 2 * NL + j][:, :1]

        def write_latent(j, grad):
            r.glat[2 * b + j // NL, rows_of(j % NL, TILE), :] = grad

        norm_back_rows(read_latent, write_latent, 2 * LR, gain_l, 2)
        put(1, two)

    repeat(G // 2, own_rows)

    for k in range(6):
        r.vec[k : k + 1, :] = jnp.sum(r.vacc[k], axis=0, keepdims=True)
    r.vec[6:8, :] = jnp.zeros((2, D), F32)

    def block(i):
        return at_rows(lax.div(i * RC, LANES) * LANES, LANES, LANES)

    def vec_step(k):
        o = lax.rem(me_i + 1 + k, ni)
        send(r.vec.at[:, block(o)], r.vec_r.at[me_i], link.vp, o, me_h, times=ni - 1)

    repeat(ni - 1, vec_step)

    scatter_sum(r.wd, r.wd1, r.wd2, FU, link.wd2, out.dn)
    scatter_sum(r.wu, r.wu1, r.wu2, FU, link.wu2, out.up)
    scatter_sum(r.wo, r.wo1, r.wo2, RC, link.wo2, r.tmp.at[:RC, : nh * W])
    for k in range(nh):
        r.wo_s[k] = r.tmp[:RC, k * W : (k + 1) * W].astype(BF16)
    to_heads(lambda o: send(r.wo_s.at[o], r.wo_z.at[me_h], link.wo3, me_i, o))
    scatter_sum(r.wa, r.wa1, r.wa2, RC, link.wa2, out.wa)
    arrived(link.vp, (ni - 1) * 8 * LANES * 4)
    r.vec_t[...] = r.vec[:, block(me_i)]

    def vec_sum(k):
        r.vec_t[...] += r.vec_r[lax.rem(me_i + 1 + k, ni)]

    repeat(ni - 1, vec_sum)
    to_heads(lambda o: send(r.vec_t, r.vec_z.at[me_h], link.vz, me_i, o))
    rows_sum(r.ffo_p, r.ffo1, r.ffo2, link.ffo2, r.mid_o, out.lat)
    arrived(link.wo3, (nh - 1) * RC * W * 2)
    total = r.tmp[:RC, own_w]
    for o in heads:
        total = total + r.wo_z[o].astype(F32)
    out.wo[...] = total
    arrived(link.vz, (nh - 1) * 8 * LANES * 4)
    total = r.vec_t[...]
    for o in heads:
        total = total + r.vec_z[o]
    out.vec[...] = total
    for k in range(len(outs)):
        if k not in (1, 2):
            put(k)
    rows_sum(r.gm_p, r.gm1, r.gm2, link.gm2, r.glat, out.lg)
    put(2)

    for to in vars(link).values():
        if to.bytes:
            await_bytes(send_sems.at[to.send], to.bytes)
    for k, name in enumerate(outs):
        pltpu.make_async_copy(getattr(out, name), getattr(dst, name), out_sems.at[k]).wait()


def finish(z, *refs):
    n = len(outputs(z)) - 1
    src, dst, buf, turned, in_sems, out_sems = (
        refs[:n], refs[n : n + 9], refs[n + 9 : 2 * n + 9], refs[-3], refs[-2], refs[-1]
    )
    W = z.W
    loads = [pltpu.make_async_copy(src[k], buf[k], in_sems.at[k]) for k in range(n)]
    for copy in loads:
        copy.start()
    stores = []

    def store(ref, k):
        stores.append(pltpu.make_async_copy(ref, dst[k], out_sems.at[k]))
        stores[-1].start()

    lat, mg, lg, wa, wo, up, dn = range(7)
    loads[mg].wait()
    store(buf[mg], 1)
    loads[up].wait()
    store(buf[up], 7)
    loads[dn].wait()
    store(buf[dn], 8)
    loads[lat].wait()
    store(buf[lat], 0)
    loads[lg].wait()
    store(buf[lg], 2)
    loads[wa].wait()
    store(buf[wa].at[:, pl.ds(2 * W, W)], 3)
    store(buf[wa].at[:, pl.ds(0, W)], 4)
    store(buf[wa].at[:, pl.ds(W, W)], 5)
    loads[wo].wait()
    turned[...] = buf[wo][...].T
    store(turned, 6)
    for copy in stores:
        copy.wait()


def body(ni, nh, media, latents, counts, media_gain, media_bias, latent_gain, latent_bias, w_query,
         w_key, w_value, w_out, ff_gain, ff_bias, w_up, w_down, cotangent):
    z = sizes(ni, nh, media, latents, w_query, w_up)
    D, W, RC = z.D, z.W, z.RC
    vm = pl.BlockSpec(memory_space=pltpu.VMEM)
    hbm = pl.BlockSpec(memory_space=pl.ANY)
    dma = pltpu.SemaphoreType.DMA
    outs = list(outputs(z).values())
    rows = [
        v.reshape(1, D)
        for v in (media_gain, media_bias, latent_gain, latent_bias, ff_gain, ff_bias)
    ]
    counted = links(z).values()
    res = pl.pallas_call(
        functools.partial(kernel, z),
        out_shape=[jax.ShapeDtypeStruct(s, d) for s, d in outs],
        in_specs=[pl.BlockSpec(memory_space=pltpu.SMEM)] + [vm] * 6 + [hbm] * 9,
        out_specs=[hbm] * len(outs),
        scratch_shapes=[pltpu.VMEM(s, d) for s, d in (*scratch(z).values(), *outs)]
        + [
            dma((sum(a for a, _ in counted),)),
            dma((sum(b for _, b in counted),)),
            dma((len(LOADS),)),
            dma((len(outs),)),
        ],
        compiler_params=pltpu.CompilerParams(
            collective_id=0, has_side_effects=True, vmem_limit_bytes=67043328
        ),
    )(counts, *rows, media, latents, w_query, w_key, w_value, w_out, w_up, w_down, cotangent)
    last = outs[:3] + [((RC, W), F32)] * 3 + [((W, RC), F32)] + outs[5:7]
    res2 = pl.pallas_call(
        functools.partial(finish, z),
        out_shape=[jax.ShapeDtypeStruct(s, d) for s, d in last],
        in_specs=[hbm] * 7,
        out_specs=[hbm] * 9,
        scratch_shapes=[pltpu.VMEM(s, d) for s, d in outs[:7]]
        + [pltpu.VMEM((W, RC), F32), dma((7,)), dma((9,))],
    )(*res[:7])
    lat_out, media_grad, lat_grad, wq, wk, wv, wo, up, down = res2
    share = D // (ni * nh)
    place = lax.axis_index("img") * nh + lax.axis_index("head")
    vec = lax.dynamic_slice(res[7], (0, lax.rem(place * share, LANES)), (8, share))
    return (
        lat_out, media_grad, lat_grad, vec[0], vec[1], vec[2], vec[3], wq, wk, wv, wo, vec[4],
        vec[5], up, down,
    )


def solution(mesh):
    ni, nh = mesh.shape["img"], mesh.shape["head"]
    both = P(("img", "head"))
    rows = P("img", "head", None)
    return jax.shard_map(
        functools.partial(body, ni, nh),
        mesh=mesh,
        in_specs=(
            P("img", None, None), P("img", None, None), P("img"), P(), P(), P(), P(),
            P(None, "head"), P(None, "head"), P(None, "head"), P("head", None), P(), P(),
            P(("img", "head"), None), P(("img", "head"), None), rows,
        ),
        out_specs=(
            rows, rows, rows, both, both, both, both, P("img", "head"), P("img", "head"),
            P("img", "head"), P("head", "img"), both, both, P(("img", "head"), None),
            P(("img", "head"), None),
        ),
        check_vma=False,
    )
```

```python
import functools
import math
from types import SimpleNamespace

import jax
import jax.numpy as jnp
from jax import lax
from jax.experimental import pallas as pl
from jax.experimental.pallas import tpu as pltpu
from jax.sharding import PartitionSpec as P

HS = 64
EPSILON = 1e-05
LANES = 128
TILE = 16
SIDE = 16
LAG = 4
BF16 = jnp.bfloat16
F32 = jnp.float32
MESH = pl.DeviceIdType.MESH
NN = ((1,), (0,))
NT = ((1,), (1,))
TN = ((0,), (0,))


def dot(a, b, dims):
    return lax.dot_general(a, b, (dims, ((), ())), preferred_element_type=F32)


def fold_rows(x):
    return jnp.sum(x.reshape(x.shape[0] // 8, 8, x.shape[1]), axis=0)


def gelu_parts(hidden):
    normal_cdf = 0.5 * (1.0 + lax.erf(hidden * (1.0 / math.sqrt(2.0))))
    density = jnp.exp(-0.5 * hidden * hidden) * (1.0 / math.sqrt(2.0 * math.pi))
    return (hidden * normal_cdf, normal_cdf + hidden * density)


def sizes(ni, nh, media, latents, w_query, w_up):
    G, S, D = media.shape
    L, W, FU = latents.shape[1], w_query.shape[1], w_up.shape[0]
    Q = min(ni, W // TILE)
    return SimpleNamespace(
        ni=ni, nh=nh, G=G, S=S, D=D, L=L, W=W, FU=FU, T=S + L, SR=S // nh, LR=L // nh, R=G * L,
        FH=ni * FU, RC=D // ni, NK=ni // 2, NH=nh // 2, HN=W // HS, Q=Q, QC=W // Q,
    )


def outputs(z):
    return dict(
        lat=((z.G, z.LR, z.D), BF16),
        mg=((z.G, z.SR, z.D), BF16),
        lg=((z.G, z.LR, z.D), BF16),
        wa=((z.RC, 3 * z.W), F32),
        wo=((z.RC, z.W), F32),
        up=((z.FU, z.D), F32),
        dn=((z.FU, z.D), F32),
        vec=((8, LANES), F32),
    )


def scratch(z):
    G, D, L, W, T, SR, LR, R, FH, RC, NK, NH, FU, nh = (
        z.G, z.D, z.L, z.W, z.T, z.SR, z.LR, z.R, z.FH, z.RC, z.NK, z.NH, z.FU, z.nh
    )
    return dict(
        media_b=((2, z.S, D), BF16),
        media_o=((G, SR, D), BF16),
        lat=((G, L, D), BF16),
        keys=((G * T, D), BF16),
        lat_n=((R, D), BF16),
        wkv_o=((D, 2 * W), BF16),
        wq_o=((D, W), BF16),
        wkv_f=((D, nh * 2 * W), BF16),
        wq_f=((D, nh * W), BF16),
        wout_f=((nh * W, D), BF16),
        up_f=((FH, D), BF16),
        down_f=((FH, D), BF16),
        cot_f=((G, L, D), BF16),
        kv=((G * T, 2 * W), BF16),
        q=((R, W), BF16),
        probs=((G * T, z.HN * L), F32),
        att_f=((G, L, nh * W), BF16),
        mid_o=((G, LR, D), F32),
        hat=((R, D), F32),
        inv=((R, LANES), F32),
        ff_in=((R, D), BF16),
        act=((R, FH), BF16),
        slope=((R, FH), F32),
        gh=((R, FH), BF16),
        tmp=((R // 2, max(D, FH)), F32),
        ffo_p=((G, L, D), BF16),
        gm_p=((G, L, D), BF16),
        ffo1=((NH, G, LR, D), BF16),
        ffo2=((NH, G, LR, D), BF16),
        gm1=((NH, G, LR, D), BF16),
        gm2=((NH, G, LR, D), BF16),
        gm_o=((G, LR, D), F32),
        ga_f=((G, L, nh * W), BF16),
        lse=((nh, G, z.HN * L), F32),
        delta=((nh, G, z.HN * L), F32),
        keys_o=((G * (SR + LR), D), BF16),
        kv_h=((nh, G * (SR + LR), 2 * W), BF16),
        q_h=((nh, R, W), BF16),
        gkv=((G, T, 2 * W), BF16),
        gq=((G, L, W), BF16),
        gkv_r=((G, SR + LR, nh * 2 * W), BF16),
        gq_r=((G, LR, nh * W), BF16),
        wu=((FH, D), BF16),
        wd=((FH, D), BF16),
        wo=((D, nh * W), BF16),
        wa=((D, 3 * W), BF16),
        wu1=((NK * FU, D), BF16),
        wd1=((NK * FU, D), BF16),
        wo1=((NK * RC, nh * W), BF16),
        wa1=((NK * RC, 3 * W), BF16),
        wu2=((NK * FU, D), BF16),
        wd2=((NK * FU, D), BF16),
        wo2=((NK * RC, nh * W), BF16),
        wa2=((NK * RC, 3 * W), BF16),
        wo_s=((nh, RC, W), BF16),
        wo_z=((nh, RC, W), BF16),
        hat_m=((G * SR // TILE, TILE, D), F32),
        inv_m=((G * SR // TILE, TILE, LANES), F32),
        hat_l=((G * LR // TILE, TILE, D), F32),
        inv_l=((G * LR // TILE, TILE, LANES), F32),
        vacc=((6, 8, D), F32),
        vec=((8, D), F32),
        vec_r=((z.ni, 8, LANES), F32),
        vec_t=((8, LANES), F32),
        vec_z=((nh, 8, LANES), F32),
    )


def links(z):
    G = z.G
    one = (1, 1)
    return dict(
        wout_z=one, wout_x=one, wout_p=one, wout_y=one, up_p=one, up_x=one, up_y=one, dn_p=one, dn_x=one, dn_y=one,
        kvq_t=one, kvq_m=one, kvq_y=one, kv_p=one, kv_x=one, kv_y=one,
        cot_t=(2, 1), cot_m=(2, 1), cot_y=(2, 1), att_t=(G, 1), att_m=(G, 1), att_y=(G, 1), lse=one,
        delta=one, ga_t=(2, 1), ga_m=(2, 1), ga_y=(2, 1), gq=one,
        ffo1=one, ffo2=one, gm1=(2, 1), gm2=(2, 1),
        wu1=one, wu2=one, wd1=one, wd2=one, wo1=one, wo2=one, wo3=one, wa1=one, wa2=one,
        vp=one, vz=one,
    )


LOADS = dict(m0=0, m1=1, w=2, lat=3, ff=4, kvq=5, mo=6)
INS = tuple(
    dict(
        counts=0, g_m=0, b_m=0, g_l=0, b_l=0, g_f=0, b_f=0, media=0, latents=0, w_query=0, w_key=0,
        w_value=0, w_out=0, w_up=0, w_down=0, cot=0,
    )
)


def kernel(z, *refs):
    outs, vmem = outputs(z), scratch(z)
    n_in, n_out = len(INS), len(outs)
    r = SimpleNamespace(
        **dict(zip(INS, refs[:n_in])),
        **dict(zip(vmem, refs[n_in + n_out :])),
    )
    dst = SimpleNamespace(**dict(zip(outs, refs[n_in : n_in + n_out])))
    out = SimpleNamespace(**dict(zip(outs, refs[n_in + n_out + len(vmem) :])))
    recv_sems, send_sems, load_sems, out_sems = refs[-4:]
    G, S, D, L, W, FU, T, SR, LR, R, FH, RC, NK, NH, HN = (
        z.G, z.S, z.D, z.L, z.W, z.FU, z.T, z.SR, z.LR, z.R, z.FH, z.RC, z.NK, z.NH, z.HN
    )
    ni, nh = z.ni, z.nh
    me_i, me_h = lax.axis_index("img"), lax.axis_index("head")
    par, half = lax.rem(me_i, 2), lax.div(me_i, 2)
    mate = me_i + 1 - 2 * par
    par_h, half_h = lax.rem(me_h, 2), lax.div(me_h, 2)
    mate_h = me_h + 1 - 2 * par_h
    halves_h = [lax.rem(half_h + k, NH) for k in range(1, NH)]
    twins_h = [2 * k + par_h for k in halves_h]

    link, n_recv, n_send = {}, 0, 0
    for name, (a, b) in links(z).items():
        link[name] = SimpleNamespace(recv=n_recv, send=n_send, bytes=0)
        n_recv, n_send = n_recv + a, n_send + b
    link = SimpleNamespace(**link)
    ld = SimpleNamespace(**LOADS)

    def size(ref):
        return math.prod(ref.shape) * jnp.dtype(ref.dtype).itemsize

    def await_bytes(sem, nbytes):
        lanes = D
        while nbytes % (2 * lanes * TILE):
            lanes //= 2
        assert lanes >= LANES and nbytes // (2 * lanes) <= G * T
        view = r.keys.at[pl.ds(0, nbytes // (2 * lanes)), pl.ds(0, lanes)]
        pltpu.make_async_copy(view, view, sem).wait()

    def load(src, dst, k):
        pltpu.make_async_copy(src, dst, load_sems.at[k]).start()

    def loaded(k, nbytes):
        await_bytes(load_sems.at[k], nbytes)

    def arrived(to, nbytes, k=0):
        await_bytes(recv_sems.at[to.recv + k], nbytes)

    def push(src, dst, to, img, head, k=0, s=0):
        pltpu.make_async_remote_copy(
            src_ref=src,
            dst_ref=dst,
            send_sem=send_sems.at[to.send + s],
            recv_sem=recv_sems.at[to.recv + k],
            device_id=(img, head),
            device_id_type=MESH,
        ).start()

    def send(src, dst, to, img, head, k=0, times=1):
        push(src, dst, to, img, head, k)
        to.bytes += size(src) * times

    def rows_of(i, n):
        return pl.ds(pl.multiple_of(i * n, n), n)

    def at_rows(start, n, unit):
        return pl.ds(pl.multiple_of(start, unit), n)

    heads = [lax.rem(me_h + d, nh) for d in range(1, nh)]

    def to_heads(f):
        for other in heads:
            f(other)

    def to_twins(f):
        def step(k, c):
            f(lax.rem(half + k, NK) * 2 + par)
            return c

        lax.fori_loop(1, NK, step, 0)

    def head_spread(view, src, twins, pair, k=0, times=1):
        for o in twins_h:
            send(src, view(me_h), twins, me_i, o, k, times)
        send(src, view(me_h), pair, me_i, mate_h, k, times)

    def head_relay(view, twins, onto, k=0, times=1):
        arrived(twins, (NH - 1) * size(view(0)), k)
        for o in twins_h:
            send(view(o), view(o), onto, me_i, mate_h, k, times)

    def head_landed(view, pair, onto, k=0):
        arrived(pair, size(view(0)), k)
        arrived(onto, (NH - 1) * size(view(0)), k)

    def head_pair(view, got, to, k=0, times=1):
        for p in range(NH):
            send(view(2 * p + 1 - par_h), got(p), to, me_i, mate_h, k, times)

    def repeat(n, f):
        if n == 1:
            return f(0)

        def step(k, c):
            f(k)
            return c

        lax.fori_loop(0, n, step, 0)

    load(r.media.at[0], r.media_b.at[0], ld.m0)
    load(r.w_key, r.wkv_o.at[:, pl.ds(0, W)], ld.w)
    load(r.w_value, r.wkv_o.at[:, pl.ds(W, W)], ld.w)
    load(r.w_query, r.wq_o, ld.w)
    load(r.latents, r.lat, ld.lat)
    load(r.media.at[1], r.media_b.at[1], ld.m1)
    barrier = pltpu.get_barrier_semaphore()
    to_heads(
        lambda o: pl.semaphore_signal(
            barrier, inc=1, device_id=(me_i, o), device_id_type=MESH
        )
    )
    repeat(
        ni - 1,
        lambda k: pl.semaphore_signal(
            barrier, inc=1, device_id=(lax.rem(me_i + 1 + k, ni), me_h), device_id_type=MESH
        ),
    )
    pl.semaphore_wait(barrier, nh - 1 + ni - 1)

    Q, QC = z.Q, z.QC
    share = lax.rem(me_i, Q)
    first = me_i - share
    wo_part = at_rows(me_h * W + share * QC, QC, QC)
    to_heads(
        lambda o: send(r.w_out.at[rows_of(share, QC)], r.wout_f.at[wo_part], link.wout_z, me_i, o)
    )
    own_f = rows_of(me_i, FU)
    own_l = rows_of(me_h, LR)

    CR, CG = R // 2, G // 2

    def cot_at(b):
        return lambda o: r.cot_f.at[pl.ds(b * CG, CG), rows_of(o, LR), :]

    def cot_spread(b):
        head_spread(cot_at(b), r.cot.at[pl.ds(b * CG, CG)], link.cot_t, link.cot_m, b)

    cot_spread(0)

    def spread_rows(src, buf, twins, pair):
        to_twins(lambda o: send(src, buf.at[own_f], twins, o, me_h, times=NK - 1))
        send(src, buf.at[own_f], pair, mate, me_h)

    spread_rows(r.w_up, r.up_f, link.up_x, link.up_p)
    load(r.w_out, r.wout_f.at[rows_of(me_h, W)], ld.ff)
    load(r.w_up, r.up_f.at[own_f], ld.ff)
    load(r.w_down, r.down_f.at[own_f], ld.ff)
    load(r.cot, r.cot_f.at[:, own_l, :], ld.ff)
    own_kv = [at_rows(me_h * 2 * W + k * W, W, W) for k in range(2)]
    own_w = rows_of(me_h, W)
    own_c = rows_of(me_i, RC)
    load(r.w_key.at[own_c], r.wkv_f.at[own_c, own_kv[0]], ld.kvq)
    load(r.w_value.at[own_c], r.wkv_f.at[own_c, own_kv[1]], ld.kvq)
    load(r.w_query.at[own_c], r.wq_f.at[own_c, own_w], ld.kvq)
    load(r.media.at[:, rows_of(me_h, SR), :], r.media_o, ld.mo)

    gain_m, bias_m = r.g_m[...], r.b_m[...]
    gain_l, bias_l = r.g_l[...], r.b_l[...]
    gain_f, bias_f = r.g_f[...], r.b_f[...]

    def normalize_rows(read, write, n):
        side = min(n // TILE, SIDE)

        def step(b):
            ks = [b * side + j for j in range(side)]
            mean = [jnp.sum(read(k), axis=-1, keepdims=True) * (1.0 / D) for k in ks]
            var = [
                jnp.sum(jnp.square(read(k) - m), axis=-1, keepdims=True) * (1.0 / D)
                for k, m in zip(ks, mean)
            ]
            inv = [lax.rsqrt(v + EPSILON) for v in var]
            for k, m, i in zip(ks, mean, inv):
                write(k, (read(k) - m) * i, i)

        repeat(n // TILE // side, step)

    def norm_back_rows(read, write, n, gain, k_gain):
        side = min(n // TILE, SIDE)

        def step(b):
            ks = [b * side + j for j in range(side)]
            means = []
            for k in ks:
                u, hat, _ = read(k)
                u = u * gain
                means.append(
                    [jnp.sum(v, axis=-1, keepdims=True) * (1.0 / D) for v in (u, u * hat)]
                )
            gains = biases = jnp.zeros((8, D), F32)
            for k, (one, two) in zip(ks, means):
                u, hat, inv = read(k)
                write(k, inv * (u * gain - one - hat * two))
                gains, biases = gains + fold_rows(u * hat), biases + fold_rows(u)
            r.vacc[k_gain] += gains
            r.vacc[k_gain + 1] += biases

        repeat(n // TILE // side, step)

    lane_head = lax.div(lax.broadcasted_iota(jnp.int32, (L, W), 1), HS)

    def spread(x):
        zero = jnp.zeros_like(x)
        return jnp.concatenate([jnp.where(lane_head == k, x, zero) for k in range(HN)], axis=0)

    def gather_diag(x):
        out = x[:L]
        for k in range(1, HN):
            out = jnp.where(lane_head == k, x[k * L : (k + 1) * L], out)
        return out

    loaded(ld.w, 3 * D * W * 2)
    loaded(ld.lat, G * L * D * 2)

    def row_of(g, n):
        return lax.broadcasted_iota(jnp.int32, (G, n), 0) == g

    def put_row(ref, g, x):
        ref[...] = jnp.where(row_of(g, x.shape[1]), x, ref[...])

    def to_all(ref, to):
        to_heads(lambda o: send(ref.at[me_h], ref.at[me_h], to, me_i, o))

    def kv_at(k):
        return lambda o: r.wkv_f.at[own_c, at_rows(o * 2 * W + k * W, W, W)]

    def kvq_views():
        return (
            (r.w_key, kv_at(0)), (r.w_value, kv_at(1)),
            (r.w_query, lambda o: r.wq_f.at[own_c, rows_of(o, W)]),
        )

    def att_at(g):
        return lambda o: r.att_f.at[g, :, rows_of(o, W)]

    def ga_at(b):
        return lambda o: r.ga_f.at[pl.ds(b * CG, CG), rows_of(o, LR), :]

    r.lse[me_h] = r.delta[me_h] = jnp.zeros((G, HN * L), F32)

    def relay(twins, onto, buf, n):
        arrived(twins, (NK - 1) * size(buf.at[rows_of(0, n)]))
        to_twins(
            lambda o: send(
                buf.at[rows_of(o, n)], buf.at[rows_of(o, n)], onto, mate, me_h, times=NK - 1
            )
        )

    def wout_send(o, s, to, img):
        at = r.wout_f.at[at_rows(o * W + s * QC, QC, QC)]
        send(at, at, to, img, me_h)

    def relay_wout():
        arrived(link.wout_x, (Q // 2 - 1) * (nh - 1) * QC * D * 2)
        for d in range(1, Q // 2):
            s = lax.rem(lax.div(share, 2) + d, Q // 2) * 2 + par
            to_heads(lambda o: wout_send(o, s, link.wout_y, mate))

    def share_wout():
        arrived(link.wout_z, (nh - 1) * QC * D * 2)

        for d in range(1, Q // 2):
            other = lax.rem(lax.div(share, 2) + d, Q // 2) * 2 + par
            to_heads(lambda o: wout_send(o, share, link.wout_x, first + other))
        to_heads(lambda o: wout_send(o, share, link.wout_p, mate))
        spread_rows(r.w_down, r.down_f, link.dn_x, link.dn_p)

    def image(g):
        slot = lax.rem(g, 2)
        for k, sem in enumerate((ld.m0, ld.m1)):

            @pl.when(slot == k)
            def _():
                loaded(sem, S * D * 2)

        def put_media(k, hat, _):
            r.keys[at_rows(g * T + k * TILE, TILE, TILE), :] = (hat * gain_m + bias_m).astype(BF16)

        def put_latent(k, hat, _):
            y = (hat * gain_l + bias_l).astype(BF16)
            r.keys[at_rows(g * T + S + k * TILE, TILE, TILE), :] = y
            r.lat_n[at_rows(g * L + k * TILE, TILE, TILE), :] = y

        normalize_rows(lambda k: r.media_b[slot, rows_of(k, TILE), :].astype(F32), put_media, S)
        normalize_rows(lambda k: r.lat[g, rows_of(k, TILE), :].astype(F32), put_latent, L)
        for k, sem in enumerate((ld.m0, ld.m1)):

            @pl.when((slot == k) & (g + 2 < G))
            def _():
                load(r.media.at[g + 2], r.media_b.at[k], sem)

        rows, lat_rows = rows_of(g, T), rows_of(g, L)
        kv = dot(r.keys[rows, :], r.wkv_o[...], NN).astype(BF16)
        r.kv[rows, :] = kv
        q = (dot(r.lat_n[lat_rows, :], r.wq_o[...], NN) * (HS**-0.5)).astype(BF16)
        r.q[lat_rows, :] = q
        scores = dot(kv[:, :W], spread(q), NT)
        place = lax.broadcasted_iota(jnp.int32, scores.shape, 0)
        scores = jnp.where((place < r.counts[g]) | (place >= S), scores, -1e30)
        top = jnp.max(scores, axis=0, keepdims=True)
        total = jnp.sum(jnp.exp(scores - top), axis=0, keepdims=True)
        lse = top + jnp.log(total)
        put_row(r.lse.at[me_h], g, lse)
        probs = jnp.exp(scores - lse)
        r.probs[rows, :] = probs
        att = gather_diag(dot(probs.astype(BF16), kv[:, W:], TN)).astype(BF16)
        r.att_f[g, :, own_w] = att
        head_spread(att_at(g), r.att_f.at[g, :, own_w], link.att_t, link.att_m, g, G)

        @pl.when(g >= LAG)
        def _():
            head_relay(att_at(g - LAG), link.att_t, link.att_y, g - LAG, G - LAG)

        @pl.when(g == 2)
        def _():
            share_wout()

        @pl.when(g == G - 1)
        def _():
            relay_wout()

        @pl.when(g == G // 2 + 1)
        def _():
            for w, view in kvq_views():
                head_spread(view, w.at[own_c], link.kvq_t, link.kvq_m)

        @pl.when(g == G // 2)
        def _():
            head_relay(cot_at(0), link.cot_t, link.cot_y, 0)

        @pl.when(g == G - 2)
        def _():
            relay(link.up_x, link.up_y, r.up_f, FU)

    repeat(G, image)
    for g in range(G - LAG, G):
        head_relay(att_at(g), link.att_t, link.att_y, g)
    cot_spread(1)
    to_all(r.lse, link.lse)
    arrived(link.kvq_t, (NH - 1) * 3 * RC * W * 2)
    for _, view in kvq_views():
        for o in twins_h:
            send(view(o), view(o), link.kvq_y, me_i, mate_h)
    r.vacc[...] = jnp.zeros_like(r.vacc)

    loaded(ld.ff, (W + 2 * FU + G * LR) * D * 2)
    arrived(link.wout_p, (nh - 1) * QC * D * 2)
    arrived(link.wout_y, (Q // 2 - 1) * (nh - 1) * QC * D * 2)

    def ff_forward(b):
        for k in range(CG):
            head_landed(att_at(b * CG + k), link.att_m, link.att_y, b * CG + k)
        at = rows_of(b, CR)
        imgs = pl.ds(b * CG, CG)
        att = r.att_f[imgs, :, :].reshape(CR, nh * W)
        base = r.lat[imgs, :, :].reshape(CR, D).astype(F32)
        r.tmp[:, :D] = dot(att, r.wout_f[...], NN) + base
        for k in range(nh):

            @pl.when(me_h == k)
            def _():
                r.mid_o[imgs] = r.tmp[:, :D].reshape(CG, nh, LR, D)[:, k]

        def put_norm(k, hat, inv):
            row = at_rows(b * CR + k * TILE, TILE, TILE)
            r.hat[row, :] = hat
            r.inv[row, :] = jnp.broadcast_to(inv, (TILE, LANES))
            r.ff_in[row, :] = (hat * gain_f + bias_f).astype(BF16)

        normalize_rows(lambda k: r.tmp[rows_of(k, TILE), :D], put_norm, CR)

        @pl.when(b == 0)
        def _():
            arrived(link.up_p, FU * D * 2)
            arrived(link.up_y, (NK - 1) * FU * D * 2)

        r.tmp[:, :FH] = dot(r.ff_in[at, :], r.up_f[...], NT)

        def gelu(k):
            row = at_rows(b * CR + k * TILE, TILE, TILE)
            value, slope = gelu_parts(r.tmp[rows_of(k, TILE), :FH])
            r.act[row, :] = value.astype(BF16)
            r.slope[row, :] = slope

        repeat(CR // TILE, gelu)

    repeat(2, ff_forward)
    head_relay(cot_at(1), link.cot_t, link.cot_y, 1)
    relay(link.dn_x, link.dn_y, r.down_f, FU)
    arrived(link.dn_p, FU * D * 2)
    arrived(link.dn_y, (NK - 1) * FU * D * 2)

    def share_kvq(o, to, times):
        for buf in (r.wkv_f, r.wq_f):
            send(buf.at[own_c], buf.at[own_c], to, o, me_h, times=times)

    def relay_kvq(o):
        for buf in (r.wkv_f, r.wq_f):
            at = buf.at[rows_of(o, RC)]
            send(at, at, link.kv_y, mate, me_h, times=NK - 1)

    loaded(ld.kvq, 3 * RC * W * 2)
    arrived(link.kvq_m, 3 * RC * W * 2)
    arrived(link.kvq_y, (NH - 1) * 3 * RC * W * 2)
    to_twins(lambda o: share_kvq(o, link.kv_x, NK - 1))
    share_kvq(mate, link.kv_p, 1)

    def rows_pair(part, got, to, imgs, k=0, times=1):
        head_pair(
            lambda o: part.at[imgs, rows_of(o, LR), :], lambda p: got.at[p, imgs], to, k, times
        )

    def rows_twins(part, got, got2, to, to2, imgs, n, k=0):
        arrived(to, NH * n * LR * D * 2, k)
        for p, o in zip(halves_h, twins_h):
            at = rows_of(o, LR)
            both = part[imgs, at, :].astype(F32) + got[p, imgs].astype(F32)
            part[imgs, at, :] = both.astype(BF16)
            send(part.at[imgs, at, :], got2.at[half_h, imgs], to2, me_i, o, k)

    def rows_total(part, got, got2, to2, imgs, n, k=0):
        arrived(to2, (NH - 1) * n * LR * D * 2, k)
        x = part[imgs, own_l, :].astype(F32) + got[half_h, imgs].astype(F32)
        for p in halves_h:
            x = x + got2[p, imgs].astype(F32)
        return x

    def ff_backward(b):
        at, imgs = rows_of(b, CR), pl.ds(b * CG, CG)
        head_landed(cot_at(b), link.cot_m, link.cot_y, b)
        r.tmp[:, :FH] = dot(r.cot_f[imgs, :, :].reshape(CR, D), r.down_f[...], NT)

        def slope(k):
            row = at_rows(b * CR + k * TILE, TILE, TILE)
            r.gh[row, :] = (r.tmp[rows_of(k, TILE), :FH] * r.slope[row, :]).astype(BF16)

        repeat(CR // TILE, slope)
        r.tmp[:, :D] = dot(r.gh[at, :], r.up_f[...], NN)

        def read(k):
            row = at_rows(b * CR + k * TILE, TILE, TILE)
            return r.tmp[rows_of(k, TILE), :D], r.hat[row, :], r.inv[row, :1]

        def write(k, grad):
            g, part = b * CG + k * TILE // L, rows_of(k % (L // TILE), TILE)
            cot = r.cot_f[g, part, :].astype(F32) * (1.0 / nh)
            r.gm_p[g, part, :] = (grad + cot).astype(BF16)

        norm_back_rows(read, write, CR, gain_f, 4)
        rows_pair(r.gm_p, r.gm1, link.gm1, imgs, b, 2)

    repeat(2, ff_backward)

    def ff_out(b):
        out = dot(r.act[rows_of(b, CR), :], r.down_f[...], NN)
        r.ffo_p[pl.ds(b * CG, CG), :, :] = out.astype(BF16).reshape(CG, L, D)

    def gm_twins(b):
        imgs = pl.ds(b * CG, CG)
        rows_twins(r.gm_p, r.gm1, r.gm2, link.gm1, link.gm2, imgs, CG, b)

    def gm_total(b):
        imgs = pl.ds(b * CG, CG)
        gm = rows_total(r.gm_p, r.gm1, r.gm2, link.gm2, imgs, CG, b)
        r.gm_o[imgs] = gm
        ga = dot(gm.astype(BF16).reshape(CG * LR, D), r.wout_f[...], NT).astype(BF16)
        r.ga_f[imgs, own_l, :] = ga.reshape(CG, LR, nh * W)
        head_spread(ga_at(b), r.ga_f.at[imgs, own_l, :], link.ga_t, link.ga_m, b)

    every = pl.ds(0, G)
    for b in range(2):
        ff_out(b)

    def scatter_pair(buf, got, n, to):
        repeat(
            NK,
            lambda k: send(
                buf.at[rows_of(2 * k + 1 - par, n)], got.at[rows_of(k, n)], to, mate, me_h, times=NK
            ),
        )

    def scatter_twins(buf, got, got2, n, to, to2):
        arrived(to, size(got))

        def step(d, c):
            k = lax.rem(half + d, NK)
            mine = rows_of(2 * k + par, n)
            both = buf[mine, :].astype(F32) + got[rows_of(k, n), :].astype(F32)
            buf[mine, :] = both.astype(BF16)
            send(
                buf.at[mine], got2.at[rows_of(half, n)], to2, 2 * k + par, me_h, times=NK - 1
            )
            return c

        lax.fori_loop(1, NK, step, 0)

    def scatter_sum(buf, got, got2, n, to2, total):
        arrived(to2, size(got2) // NK * (NK - 1))
        total[...] = buf[rows_of(me_i, n), :].astype(F32) + got[rows_of(half, n), :].astype(F32)

        def step(d, c):
            total[...] += got2[rows_of(lax.rem(half + d, NK), n), :].astype(F32)
            return c

        lax.fori_loop(1, NK, step, 0)

    FT = 2 * LANES

    def out_grad(t):
        at = rows_of(t, FT)
        left = r.gm_p[:, :, at].reshape(R, FT)
        r.wo[at, :] = dot(left, r.att_f[...].reshape(R, nh * W), TN).astype(BF16)

    repeat(D // FT, out_grad)
    scatter_pair(r.wo, r.wo1, RC, link.wo1)

    def down_grad(t):
        at = rows_of(t, FT)
        r.wd[at, :] = dot(r.act[:, at], r.cot_f[...].reshape(R, D), TN).astype(BF16)

    repeat(FH // FT, down_grad)
    scatter_pair(r.wd, r.wd1, FU, link.wd1)
    gm_twins(0)

    def up_grad(t):
        at = rows_of(t, FT)
        r.wu[at, :] = dot(r.gh[:, at], r.ff_in[...], TN).astype(BF16)

    repeat(FH // FT, up_grad)
    scatter_pair(r.wu, r.wu1, FU, link.wu1)

    gm_twins(1)
    scatter_twins(r.wd, r.wd1, r.wd2, FU, link.wd1, link.wd2)
    gm_total(0)
    scatter_twins(r.wu, r.wu1, r.wu2, FU, link.wu1, link.wu2)

    loaded(ld.mo, G * SR * D * 2)

    def keep(hats, invs):
        def put(k, hat, inv):
            hats[k] = hat
            invs[k] = jnp.broadcast_to(inv, (TILE, LANES))

        return put

    NM, NL = SR // TILE, LR // TILE
    normalize_rows(
        lambda k: r.media_o[k // NM, rows_of(k % NM, TILE), :].astype(F32),
        keep(r.hat_m, r.inv_m), G * SR,
    )
    normalize_rows(
        lambda k: r.lat[k // NL, at_rows(me_h * LR + (k % NL) * TILE, TILE, TILE), :].astype(F32),
        keep(r.hat_l, r.inv_l), G * LR,
    )

    arrived(link.kv_x, (NK - 1) * 3 * nh * RC * W * 2)
    to_twins(relay_kvq)
    gm_total(1)
    head_relay(ga_at(0), link.ga_t, link.ga_y, 0)

    KR = SR + LR

    def take_rows(g):
        at = at_rows(g * KR, SR, LR)
        r.keys_o[at, :] = r.keys[at_rows(g * T + me_h * SR, SR, SR), :]
        at = at_rows(g * KR + SR, LR, LR)
        r.keys_o[at, :] = r.keys[at_rows(g * T + S + me_h * LR, LR, LR), :]

    repeat(G, take_rows)
    scatter_twins(r.wo, r.wo1, r.wo2, RC, link.wo1, link.wo2)
    arrived(link.kv_p, 3 * nh * RC * W * 2)
    arrived(link.kv_y, (NK - 1) * 3 * nh * RC * W * 2)

    def heads_project(o):
        r.kv_h[o] = dot(r.keys_o[...], r.wkv_f[:, rows_of(o, 2 * W)], NN).astype(BF16)
        q_all = dot(r.lat_n[...], r.wq_f[:, rows_of(o, W)], NN) * (HS**-0.5)
        r.q_h[o] = q_all.astype(BF16)

    repeat(nh, heads_project)
    head_relay(ga_at(1), link.ga_t, link.ga_y, 1)

    def image_back(g):
        rows, lat_rows = rows_of(g, T), rows_of(g, L)
        ga = spread(r.ga_f[g, :, own_w])
        q = spread(r.q[lat_rows, :])
        key, value = r.kv[rows, :W], r.kv[rows, W:]
        probs = r.probs[rows, :]
        grad_probs = dot(value, ga, NT)
        delta = jnp.sum(probs * grad_probs, axis=0, keepdims=True)
        put_row(r.delta.at[me_h], g, delta)
        grad_scores = (probs * (grad_probs - delta)).astype(BF16)
        r.gkv[g, :, W:] = dot(probs.astype(BF16), ga, NN).astype(BF16)
        r.gkv[g, :, :W] = dot(grad_scores, q, NN).astype(BF16)
        grad_query = gather_diag(dot(grad_scores, key, TN)).astype(BF16)
        r.gq[g] = (grad_query.astype(F32) * (HS**-0.5)).astype(BF16)

    for b in range(2):
        head_landed(ga_at(b), link.ga_m, link.ga_y, b)
        repeat(CG, lambda k: image_back(b * CG + k))
    to_all(r.delta, link.delta)
    to_heads(
        lambda o: send(r.gq.at[:, rows_of(o, LR), :], r.gq_r.at[:, :, own_w], link.gq, me_i, o)
    )
    r.gq_r[:, :, own_w] = r.gq[:, own_l, :]
    rows_pair(r.ffo_p, r.ffo1, link.ffo1, every)

    def proj_grad(t):
        at = rows_of(t, FT)
        left = r.gkv[...].reshape(G * T, 2 * W)
        r.wa[at, : 2 * W] = dot(r.keys[:, at], left, TN).astype(BF16)
        r.wa[at, 2 * W :] = dot(r.lat_n[:, at], r.gq[...].reshape(R, W), TN).astype(BF16)

    repeat(D // FT, proj_grad)
    scatter_pair(r.wa, r.wa1, RC, link.wa1)
    scatter_twins(r.wa, r.wa1, r.wa2, RC, link.wa1, link.wa2)
    arrived(link.lse, (nh - 1) * G * HN * L * 4)
    arrived(link.delta, (nh - 1) * G * HN * L * 4)

    def heads_back(o):
        wide = rows_of(o, 2 * W)
        for g in range(G):
            rows = pl.ds(g * KR, KR)
            ga = spread(r.ga_f[g, :, rows_of(o, W)])
            q = spread(r.q_h[o, g * L : (g + 1) * L, :])
            key, value = r.kv_h[o, rows, :W], r.kv_h[o, rows, W:]
            scores = dot(key, q, NT)
            place = lax.broadcasted_iota(jnp.int32, scores.shape, 0)
            valid = (place + me_h * SR < r.counts[g]) | (place >= SR)
            probs = jnp.exp(jnp.where(valid, scores, -1e30) - r.lse[o, g : g + 1, :])
            grad_probs = dot(value, ga, NT)
            grad_scores = (probs * (grad_probs - r.delta[o, g : g + 1, :])).astype(BF16)
            grad_value = dot(probs.astype(BF16), ga, NN)
            grad_key = dot(grad_scores, q, NN)
            both = jnp.concatenate([grad_key, grad_value], axis=1)
            r.gkv_r[g, :, wide] = both.astype(BF16)

    repeat(nh, heads_back)
    scatter_sum(r.wo, r.wo1, r.wo2, RC, link.wo2, r.tmp.at[:RC, : nh * W])
    for k in range(nh):
        r.wo_s[k] = r.tmp[:RC, k * W : (k + 1) * W].astype(BF16)
    out.wo[...] = r.tmp[:RC, own_w]
    to_heads(lambda o: send(r.wo_s.at[o], r.wo_z.at[me_h], link.wo3, me_i, o))
    rows_twins(r.ffo_p, r.ffo1, r.ffo2, link.ffo1, link.ffo2, every, G)

    arrived(link.gq, (nh - 1) * G * LR * W * 2)

    def put(k, at=slice(None)):
        name = list(outs)[k]
        a, b = getattr(out, name).at[at], getattr(dst, name).at[at]
        pltpu.make_async_copy(a, b, out_sems.at[k]).start()

    def own_rows(b):
        two = pl.ds(2 * b, 2)
        left = r.gkv_r[two, :, :].reshape(2 * KR, nh * 2 * W)
        r.tmp[: 2 * KR, :D] = dot(left, r.wkv_f[...], NT)
        query = dot(r.gq_r[two, :, :].reshape(2 * LR, nh * W), r.wq_f[...], NT)
        for k in range(2):
            r.tmp[pl.ds(k * KR + SR, LR), :D] += query[k * LR : (k + 1) * LR]

        def read_media(j):
            k = j // NM
            u = r.tmp[at_rows(k * KR + (j % NM) * TILE, TILE, TILE), :D]
            return u, r.hat_m[b * 2 * NM + j], r.inv_m[b * 2 * NM + j][:, :1]

        def write_media(j, grad):
            out.mg[2 * b + j // NM, rows_of(j % NM, TILE), :] = grad.astype(BF16)

        norm_back_rows(read_media, write_media, 2 * SR, gain_m, 0)
        def read_latent(j):
            at = at_rows((j // NL) * KR + SR + (j % NL) * TILE, TILE, TILE)
            return r.tmp[at, :D], r.hat_l[b * 2 * NL + j], r.inv_l[b * 2 * NL + j][:, :1]

        def write_latent(j, grad):
            g, part = 2 * b + j // NL, rows_of(j % NL, TILE)
            out.lg[g, part, :] = (grad + r.gm_o[g, part, :]).astype(BF16)

        norm_back_rows(read_latent, write_latent, 2 * LR, gain_l, 2)
        put(1, two)
        put(2, two)

    repeat(G // 2, own_rows)

    for k in range(6):
        r.vec[k : k + 1, :] = jnp.sum(r.vacc[k], axis=0, keepdims=True)
    r.vec[6:8, :] = jnp.zeros((2, D), F32)

    def block(i):
        return at_rows(lax.div(i * RC, LANES) * LANES, LANES, LANES)

    def vec_step(k):
        o = lax.rem(me_i + 1 + k, ni)
        send(r.vec.at[:, block(o)], r.vec_r.at[me_i], link.vp, o, me_h, times=ni - 1)

    repeat(ni - 1, vec_step)

    scatter_sum(r.wd, r.wd1, r.wd2, FU, link.wd2, out.dn)
    put(6)
    scatter_sum(r.wu, r.wu1, r.wu2, FU, link.wu2, out.up)
    put(5)
    scatter_sum(r.wa, r.wa1, r.wa2, RC, link.wa2, out.wa)
    put(3)
    arrived(link.vp, (ni - 1) * 8 * LANES * 4)
    r.vec_t[...] = r.vec[:, block(me_i)]

    def vec_sum(k):
        r.vec_t[...] += r.vec_r[lax.rem(me_i + 1 + k, ni)]

    repeat(ni - 1, vec_sum)
    to_heads(lambda o: send(r.vec_t, r.vec_z.at[me_h], link.vz, me_i, o))
    total = rows_total(r.ffo_p, r.ffo1, r.ffo2, link.ffo2, every, G)
    out.lat[...] = (r.mid_o[...] + total).astype(BF16)
    arrived(link.wo3, (nh - 1) * RC * W * 2)
    total = out.wo[...]
    for o in heads:
        total = total + r.wo_z[o].astype(F32)
    out.wo[...] = total
    arrived(link.vz, (nh - 1) * 8 * LANES * 4)
    total = r.vec_t[...]
    for o in heads:
        total = total + r.vec_z[o]
    out.vec[...] = total
    for k in (0, 4, 7):
        put(k)

    for to in vars(link).values():
        if to.bytes:
            await_bytes(send_sems.at[to.send], to.bytes)
    for k, name in enumerate(outs):
        pltpu.make_async_copy(getattr(out, name), getattr(dst, name), out_sems.at[k]).wait()


def finish(z, *refs):
    n = len(outputs(z)) - 1
    src, dst, buf, turned, in_sems, out_sems = (
        refs[:n], refs[n : n + 9], refs[n + 9 : 2 * n + 9], refs[-3], refs[-2], refs[-1]
    )
    W = z.W
    loads = [pltpu.make_async_copy(src[k], buf[k], in_sems.at[k]) for k in range(n)]
    for copy in loads:
        copy.start()
    stores = []

    def store(ref, k):
        stores.append(pltpu.make_async_copy(ref, dst[k], out_sems.at[k]))
        stores[-1].start()

    lat, mg, lg, wa, wo, up, dn = range(7)
    loads[mg].wait()
    store(buf[mg], 1)
    loads[up].wait()
    store(buf[up], 7)
    loads[dn].wait()
    store(buf[dn], 8)
    loads[lat].wait()
    store(buf[lat], 0)
    loads[lg].wait()
    store(buf[lg], 2)
    loads[wa].wait()
    store(buf[wa].at[:, pl.ds(2 * W, W)], 3)
    store(buf[wa].at[:, pl.ds(0, W)], 4)
    store(buf[wa].at[:, pl.ds(W, W)], 5)
    loads[wo].wait()
    turned[...] = buf[wo][...].T
    store(turned, 6)
    for copy in stores:
        copy.wait()


def body(ni, nh, media, latents, counts, media_gain, media_bias, latent_gain, latent_bias, w_query,
         w_key, w_value, w_out, ff_gain, ff_bias, w_up, w_down, cotangent):
    z = sizes(ni, nh, media, latents, w_query, w_up)
    D, W, RC = z.D, z.W, z.RC
    vm = pl.BlockSpec(memory_space=pltpu.VMEM)
    hbm = pl.BlockSpec(memory_space=pl.ANY)
    dma = pltpu.SemaphoreType.DMA
    outs = list(outputs(z).values())
    rows = [
        v.reshape(1, D)
        for v in (media_gain, media_bias, latent_gain, latent_bias, ff_gain, ff_bias)
    ]
    counted = links(z).values()
    res = pl.pallas_call(
        functools.partial(kernel, z),
        out_shape=[jax.ShapeDtypeStruct(s, d) for s, d in outs],
        in_specs=[pl.BlockSpec(memory_space=pltpu.SMEM)] + [vm] * 6 + [hbm] * 9,
        out_specs=[hbm] * len(outs),
        scratch_shapes=[pltpu.VMEM(s, d) for s, d in (*scratch(z).values(), *outs)]
        + [
            dma((sum(a for a, _ in counted),)),
            dma((sum(b for _, b in counted),)),
            dma((len(LOADS),)),
            dma((len(outs),)),
        ],
        compiler_params=pltpu.CompilerParams(
            collective_id=0, has_side_effects=True, vmem_limit_bytes=67043328
        ),
    )(counts, *rows, media, latents, w_query, w_key, w_value, w_out, w_up, w_down, cotangent)
    last = outs[:3] + [((RC, W), F32)] * 3 + [((W, RC), F32)] + outs[5:7]
    res2 = pl.pallas_call(
        functools.partial(finish, z),
        out_shape=[jax.ShapeDtypeStruct(s, d) for s, d in last],
        in_specs=[hbm] * 7,
        out_specs=[hbm] * 9,
        scratch_shapes=[pltpu.VMEM(s, d) for s, d in outs[:7]]
        + [pltpu.VMEM((W, RC), F32), dma((7,)), dma((9,))],
    )(*res[:7])
    lat_out, media_grad, lat_grad, wq, wk, wv, wo, up, down = res2
    share = D // (ni * nh)
    place = lax.axis_index("img") * nh + lax.axis_index("head")
    vec = lax.dynamic_slice(res[7], (0, lax.rem(place * share, LANES)), (8, share))
    return (
        lat_out, media_grad, lat_grad, vec[0], vec[1], vec[2], vec[3], wq, wk, wv, wo, vec[4],
        vec[5], up, down,
    )


def solution(mesh):
    ni, nh = mesh.shape["img"], mesh.shape["head"]
    both = P(("img", "head"))
    rows = P("img", "head", None)
    return jax.shard_map(
        functools.partial(body, ni, nh),
        mesh=mesh,
        in_specs=(
            P("img", None, None), P("img", None, None), P("img"), P(), P(), P(), P(),
            P(None, "head"), P(None, "head"), P(None, "head"), P("head", None), P(), P(),
            P(("img", "head"), None), P(("img", "head"), None), rows,
        ),
        out_specs=(
            rows, rows, rows, both, both, both, both, P("img", "head"), P("img", "head"),
            P("img", "head"), P("head", "img"), both, both, P(("img", "head"), None),
            P(("img", "head"), None),
        ),
        check_vma=False,
    )
```

```python
import functools
import math
from types import SimpleNamespace

import jax
import jax.numpy as jnp
from jax import lax
from jax.experimental import pallas as pl
from jax.experimental.pallas import tpu as pltpu
from jax.sharding import PartitionSpec as P

HS = 64
EPSILON = 1e-05
LANES = 128
TILE = 16
SIDE = 16
LAG = 4
BF16 = jnp.bfloat16
F32 = jnp.float32
MESH = pl.DeviceIdType.MESH
NN = ((1,), (0,))
NT = ((1,), (1,))
TN = ((0,), (0,))


def dot(a, b, dims):
    return lax.dot_general(a, b, (dims, ((), ())), preferred_element_type=F32)


def fold_rows(x):
    return jnp.sum(x.reshape(x.shape[0] // 8, 8, x.shape[1]), axis=0)


def gelu_parts(hidden):
    normal_cdf = 0.5 * (1.0 + lax.erf(hidden * (1.0 / math.sqrt(2.0))))
    density = jnp.exp(-0.5 * hidden * hidden) * (1.0 / math.sqrt(2.0 * math.pi))
    return (hidden * normal_cdf, normal_cdf + hidden * density)


def sizes(ni, nh, media, latents, w_query, w_up):
    G, S, D = media.shape
    L, W, FU = latents.shape[1], w_query.shape[1], w_up.shape[0]
    Q = min(ni, W // TILE)
    return SimpleNamespace(
        ni=ni, nh=nh, G=G, S=S, D=D, L=L, W=W, FU=FU, T=S + L, SR=S // nh, LR=L // nh, R=G * L,
        FH=ni * FU, RC=D // ni, NK=ni // 2, NH=nh // 2, HN=W // HS, Q=Q, QC=W // Q,
    )


def outputs(z):
    return dict(
        lat=((z.G, z.LR, z.D), BF16),
        mg=((z.G, z.SR, z.D), BF16),
        lg=((z.G, z.LR, z.D), BF16),
        wa=((z.RC, 3 * z.W), F32),
        wo=((z.RC, z.W), F32),
        up=((z.FU, z.D), F32),
        dn=((z.FU, z.D), F32),
        vec=((8, LANES), F32),
    )


def scratch(z):
    G, D, L, W, T, SR, LR, R, FH, RC, NK, NH, FU, nh = (
        z.G, z.D, z.L, z.W, z.T, z.SR, z.LR, z.R, z.FH, z.RC, z.NK, z.NH, z.FU, z.nh
    )
    return dict(
        media_b=((2, z.S, D), BF16),
        media_o=((G, SR, D), BF16),
        lat=((G, L, D), BF16),
        keys=((G * T, D), BF16),
        lat_n=((R, D), BF16),
        wkv_o=((D, 2 * W), BF16),
        wq_o=((D, W), BF16),
        wkv_f=((D, nh * 2 * W), BF16),
        wq_f=((D, nh * W), BF16),
        wout_f=((nh * W, D), BF16),
        up_f=((FH, D), BF16),
        down_f=((FH, D), BF16),
        cot_f=((G, L, D), BF16),
        kv=((G * T, 2 * W), BF16),
        q=((R, W), BF16),
        probs=((G * T, z.HN * L), F32),
        att_f=((G, L, nh * W), BF16),
        mid_o=((G, LR, D), F32),
        hat=((R, D), F32),
        inv=((R, LANES), F32),
        ff_in=((R, D), BF16),
        act=((R, FH), BF16),
        slope=((R, FH), F32),
        gh=((R, FH), BF16),
        tmp=((max(R // 2, 4 * (SR + LR)), max(D, FH)), F32),
        ffo_p=((G, L, D), BF16),
        gm_p=((G, L, D), BF16),
        ffo1=((NH, G, LR, D), BF16),
        ffo2=((NH, G, LR, D), BF16),
        gm1=((NH, G, LR, D), BF16),
        gm2=((NH, G, LR, D), BF16),
        gm_o=((G, LR, D), F32),
        ga_f=((G, L, nh * W), BF16),
        lse=((nh, G, z.HN * L), F32),
        delta=((nh, G, z.HN * L), F32),
        keys_o=((G * (SR + LR), D), BF16),
        kv_h=((nh, G * (SR + LR), 2 * W), BF16),
        q_h=((nh, R, W), BF16),
        probs_h=((nh, G * (SR + LR), z.HN * L), F32),
        gkv=((G, T, 2 * W), BF16),
        gq=((G, L, W), BF16),
        gkv_r=((G, SR + LR, nh * 2 * W), BF16),
        gq_r=((G, LR, nh * W), BF16),
        wu=((FH, D), BF16),
        wd=((FH, D), BF16),
        wo=((D, nh * W), BF16),
        wa=((D, 3 * W), BF16),
        wu1=((NK * FU, D), BF16),
        wd1=((NK * FU, D), BF16),
        wo1=((NK * RC, nh * W), BF16),
        wa1=((NK * RC, 3 * W), BF16),
        wu2=((NK * FU, D), BF16),
        wd2=((NK * FU, D), BF16),
        wo2=((NK * RC, nh * W), BF16),
        wa2=((NK * RC, 3 * W), BF16),
        wo_s=((nh, RC, W), BF16),
        wo_z=((nh, RC, W), BF16),
        hat_m=((G * SR // TILE, TILE, D), F32),
        inv_m=((G * SR // TILE, TILE, LANES), F32),
        hat_l=((G * LR // TILE, TILE, D), F32),
        inv_l=((G * LR // TILE, TILE, LANES), F32),
        vacc=((6, 8, D), F32),
        vec=((8, D), F32),
        vec_r=((z.ni, 8, LANES), F32),
        vec_t=((8, LANES), F32),
        vec_z=((nh, 8, LANES), F32),
    )


def links(z):
    G = z.G
    one = (1, 1)
    return dict(
        wout_z=one, wout_x=one, wout_p=one, wout_y=one, up_p=one, up_x=one, up_y=one, dn_p=one, dn_x=one, dn_y=one,
        kvq_t=one, kvq_m=one, kvq_y=one, kv_p=one, kv_x=one, kv_y=one,
        cot_t=(2, 1), cot_m=(2, 1), cot_y=(2, 1), att_t=(G, 1), att_m=(G, 1), att_y=(G, 1), lse=one,
        delta=one, ga_t=(2, 1), ga_m=(2, 1), ga_y=(2, 1), gq=one,
        ffo1=(2, 1), ffo2=(2, 1), gm1=(2, 1), gm2=(2, 1),
        wu1=one, wu2=one, wd1=one, wd2=one, wo1=one, wo2=one, wo3=one, wa1=one, wa2=one,
        vp=one, vz=one,
    )


LOADS = dict(m0=0, m1=1, w=2, lat=3, ff=4, kvq=5, mo=6)
INS = tuple(
    dict(
        counts=0, g_m=0, b_m=0, g_l=0, b_l=0, g_f=0, b_f=0, media=0, latents=0, w_query=0, w_key=0,
        w_value=0, w_out=0, w_up=0, w_down=0, cot=0,
    )
)


def kernel(z, *refs):
    outs, vmem = outputs(z), scratch(z)
    n_in, n_out = len(INS), len(outs)
    r = SimpleNamespace(
        **dict(zip(INS, refs[:n_in])),
        **dict(zip(vmem, refs[n_in + n_out :])),
    )
    dst = SimpleNamespace(**dict(zip(outs, refs[n_in : n_in + n_out])))
    out = SimpleNamespace(**dict(zip(outs, refs[n_in + n_out + len(vmem) :])))
    recv_sems, send_sems, load_sems, out_sems = refs[-4:]
    G, S, D, L, W, FU, T, SR, LR, R, FH, RC, NK, NH, HN = (
        z.G, z.S, z.D, z.L, z.W, z.FU, z.T, z.SR, z.LR, z.R, z.FH, z.RC, z.NK, z.NH, z.HN
    )
    ni, nh = z.ni, z.nh
    me_i, me_h = lax.axis_index("img"), lax.axis_index("head")
    par, half = lax.rem(me_i, 2), lax.div(me_i, 2)
    mate = me_i + 1 - 2 * par
    par_h, half_h = lax.rem(me_h, 2), lax.div(me_h, 2)
    mate_h = me_h + 1 - 2 * par_h
    halves_h = [lax.rem(half_h + k, NH) for k in range(1, NH)]
    twins_h = [2 * k + par_h for k in halves_h]

    link, n_recv, n_send = {}, 0, 0
    for name, (a, b) in links(z).items():
        link[name] = SimpleNamespace(recv=n_recv, send=n_send, bytes=0)
        n_recv, n_send = n_recv + a, n_send + b
    link = SimpleNamespace(**link)
    ld = SimpleNamespace(**LOADS)

    def size(ref):
        return math.prod(ref.shape) * jnp.dtype(ref.dtype).itemsize

    def await_bytes(sem, nbytes):
        lanes = D
        while nbytes % (2 * lanes * TILE):
            lanes //= 2
        assert lanes >= LANES and nbytes // (2 * lanes) <= G * T
        view = r.keys.at[pl.ds(0, nbytes // (2 * lanes)), pl.ds(0, lanes)]
        pltpu.make_async_copy(view, view, sem).wait()

    def load(src, dst, k):
        pltpu.make_async_copy(src, dst, load_sems.at[k]).start()

    def loaded(k, nbytes):
        await_bytes(load_sems.at[k], nbytes)

    def arrived(to, nbytes, k=0):
        await_bytes(recv_sems.at[to.recv + k], nbytes)

    def push(src, dst, to, img, head, k=0, s=0):
        pltpu.make_async_remote_copy(
            src_ref=src,
            dst_ref=dst,
            send_sem=send_sems.at[to.send + s],
            recv_sem=recv_sems.at[to.recv + k],
            device_id=(img, head),
            device_id_type=MESH,
        ).start()

    def send(src, dst, to, img, head, k=0, times=1):
        push(src, dst, to, img, head, k)
        to.bytes += size(src) * times

    def rows_of(i, n):
        return pl.ds(pl.multiple_of(i * n, n), n)

    def at_rows(start, n, unit):
        return pl.ds(pl.multiple_of(start, unit), n)

    heads = [lax.rem(me_h + d, nh) for d in range(1, nh)]

    def to_heads(f):
        for other in heads:
            f(other)

    def to_twins(f):
        def step(k, c):
            f(lax.rem(half + k, NK) * 2 + par)
            return c

        lax.fori_loop(1, NK, step, 0)

    def head_spread(view, src, twins, pair, k=0, times=1):
        for o in twins_h:
            send(src, view(me_h), twins, me_i, o, k, times)
        send(src, view(me_h), pair, me_i, mate_h, k, times)

    def head_relay(view, twins, onto, k=0, times=1):
        arrived(twins, (NH - 1) * size(view(0)), k)
        for o in twins_h:
            send(view(o), view(o), onto, me_i, mate_h, k, times)

    def head_landed(view, pair, onto, k=0):
        arrived(pair, size(view(0)), k)
        arrived(onto, (NH - 1) * size(view(0)), k)

    def head_pair(view, got, to, k=0, times=1):
        for p in range(NH):
            send(view(2 * p + 1 - par_h), got(p), to, me_i, mate_h, k, times)

    def repeat(n, f):
        if n == 1:
            return f(0)

        def step(k, c):
            f(k)
            return c

        lax.fori_loop(0, n, step, 0)

    load(r.media.at[0], r.media_b.at[0], ld.m0)
    load(r.w_key, r.wkv_o.at[:, pl.ds(0, W)], ld.w)
    load(r.w_value, r.wkv_o.at[:, pl.ds(W, W)], ld.w)
    load(r.w_query, r.wq_o, ld.w)
    load(r.latents, r.lat, ld.lat)
    load(r.media.at[1], r.media_b.at[1], ld.m1)
    barrier = pltpu.get_barrier_semaphore()
    to_heads(
        lambda o: pl.semaphore_signal(
            barrier, inc=1, device_id=(me_i, o), device_id_type=MESH
        )
    )
    repeat(
        ni - 1,
        lambda k: pl.semaphore_signal(
            barrier, inc=1, device_id=(lax.rem(me_i + 1 + k, ni), me_h), device_id_type=MESH
        ),
    )
    pl.semaphore_wait(barrier, nh - 1 + ni - 1)

    Q, QC = z.Q, z.QC
    share = lax.rem(me_i, Q)
    first = me_i - share
    wo_part = at_rows(me_h * W + share * QC, QC, QC)
    to_heads(
        lambda o: send(r.w_out.at[rows_of(share, QC)], r.wout_f.at[wo_part], link.wout_z, me_i, o)
    )
    own_f = rows_of(me_i, FU)
    own_l = rows_of(me_h, LR)

    CR, CG = R // 2, G // 2

    def cot_at(b):
        return lambda o: r.cot_f.at[pl.ds(b * CG, CG), rows_of(o, LR), :]

    def cot_spread(b):
        head_spread(cot_at(b), r.cot.at[pl.ds(b * CG, CG)], link.cot_t, link.cot_m, b)

    cot_spread(0)

    def spread_rows(src, buf, twins, pair):
        to_twins(lambda o: send(src, buf.at[own_f], twins, o, me_h, times=NK - 1))
        send(src, buf.at[own_f], pair, mate, me_h)

    spread_rows(r.w_up, r.up_f, link.up_x, link.up_p)
    load(r.w_out, r.wout_f.at[rows_of(me_h, W)], ld.ff)
    load(r.w_up, r.up_f.at[own_f], ld.ff)
    load(r.w_down, r.down_f.at[own_f], ld.ff)
    load(r.cot, r.cot_f.at[:, own_l, :], ld.ff)
    own_kv = [at_rows(me_h * 2 * W + k * W, W, W) for k in range(2)]
    own_w = rows_of(me_h, W)
    own_c = rows_of(me_i, RC)
    load(r.w_key.at[own_c], r.wkv_f.at[own_c, own_kv[0]], ld.kvq)
    load(r.w_value.at[own_c], r.wkv_f.at[own_c, own_kv[1]], ld.kvq)
    load(r.w_query.at[own_c], r.wq_f.at[own_c, own_w], ld.kvq)
    load(r.media.at[:, rows_of(me_h, SR), :], r.media_o, ld.mo)

    gain_m, bias_m = r.g_m[...], r.b_m[...]
    gain_l, bias_l = r.g_l[...], r.b_l[...]
    gain_f, bias_f = r.g_f[...], r.b_f[...]

    def normalize_rows(read, write, n):
        side = min(n // TILE, SIDE)

        def step(b):
            ks = [b * side + j for j in range(side)]
            mean = [jnp.sum(read(k), axis=-1, keepdims=True) * (1.0 / D) for k in ks]
            var = [
                jnp.sum(jnp.square(read(k) - m), axis=-1, keepdims=True) * (1.0 / D)
                for k, m in zip(ks, mean)
            ]
            inv = [lax.rsqrt(v + EPSILON) for v in var]
            for k, m, i in zip(ks, mean, inv):
                write(k, (read(k) - m) * i, i)

        repeat(n // TILE // side, step)

    def norm_back_rows(read, write, n, gain, k_gain):
        side = min(n // TILE, SIDE)

        def step(b):
            ks = [b * side + j for j in range(side)]
            means = []
            for k in ks:
                u, hat, _ = read(k)
                u = u * gain
                means.append(
                    [jnp.sum(v, axis=-1, keepdims=True) * (1.0 / D) for v in (u, u * hat)]
                )
            gains = biases = jnp.zeros((8, D), F32)
            for k, (one, two) in zip(ks, means):
                u, hat, inv = read(k)
                write(k, inv * (u * gain - one - hat * two))
                gains, biases = gains + fold_rows(u * hat), biases + fold_rows(u)
            r.vacc[k_gain] += gains
            r.vacc[k_gain + 1] += biases

        repeat(n // TILE // side, step)

    lane_head = lax.div(lax.broadcasted_iota(jnp.int32, (L, W), 1), HS)

    def spread(x):
        zero = jnp.zeros_like(x)
        return jnp.concatenate([jnp.where(lane_head == k, x, zero) for k in range(HN)], axis=0)

    def gather_diag(x):
        out = x[:L]
        for k in range(1, HN):
            out = jnp.where(lane_head == k, x[k * L : (k + 1) * L], out)
        return out

    loaded(ld.w, 3 * D * W * 2)
    loaded(ld.lat, G * L * D * 2)

    def row_of(g, n):
        return lax.broadcasted_iota(jnp.int32, (G, n), 0) == g

    def put_row(ref, g, x):
        ref[...] = jnp.where(row_of(g, x.shape[1]), x, ref[...])

    def to_all(ref, to):
        to_heads(lambda o: send(ref.at[me_h], ref.at[me_h], to, me_i, o))

    def kv_at(k):
        return lambda o: r.wkv_f.at[own_c, at_rows(o * 2 * W + k * W, W, W)]

    def kvq_views():
        return (
            (r.w_key, kv_at(0)), (r.w_value, kv_at(1)),
            (r.w_query, lambda o: r.wq_f.at[own_c, rows_of(o, W)]),
        )

    def att_at(g):
        return lambda o: r.att_f.at[g, :, rows_of(o, W)]

    def ga_at(b):
        return lambda o: r.ga_f.at[pl.ds(b * CG, CG), rows_of(o, LR), :]

    r.lse[me_h] = r.delta[me_h] = jnp.zeros((G, HN * L), F32)

    def relay(twins, onto, buf, n):
        arrived(twins, (NK - 1) * size(buf.at[rows_of(0, n)]))
        to_twins(
            lambda o: send(
                buf.at[rows_of(o, n)], buf.at[rows_of(o, n)], onto, mate, me_h, times=NK - 1
            )
        )

    def wout_send(o, s, to, img):
        at = r.wout_f.at[at_rows(o * W + s * QC, QC, QC)]
        send(at, at, to, img, me_h)

    def relay_wout():
        arrived(link.wout_x, (Q // 2 - 1) * (nh - 1) * QC * D * 2)
        for d in range(1, Q // 2):
            s = lax.rem(lax.div(share, 2) + d, Q // 2) * 2 + par
            to_heads(lambda o: wout_send(o, s, link.wout_y, mate))

    def share_wout():
        arrived(link.wout_z, (nh - 1) * QC * D * 2)

        for d in range(1, Q // 2):
            other = lax.rem(lax.div(share, 2) + d, Q // 2) * 2 + par
            to_heads(lambda o: wout_send(o, share, link.wout_x, first + other))
        to_heads(lambda o: wout_send(o, share, link.wout_p, mate))
        spread_rows(r.w_down, r.down_f, link.dn_x, link.dn_p)

    def image(g):
        slot = lax.rem(g, 2)
        for k, sem in enumerate((ld.m0, ld.m1)):

            @pl.when(slot == k)
            def _():
                loaded(sem, S * D * 2)

        def put_media(k, hat, _):
            r.keys[at_rows(g * T + k * TILE, TILE, TILE), :] = (hat * gain_m + bias_m).astype(BF16)

        def put_latent(k, hat, _):
            y = (hat * gain_l + bias_l).astype(BF16)
            r.keys[at_rows(g * T + S + k * TILE, TILE, TILE), :] = y
            r.lat_n[at_rows(g * L + k * TILE, TILE, TILE), :] = y

        normalize_rows(lambda k: r.media_b[slot, rows_of(k, TILE), :].astype(F32), put_media, S)
        normalize_rows(lambda k: r.lat[g, rows_of(k, TILE), :].astype(F32), put_latent, L)
        for k, sem in enumerate((ld.m0, ld.m1)):

            @pl.when((slot == k) & (g + 2 < G))
            def _():
                load(r.media.at[g + 2], r.media_b.at[k], sem)

        rows, lat_rows = rows_of(g, T), rows_of(g, L)
        kv = dot(r.keys[rows, :], r.wkv_o[...], NN).astype(BF16)
        r.kv[rows, :] = kv
        q = (dot(r.lat_n[lat_rows, :], r.wq_o[...], NN) * (HS**-0.5)).astype(BF16)
        r.q[lat_rows, :] = q
        scores = dot(kv[:, :W], spread(q), NT)
        place = lax.broadcasted_iota(jnp.int32, scores.shape, 0)
        scores = jnp.where((place < r.counts[g]) | (place >= S), scores, -1e30)
        top = jnp.max(scores, axis=0, keepdims=True)
        total = jnp.sum(jnp.exp(scores - top), axis=0, keepdims=True)
        lse = top + jnp.log(total)
        put_row(r.lse.at[me_h], g, lse)
        probs = jnp.exp(scores - lse)
        r.probs[rows, :] = probs
        att = gather_diag(dot(probs.astype(BF16), kv[:, W:], TN)).astype(BF16)
        r.att_f[g, :, own_w] = att
        head_spread(att_at(g), r.att_f.at[g, :, own_w], link.att_t, link.att_m, g, G)

        @pl.when(g >= LAG)
        def _():
            head_relay(att_at(g - LAG), link.att_t, link.att_y, g - LAG, G - LAG)

        @pl.when(g == 2)
        def _():
            share_wout()

        @pl.when(g == G - 1)
        def _():
            relay_wout()

        @pl.when(g == G // 2 + 1)
        def _():
            for w, view in kvq_views():
                head_spread(view, w.at[own_c], link.kvq_t, link.kvq_m)

        @pl.when(g == G // 2)
        def _():
            head_relay(cot_at(0), link.cot_t, link.cot_y, 0)

        @pl.when(g == G - 2)
        def _():
            relay(link.up_x, link.up_y, r.up_f, FU)

    repeat(G, image)
    for g in range(G - LAG, G):
        head_relay(att_at(g), link.att_t, link.att_y, g)
    arrived(link.kvq_t, (NH - 1) * 3 * RC * W * 2)
    for _, view in kvq_views():
        for o in twins_h:
            send(view(o), view(o), link.kvq_y, me_i, mate_h)
    to_all(r.lse, link.lse)
    cot_spread(1)
    r.vacc[...] = jnp.zeros_like(r.vacc)

    loaded(ld.ff, (W + 2 * FU + G * LR) * D * 2)
    arrived(link.wout_p, (nh - 1) * QC * D * 2)
    arrived(link.wout_y, (Q // 2 - 1) * (nh - 1) * QC * D * 2)

    def ff_forward(b):
        for k in range(CG):
            head_landed(att_at(b * CG + k), link.att_m, link.att_y, b * CG + k)
        at = rows_of(b, CR)
        imgs = pl.ds(b * CG, CG)
        att = r.att_f[imgs, :, :].reshape(CR, nh * W)
        base = r.lat[imgs, :, :].reshape(CR, D).astype(F32)
        r.tmp[:CR, :D] = dot(att, r.wout_f[...], NN) + base
        for k in range(nh):

            @pl.when(me_h == k)
            def _():
                r.mid_o[imgs] = r.tmp[:CR, :D].reshape(CG, nh, LR, D)[:, k]

        def put_norm(k, hat, inv):
            row = at_rows(b * CR + k * TILE, TILE, TILE)
            r.hat[row, :] = hat
            r.inv[row, :] = jnp.broadcast_to(inv, (TILE, LANES))
            r.ff_in[row, :] = (hat * gain_f + bias_f).astype(BF16)

        normalize_rows(lambda k: r.tmp[rows_of(k, TILE), :D], put_norm, CR)

        @pl.when(b == 0)
        def _():
            arrived(link.up_p, FU * D * 2)
            arrived(link.up_y, (NK - 1) * FU * D * 2)

        r.tmp[:CR, :FH] = dot(r.ff_in[at, :], r.up_f[...], NT)

        def gelu(k):
            row = at_rows(b * CR + k * TILE, TILE, TILE)
            value, slope = gelu_parts(r.tmp[rows_of(k, TILE), :FH])
            r.act[row, :] = value.astype(BF16)
            r.slope[row, :] = slope

        repeat(CR // TILE, gelu)

    repeat(2, ff_forward)

    def share_kvq(o, to, times):
        for buf in (r.wkv_f, r.wq_f):
            send(buf.at[own_c], buf.at[own_c], to, o, me_h, times=times)

    def relay_kvq(o):
        for buf in (r.wkv_f, r.wq_f):
            at = buf.at[rows_of(o, RC)]
            send(at, at, link.kv_y, mate, me_h, times=NK - 1)

    loaded(ld.kvq, 3 * RC * W * 2)
    arrived(link.kvq_m, 3 * RC * W * 2)
    arrived(link.kvq_y, (NH - 1) * 3 * RC * W * 2)
    to_twins(lambda o: share_kvq(o, link.kv_x, NK - 1))
    share_kvq(mate, link.kv_p, 1)

    head_relay(cot_at(1), link.cot_t, link.cot_y, 1)
    relay(link.dn_x, link.dn_y, r.down_f, FU)

    loaded(ld.mo, G * SR * D * 2)

    def keep(hats, invs):
        def put(k, hat, inv):
            hats[k] = hat
            invs[k] = jnp.broadcast_to(inv, (TILE, LANES))

        return put

    NM, NL = SR // TILE, LR // TILE
    normalize_rows(
        lambda k: r.media_o[k // NM, rows_of(k % NM, TILE), :].astype(F32),
        keep(r.hat_m, r.inv_m), G * SR,
    )
    normalize_rows(
        lambda k: r.lat[k // NL, at_rows(me_h * LR + (k % NL) * TILE, TILE, TILE), :].astype(F32),
        keep(r.hat_l, r.inv_l), G * LR,
    )
    KR = SR + LR

    def take_rows(g):
        at = at_rows(g * KR, SR, LR)
        r.keys_o[at, :] = r.keys[at_rows(g * T + me_h * SR, SR, SR), :]
        at = at_rows(g * KR + SR, LR, LR)
        r.keys_o[at, :] = r.keys[at_rows(g * T + S + me_h * LR, LR, LR), :]

    repeat(G, take_rows)
    arrived(link.dn_p, FU * D * 2)
    arrived(link.dn_y, (NK - 1) * FU * D * 2)

    def rows_pair(part, got, to, imgs, k=0, times=1):
        head_pair(
            lambda o: part.at[imgs, rows_of(o, LR), :], lambda p: got.at[p, imgs], to, k, times
        )

    def rows_twins(part, got, got2, to, to2, imgs, n, k=0):
        arrived(to, NH * n * LR * D * 2, k)
        for p, o in zip(halves_h, twins_h):
            at = rows_of(o, LR)
            both = part[imgs, at, :].astype(F32) + got[p, imgs].astype(F32)
            part[imgs, at, :] = both.astype(BF16)
            send(part.at[imgs, at, :], got2.at[half_h, imgs], to2, me_i, o, k)

    def rows_total(part, got, got2, to2, imgs, n, k=0):
        arrived(to2, (NH - 1) * n * LR * D * 2, k)
        x = part[imgs, own_l, :].astype(F32) + got[half_h, imgs].astype(F32)
        for p in halves_h:
            x = x + got2[p, imgs].astype(F32)
        return x

    def ff_out(b):
        out = dot(r.act[rows_of(b, CR), :], r.down_f[...], NN)
        r.ffo_p[pl.ds(b * CG, CG), :, :] = out.astype(BF16).reshape(CG, L, D)

    FIRST = CG // 2
    ff_out(0)
    rows_pair(r.ffo_p, r.ffo1, link.ffo1, pl.ds(0, FIRST), 0)

    def ff_backward(b):
        at, imgs = rows_of(b, CR), pl.ds(b * CG, CG)
        head_landed(cot_at(b), link.cot_m, link.cot_y, b)
        r.tmp[:CR, :FH] = dot(r.cot_f[imgs, :, :].reshape(CR, D), r.down_f[...], NT)

        def slope(k):
            row = at_rows(b * CR + k * TILE, TILE, TILE)
            r.gh[row, :] = (r.tmp[rows_of(k, TILE), :FH] * r.slope[row, :]).astype(BF16)

        repeat(CR // TILE, slope)
        r.tmp[:CR, :D] = dot(r.gh[at, :], r.up_f[...], NN)

        def read(k):
            row = at_rows(b * CR + k * TILE, TILE, TILE)
            return r.tmp[rows_of(k, TILE), :D], r.hat[row, :], r.inv[row, :1]

        def write(k, grad):
            g, part = b * CG + k * TILE // L, rows_of(k % (L // TILE), TILE)
            cot = r.cot_f[g, part, :].astype(F32) * (1.0 / nh)
            r.gm_p[g, part, :] = (grad + cot).astype(BF16)

        norm_back_rows(read, write, CR, gain_f, 4)
        rows_pair(r.gm_p, r.gm1, link.gm1, imgs, b, 2)

    repeat(2, ff_backward)

    def ffo_twins(b):
        imgs = pl.ds(b * CG, CG)
        rows_twins(r.ffo_p, r.ffo1, r.ffo2, link.ffo1, link.ffo2, imgs, CG, b)

    def gm_twins(b):
        imgs = pl.ds(b * CG, CG)
        rows_twins(r.gm_p, r.gm1, r.gm2, link.gm1, link.gm2, imgs, CG, b)

    def gm_total(b):
        imgs = pl.ds(b * CG, CG)
        gm = rows_total(r.gm_p, r.gm1, r.gm2, link.gm2, imgs, CG, b)
        r.gm_o[imgs] = gm
        ga = dot(gm.astype(BF16).reshape(CG * LR, D), r.wout_f[...], NT).astype(BF16)
        r.ga_f[imgs, own_l, :] = ga.reshape(CG, LR, nh * W)
        head_spread(ga_at(b), r.ga_f.at[imgs, own_l, :], link.ga_t, link.ga_m, b)

    ff_out(1)

    def scatter_pair(buf, got, n, to):
        repeat(
            NK,
            lambda k: send(
                buf.at[rows_of(2 * k + 1 - par, n)], got.at[rows_of(k, n)], to, mate, me_h, times=NK
            ),
        )

    def scatter_twins(buf, got, got2, n, to, to2):
        arrived(to, size(got))

        def step(d, c):
            k = lax.rem(half + d, NK)
            mine = rows_of(2 * k + par, n)
            both = buf[mine, :].astype(F32) + got[rows_of(k, n), :].astype(F32)
            buf[mine, :] = both.astype(BF16)
            send(
                buf.at[mine], got2.at[rows_of(half, n)], to2, 2 * k + par, me_h, times=NK - 1
            )
            return c

        lax.fori_loop(1, NK, step, 0)

    def scatter_sum(buf, got, got2, n, to2, total):
        arrived(to2, size(got2) // NK * (NK - 1))
        total[...] = buf[rows_of(me_i, n), :].astype(F32) + got[rows_of(half, n), :].astype(F32)

        def step(d, c):
            total[...] += got2[rows_of(lax.rem(half + d, NK), n), :].astype(F32)
            return c

        lax.fori_loop(1, NK, step, 0)

    FT = 2 * LANES

    def out_grad(t):
        at = rows_of(t, FT)
        left = r.gm_p[:, :, at].reshape(R, FT)
        r.wo[at, :] = dot(left, r.att_f[...].reshape(R, nh * W), TN).astype(BF16)

    repeat(D // FT, out_grad)
    scatter_pair(r.wo, r.wo1, RC, link.wo1)

    def down_grad(t):
        at = rows_of(t, FT)
        r.wd[at, :] = dot(r.act[:, at], r.cot_f[...].reshape(R, D), TN).astype(BF16)

    repeat(FH // FT, down_grad)
    scatter_pair(r.wd, r.wd1, FU, link.wd1)
    gm_twins(0)
    scatter_twins(r.wo, r.wo1, r.wo2, RC, link.wo1, link.wo2)

    def up_grad(t):
        at = rows_of(t, FT)
        r.wu[at, :] = dot(r.gh[:, at], r.ff_in[...], TN).astype(BF16)

    repeat(FH // FT, up_grad)
    scatter_pair(r.wu, r.wu1, FU, link.wu1)

    gm_twins(1)
    arrived(link.kv_x, (NK - 1) * 3 * nh * RC * W * 2)
    to_twins(relay_kvq)
    scatter_twins(r.wd, r.wd1, r.wd2, FU, link.wd1, link.wd2)
    gm_total(0)
    scatter_twins(r.wu, r.wu1, r.wu2, FU, link.wu1, link.wu2)

    arrived(link.lse, (nh - 1) * G * HN * L * 4)
    arrived(link.kv_p, 3 * nh * RC * W * 2)
    arrived(link.kv_y, (NK - 1) * 3 * nh * RC * W * 2)

    def heads_project(o):
        r.kv_h[o] = dot(r.keys_o[...], r.wkv_f[:, rows_of(o, 2 * W)], NN).astype(BF16)
        q_all = dot(r.lat_n[...], r.wq_f[:, rows_of(o, W)], NN) * (HS**-0.5)
        r.q_h[o] = q_all.astype(BF16)
        for g in range(G):
            rows = pl.ds(g * KR, KR)
            q = spread(r.q_h[o, g * L : (g + 1) * L, :])
            scores = dot(r.kv_h[o, rows, :W], q, NT)
            place = lax.broadcasted_iota(jnp.int32, scores.shape, 0)
            valid = (place + me_h * SR < r.counts[g]) | (place >= SR)
            scores = jnp.where(valid, scores, -1e30)
            r.probs_h[o, rows, :] = jnp.exp(scores - r.lse[o, g : g + 1, :])

    repeat(nh, heads_project)
    gm_total(1)
    head_relay(ga_at(0), link.ga_t, link.ga_y, 0)

    head_relay(ga_at(1), link.ga_t, link.ga_y, 1)
    rows_pair(r.ffo_p, r.ffo1, link.ffo1, pl.ds(FIRST, CG - FIRST), 0)

    def image_back(g):
        rows, lat_rows = rows_of(g, T), rows_of(g, L)
        ga = spread(r.ga_f[g, :, own_w])
        q = spread(r.q[lat_rows, :])
        key, value = r.kv[rows, :W], r.kv[rows, W:]
        probs = r.probs[rows, :]
        grad_probs = dot(value, ga, NT)
        delta = jnp.sum(probs * grad_probs, axis=0, keepdims=True)
        put_row(r.delta.at[me_h], g, delta)
        grad_scores = (probs * (grad_probs - delta)).astype(BF16)
        r.gkv[g, :, W:] = dot(probs.astype(BF16), ga, NN).astype(BF16)
        r.gkv[g, :, :W] = dot(grad_scores, q, NN).astype(BF16)
        grad_query = gather_diag(dot(grad_scores, key, TN)).astype(BF16)
        r.gq[g] = (grad_query.astype(F32) * (HS**-0.5)).astype(BF16)

    for b in range(2):
        head_landed(ga_at(b), link.ga_m, link.ga_y, b)
        repeat(CG, lambda k: image_back(b * CG + k))
    to_all(r.delta, link.delta)
    to_heads(
        lambda o: send(r.gq.at[:, rows_of(o, LR), :], r.gq_r.at[:, :, own_w], link.gq, me_i, o)
    )
    r.gq_r[:, :, own_w] = r.gq[:, own_l, :]
    rows_pair(r.ffo_p, r.ffo1, link.ffo1, pl.ds(CG, CG), 1)

    def proj_grad(t):
        at = rows_of(t, FT)
        left = r.gkv[...].reshape(G * T, 2 * W)
        r.wa[at, : 2 * W] = dot(r.keys[:, at], left, TN).astype(BF16)
        r.wa[at, 2 * W :] = dot(r.lat_n[:, at], r.gq[...].reshape(R, W), TN).astype(BF16)

    repeat(D // FT, proj_grad)
    scatter_pair(r.wa, r.wa1, RC, link.wa1)
    scatter_twins(r.wa, r.wa1, r.wa2, RC, link.wa1, link.wa2)
    arrived(link.delta, (nh - 1) * G * HN * L * 4)

    def heads_back(o):
        wide = rows_of(o, 2 * W)
        for g in range(G):
            rows = pl.ds(g * KR, KR)
            ga = spread(r.ga_f[g, :, rows_of(o, W)])
            q = spread(r.q_h[o, g * L : (g + 1) * L, :])
            value = r.kv_h[o, rows, W:]
            probs = r.probs_h[o, rows, :]
            grad_probs = dot(value, ga, NT)
            grad_scores = (probs * (grad_probs - r.delta[o, g : g + 1, :])).astype(BF16)
            grad_value = dot(probs.astype(BF16), ga, NN)
            grad_key = dot(grad_scores, q, NN)
            both = jnp.concatenate([grad_key, grad_value], axis=1)
            r.gkv_r[g, :, wide] = both.astype(BF16)

    ffo_twins(0)
    repeat(nh, heads_back)
    scatter_sum(r.wo, r.wo1, r.wo2, RC, link.wo2, r.tmp.at[:RC, : nh * W])
    for k in range(nh):
        r.wo_s[k] = r.tmp[:RC, k * W : (k + 1) * W].astype(BF16)
    out.wo[...] = r.tmp[:RC, own_w]
    to_heads(lambda o: send(r.wo_s.at[o], r.wo_z.at[me_h], link.wo3, me_i, o))

    arrived(link.gq, (nh - 1) * G * LR * W * 2)

    def put(k, at=slice(None)):
        name = list(outs)[k]
        a, b = getattr(out, name).at[at], getattr(dst, name).at[at]
        pltpu.make_async_copy(a, b, out_sems.at[k]).start()

    GB = min(4, G)

    def own_rows(b):
        imgs = pl.ds(GB * b, GB)
        left = r.gkv_r[imgs, :, :].reshape(GB * KR, nh * 2 * W)
        r.tmp[: GB * KR, :D] = dot(left, r.wkv_f[...], NT)
        query = dot(r.gq_r[imgs, :, :].reshape(GB * LR, nh * W), r.wq_f[...], NT)
        for k in range(GB):
            r.tmp[pl.ds(k * KR + SR, LR), :D] += query[k * LR : (k + 1) * LR]

        def read_media(j):
            k = j // NM
            u = r.tmp[at_rows(k * KR + (j % NM) * TILE, TILE, TILE), :D]
            return u, r.hat_m[b * GB * NM + j], r.inv_m[b * GB * NM + j][:, :1]

        def write_media(j, grad):
            out.mg[GB * b + j // NM, rows_of(j % NM, TILE), :] = grad.astype(BF16)

        norm_back_rows(read_media, write_media, GB * SR, gain_m, 0)

        def read_latent(j):
            at = at_rows((j // NL) * KR + SR + (j % NL) * TILE, TILE, TILE)
            return r.tmp[at, :D], r.hat_l[b * GB * NL + j], r.inv_l[b * GB * NL + j][:, :1]

        def write_latent(j, grad):
            g, part = GB * b + j // NL, rows_of(j % NL, TILE)
            out.lg[g, part, :] = (grad + r.gm_o[g, part, :]).astype(BF16)

        norm_back_rows(read_latent, write_latent, GB * LR, gain_l, 2)
        put(1, imgs)
        put(2, imgs)

    for b in range(G // GB):
        own_rows(b)
        if b == 0:
            ffo_twins(1)

    for k in range(6):
        r.vec[k : k + 1, :] = jnp.sum(r.vacc[k], axis=0, keepdims=True)
    r.vec[6:8, :] = jnp.zeros((2, D), F32)

    def block(i):
        return at_rows(lax.div(i * RC, LANES) * LANES, LANES, LANES)

    def vec_step(k):
        o = lax.rem(me_i + 1 + k, ni)
        send(r.vec.at[:, block(o)], r.vec_r.at[me_i], link.vp, o, me_h, times=ni - 1)

    repeat(ni - 1, vec_step)

    scatter_sum(r.wd, r.wd1, r.wd2, FU, link.wd2, out.dn)
    put(6)
    scatter_sum(r.wu, r.wu1, r.wu2, FU, link.wu2, out.up)
    put(5)
    scatter_sum(r.wa, r.wa1, r.wa2, RC, link.wa2, out.wa)
    put(3)
    arrived(link.vp, (ni - 1) * 8 * LANES * 4)
    r.vec_t[...] = r.vec[:, block(me_i)]

    def vec_sum(k):
        r.vec_t[...] += r.vec_r[lax.rem(me_i + 1 + k, ni)]

    repeat(ni - 1, vec_sum)
    to_heads(lambda o: send(r.vec_t, r.vec_z.at[me_h], link.vz, me_i, o))
    for b in range(2):
        imgs = pl.ds(b * CG, CG)
        total = rows_total(r.ffo_p, r.ffo1, r.ffo2, link.ffo2, imgs, CG, b)
        out.lat[imgs] = (r.mid_o[imgs] + total).astype(BF16)
    arrived(link.wo3, (nh - 1) * RC * W * 2)
    total = out.wo[...]
    for o in heads:
        total = total + r.wo_z[o].astype(F32)
    out.wo[...] = total
    arrived(link.vz, (nh - 1) * 8 * LANES * 4)
    total = r.vec_t[...]
    for o in heads:
        total = total + r.vec_z[o]
    out.vec[...] = total
    for k in (0, 4, 7):
        put(k)

    for to in vars(link).values():
        if to.bytes:
            await_bytes(send_sems.at[to.send], to.bytes)
    for k, name in enumerate(outs):
        pltpu.make_async_copy(getattr(out, name), getattr(dst, name), out_sems.at[k]).wait()


def finish(z, *refs):
    n = len(outputs(z)) - 1
    src, dst, buf, turned, in_sems, out_sems = (
        refs[:n], refs[n : n + 9], refs[n + 9 : 2 * n + 9], refs[-3], refs[-2], refs[-1]
    )
    W = z.W
    loads = [pltpu.make_async_copy(src[k], buf[k], in_sems.at[k]) for k in range(n)]
    for copy in loads:
        copy.start()
    stores = []

    def store(ref, k):
        stores.append(pltpu.make_async_copy(ref, dst[k], out_sems.at[k]))
        stores[-1].start()

    lat, mg, lg, wa, wo, up, dn = range(7)
    loads[mg].wait()
    store(buf[mg], 1)
    loads[up].wait()
    store(buf[up], 7)
    loads[dn].wait()
    store(buf[dn], 8)
    loads[lat].wait()
    store(buf[lat], 0)
    loads[lg].wait()
    store(buf[lg], 2)
    loads[wa].wait()
    store(buf[wa].at[:, pl.ds(2 * W, W)], 3)
    store(buf[wa].at[:, pl.ds(0, W)], 4)
    store(buf[wa].at[:, pl.ds(W, W)], 5)
    loads[wo].wait()
    turned[...] = buf[wo][...].T
    store(turned, 6)
    for copy in stores:
        copy.wait()


def body(ni, nh, media, latents, counts, media_gain, media_bias, latent_gain, latent_bias, w_query,
         w_key, w_value, w_out, ff_gain, ff_bias, w_up, w_down, cotangent):
    z = sizes(ni, nh, media, latents, w_query, w_up)
    D, W, RC = z.D, z.W, z.RC
    vm = pl.BlockSpec(memory_space=pltpu.VMEM)
    hbm = pl.BlockSpec(memory_space=pl.ANY)
    dma = pltpu.SemaphoreType.DMA
    outs = list(outputs(z).values())
    rows = [
        v.reshape(1, D)
        for v in (media_gain, media_bias, latent_gain, latent_bias, ff_gain, ff_bias)
    ]
    counted = links(z).values()
    res = pl.pallas_call(
        functools.partial(kernel, z),
        out_shape=[jax.ShapeDtypeStruct(s, d) for s, d in outs],
        in_specs=[pl.BlockSpec(memory_space=pltpu.SMEM)] + [vm] * 6 + [hbm] * 9,
        out_specs=[hbm] * len(outs),
        scratch_shapes=[pltpu.VMEM(s, d) for s, d in (*scratch(z).values(), *outs)]
        + [
            dma((sum(a for a, _ in counted),)),
            dma((sum(b for _, b in counted),)),
            dma((len(LOADS),)),
            dma((len(outs),)),
        ],
        compiler_params=pltpu.CompilerParams(
            collective_id=0, has_side_effects=True, vmem_limit_bytes=67043328
        ),
    )(counts, *rows, media, latents, w_query, w_key, w_value, w_out, w_up, w_down, cotangent)
    last = outs[:3] + [((RC, W), F32)] * 3 + [((W, RC), F32)] + outs[5:7]
    res2 = pl.pallas_call(
        functools.partial(finish, z),
        out_shape=[jax.ShapeDtypeStruct(s, d) for s, d in last],
        in_specs=[hbm] * 7,
        out_specs=[hbm] * 9,
        scratch_shapes=[pltpu.VMEM(s, d) for s, d in outs[:7]]
        + [pltpu.VMEM((W, RC), F32), dma((7,)), dma((9,))],
    )(*res[:7])
    lat_out, media_grad, lat_grad, wq, wk, wv, wo, up, down = res2
    share = D // (ni * nh)
    place = lax.axis_index("img") * nh + lax.axis_index("head")
    vec = lax.dynamic_slice(res[7], (0, lax.rem(place * share, LANES)), (8, share))
    return (
        lat_out, media_grad, lat_grad, vec[0], vec[1], vec[2], vec[3], wq, wk, wv, wo, vec[4],
        vec[5], up, down,
    )


def solution(mesh):
    ni, nh = mesh.shape["img"], mesh.shape["head"]
    both = P(("img", "head"))
    rows = P("img", "head", None)
    return jax.shard_map(
        functools.partial(body, ni, nh),
        mesh=mesh,
        in_specs=(
            P("img", None, None), P("img", None, None), P("img"), P(), P(), P(), P(),
            P(None, "head"), P(None, "head"), P(None, "head"), P("head", None), P(), P(),
            P(("img", "head"), None), P(("img", "head"), None), rows,
        ),
        out_specs=(
            rows, rows, rows, both, both, both, both, P("img", "head"), P("img", "head"),
            P("img", "head"), P("head", "img"), both, both, P(("img", "head"), None),
            P(("img", "head"), None),
        ),
        check_vma=False,
    )
```

```python
import functools
import math
from types import SimpleNamespace

import jax
import jax.numpy as jnp
from jax import lax
from jax.experimental import pallas as pl
from jax.experimental.pallas import tpu as pltpu
from jax.sharding import PartitionSpec as P

HS = 64
EPSILON = 1e-05
LANES = 128
TILE = 16
SIDE = 16
LAG = 5
BF16 = jnp.bfloat16
F32 = jnp.float32
MESH = pl.DeviceIdType.MESH
NN = ((1,), (0,))
NT = ((1,), (1,))
TN = ((0,), (0,))


def dot(a, b, dims):
    return lax.dot_general(a, b, (dims, ((), ())), preferred_element_type=F32)


def fold_rows(x):
    return jnp.sum(x.reshape(x.shape[0] // 8, 8, x.shape[1]), axis=0)


def gelu_parts(hidden):
    normal_cdf = 0.5 * (1.0 + lax.erf(hidden * (1.0 / math.sqrt(2.0))))
    density = jnp.exp(-0.5 * hidden * hidden) * (1.0 / math.sqrt(2.0 * math.pi))
    return (hidden * normal_cdf, normal_cdf + hidden * density)


def sizes(ni, nh, media, latents, w_query, w_up):
    G, S, D = media.shape
    L, W, FU = latents.shape[1], w_query.shape[1], w_up.shape[0]
    Q = min(ni, W // TILE)
    return SimpleNamespace(
        ni=ni, nh=nh, G=G, S=S, D=D, L=L, W=W, FU=FU, T=S + L, SR=S // nh, LR=L // nh, R=G * L,
        FH=ni * FU, RC=D // ni, NK=ni // 2, NH=nh // 2, HN=W // HS, Q=Q, QC=W // Q,
    )


def outputs(z):
    return dict(
        lat=((z.G, z.LR, z.D), BF16),
        mg=((z.G, z.SR, z.D), BF16),
        lg=((z.G, z.LR, z.D), BF16),
        wa=((z.RC, 3 * z.W), F32),
        wo=((z.RC, z.W), F32),
        up=((z.FU, z.D), F32),
        dn=((z.FU, z.D), F32),
        vec=((8, LANES), F32),
    )


def scratch(z):
    G, D, L, W, T, SR, LR, R, FH, RC, NK, NH, FU, nh = (
        z.G, z.D, z.L, z.W, z.T, z.SR, z.LR, z.R, z.FH, z.RC, z.NK, z.NH, z.FU, z.nh
    )
    return dict(
        media_b=((2, z.S, D), BF16),
        media_o=((G, SR, D), BF16),
        lat=((G, L, D), BF16),
        keys=((G * T, D), BF16),
        lat_n=((R, D), BF16),
        wkv_o=((D, 2 * W), BF16),
        wq_o=((D, W), BF16),
        wkv_f=((D, nh * 2 * W), BF16),
        wq_f=((D, nh * W), BF16),
        wout_f=((nh * W, D), BF16),
        up_f=((FH, D), BF16),
        down_f=((FH, D), BF16),
        cot_f=((G, L, D), BF16),
        kv=((G * T, 2 * W), BF16),
        q=((R, W), BF16),
        probs=((G * T, z.HN * L), F32),
        att_f=((G, L, nh * W), BF16),
        mid_o=((G, LR, D), F32),
        hat=((R, D), F32),
        inv=((R, LANES), F32),
        ff_in=((R, D), BF16),
        act=((R, FH), BF16),
        slope=((R, FH), F32),
        gh=((R, FH), BF16),
        tmp=((max(R // 2, 4 * (SR + LR)), max(D, FH)), F32),
        ffo_p=((G, L, D), BF16),
        gm_p=((G, L, D), BF16),
        ffo1=((NH, G, LR, D), BF16),
        ffo2=((NH, G, LR, D), BF16),
        gm1=((NH, G, LR, D), BF16),
        gm2=((NH, G, LR, D), BF16),
        gm_o=((G, LR, D), F32),
        ga_f=((G, L, nh * W), BF16),
        lse=((nh, G, z.HN * L), F32),
        delta=((nh, G, z.HN * L), F32),
        keys_o=((G * (SR + LR), D), BF16),
        kv_h=((nh, G * (SR + LR), 2 * W), BF16),
        q_h=((nh, R, W), BF16),
        probs_h=((nh, G * (SR + LR), z.HN * L), F32),
        gkv=((G, T, 2 * W), BF16),
        gq=((G, L, W), BF16),
        gkv_r=((G, SR + LR, nh * 2 * W), BF16),
        gq_r=((G, LR, nh * W), BF16),
        wu=((FH, D), BF16),
        wd=((FH, D), BF16),
        wo=((D, nh * W), BF16),
        wa=((D, 3 * W), BF16),
        wu1=((NK * FU, D), BF16),
        wd1=((NK * FU, D), BF16),
        wo1=((NK * RC, nh * W), BF16),
        wa1=((NK * RC, 3 * W), BF16),
        wu2=((NK * FU, D), BF16),
        wd2=((NK * FU, D), BF16),
        wo2=((NK * RC, nh * W), BF16),
        wa2=((NK * RC, 3 * W), BF16),
        wo_s=((nh, RC, W), BF16),
        wo_z=((nh, RC, W), BF16),
        hat_m=((G * SR // TILE, TILE, D), F32),
        inv_m=((G * SR // TILE, TILE, LANES), F32),
        hat_l=((G * LR // TILE, TILE, D), F32),
        inv_l=((G * LR // TILE, TILE, LANES), F32),
        vacc=((6, 8, D), F32),
        vec=((8, D), F32),
        vec_r=((z.ni, 8, LANES), F32),
        vec_t=((8, LANES), F32),
        vec_z=((nh, 8, LANES), F32),
    )


def links(z):
    G = z.G
    one = (1, 1)
    return dict(
        wout_z=one, wout_x=one, wout_p=one, wout_y=one, up_p=one, up_x=one, up_y=one, dn_p=one, dn_x=one, dn_y=one,
        kvq_t=one, kvq_m=one, kvq_y=one, kv_p=one, kv_x=one, kv_y=one,
        cot_t=(2, 1), cot_m=(2, 1), cot_y=(2, 1), att_t=(G, 1), att_m=(G, 1), att_y=(G, 1), lse=one,
        delta=one, ga_t=(2, 1), ga_m=(2, 1), ga_y=(2, 1), gq=one,
        ffo1=(2, 1), ffo2=(2, 1), gm1=(2, 1), gm2=(2, 1),
        wu1=one, wu2=one, wd1=one, wd2=one, wo1=one, wo2=one, wo3=one, wa1=one, wa2=one,
        vp=one, vz=one,
    )


LOADS = dict(m0=0, m1=1, w=2, lat=3, ff=4, kvq=5, mo=6)
INS = tuple(
    dict(
        counts=0, g_m=0, b_m=0, g_l=0, b_l=0, g_f=0, b_f=0, media=0, latents=0, w_query=0, w_key=0,
        w_value=0, w_out=0, w_up=0, w_down=0, cot=0,
    )
)


def kernel(z, *refs):
    outs, vmem = outputs(z), scratch(z)
    n_in, n_out = len(INS), len(outs)
    r = SimpleNamespace(
        **dict(zip(INS, refs[:n_in])),
        **dict(zip(vmem, refs[n_in + n_out :])),
    )
    dst = SimpleNamespace(**dict(zip(outs, refs[n_in : n_in + n_out])))
    out = SimpleNamespace(**dict(zip(outs, refs[n_in + n_out + len(vmem) :])))
    recv_sems, send_sems, load_sems, out_sems = refs[-4:]
    G, S, D, L, W, FU, T, SR, LR, R, FH, RC, NK, NH, HN = (
        z.G, z.S, z.D, z.L, z.W, z.FU, z.T, z.SR, z.LR, z.R, z.FH, z.RC, z.NK, z.NH, z.HN
    )
    ni, nh = z.ni, z.nh
    me_i, me_h = lax.axis_index("img"), lax.axis_index("head")
    par, half = lax.rem(me_i, 2), lax.div(me_i, 2)
    mate = me_i + 1 - 2 * par
    par_h, half_h = lax.rem(me_h, 2), lax.div(me_h, 2)
    mate_h = me_h + 1 - 2 * par_h
    halves_h = [lax.rem(half_h + k, NH) for k in range(1, NH)]
    twins_h = [2 * k + par_h for k in halves_h]

    link, n_recv, n_send = {}, 0, 0
    for name, (a, b) in links(z).items():
        link[name] = SimpleNamespace(recv=n_recv, send=n_send, bytes=0)
        n_recv, n_send = n_recv + a, n_send + b
    link = SimpleNamespace(**link)
    ld = SimpleNamespace(**LOADS)

    def size(ref):
        return math.prod(ref.shape) * jnp.dtype(ref.dtype).itemsize

    def await_bytes(sem, nbytes):
        lanes = D
        while nbytes % (2 * lanes * TILE):
            lanes //= 2
        assert lanes >= LANES and nbytes // (2 * lanes) <= G * T
        view = r.keys.at[pl.ds(0, nbytes // (2 * lanes)), pl.ds(0, lanes)]
        pltpu.make_async_copy(view, view, sem).wait()

    def load(src, dst, k):
        pltpu.make_async_copy(src, dst, load_sems.at[k]).start()

    def loaded(k, nbytes):
        await_bytes(load_sems.at[k], nbytes)

    def arrived(to, nbytes, k=0):
        await_bytes(recv_sems.at[to.recv + k], nbytes)

    def push(src, dst, to, img, head, k=0, s=0):
        pltpu.make_async_remote_copy(
            src_ref=src,
            dst_ref=dst,
            send_sem=send_sems.at[to.send + s],
            recv_sem=recv_sems.at[to.recv + k],
            device_id=(img, head),
            device_id_type=MESH,
        ).start()

    def send(src, dst, to, img, head, k=0, times=1):
        push(src, dst, to, img, head, k)
        to.bytes += size(src) * times

    def rows_of(i, n):
        return pl.ds(pl.multiple_of(i * n, n), n)

    def at_rows(start, n, unit):
        return pl.ds(pl.multiple_of(start, unit), n)

    heads = [lax.rem(me_h + d, nh) for d in range(1, nh)]

    def to_heads(f):
        for other in heads:
            f(other)

    def to_twins(f):
        def step(k, c):
            f(lax.rem(half + k, NK) * 2 + par)
            return c

        lax.fori_loop(1, NK, step, 0)

    def head_spread(view, src, twins, pair, k=0, times=1):
        for o in twins_h:
            send(src, view(me_h), twins, me_i, o, k, times)
        send(src, view(me_h), pair, me_i, mate_h, k, times)

    def head_relay(view, twins, onto, k=0, times=1):
        arrived(twins, (NH - 1) * size(view(0)), k)
        for o in twins_h:
            send(view(o), view(o), onto, me_i, mate_h, k, times)

    def head_landed(view, pair, onto, k=0):
        arrived(pair, size(view(0)), k)
        arrived(onto, (NH - 1) * size(view(0)), k)

    def head_pair(view, got, to, k=0, times=1):
        for p in range(NH):
            send(view(2 * p + 1 - par_h), got(p), to, me_i, mate_h, k, times)

    def repeat(n, f):
        if n == 1:
            return f(0)

        def step(k, c):
            f(k)
            return c

        lax.fori_loop(0, n, step, 0)

    load(r.media.at[0], r.media_b.at[0], ld.m0)
    load(r.w_key, r.wkv_o.at[:, pl.ds(0, W)], ld.w)
    load(r.w_value, r.wkv_o.at[:, pl.ds(W, W)], ld.w)
    load(r.w_query, r.wq_o, ld.w)
    load(r.latents, r.lat, ld.lat)
    load(r.media.at[1], r.media_b.at[1], ld.m1)
    barrier = pltpu.get_barrier_semaphore()
    to_heads(
        lambda o: pl.semaphore_signal(
            barrier, inc=1, device_id=(me_i, o), device_id_type=MESH
        )
    )
    repeat(
        ni - 1,
        lambda k: pl.semaphore_signal(
            barrier, inc=1, device_id=(lax.rem(me_i + 1 + k, ni), me_h), device_id_type=MESH
        ),
    )
    pl.semaphore_wait(barrier, nh - 1 + ni - 1)

    Q, QC = z.Q, z.QC
    share = lax.rem(me_i, Q)
    first = me_i - share
    wo_part = at_rows(me_h * W + share * QC, QC, QC)
    to_heads(
        lambda o: send(r.w_out.at[rows_of(share, QC)], r.wout_f.at[wo_part], link.wout_z, me_i, o)
    )
    own_f = rows_of(me_i, FU)
    own_l = rows_of(me_h, LR)

    CR, CG = R // 2, G // 2

    def cot_at(b):
        return lambda o: r.cot_f.at[pl.ds(b * CG, CG), rows_of(o, LR), :]

    def cot_spread(b):
        head_spread(cot_at(b), r.cot.at[pl.ds(b * CG, CG)], link.cot_t, link.cot_m, b)

    cot_spread(0)

    def spread_rows(src, buf, twins, pair):
        to_twins(lambda o: send(src, buf.at[own_f], twins, o, me_h, times=NK - 1))
        send(src, buf.at[own_f], pair, mate, me_h)

    spread_rows(r.w_up, r.up_f, link.up_x, link.up_p)
    load(r.w_out, r.wout_f.at[rows_of(me_h, W)], ld.ff)
    load(r.w_up, r.up_f.at[own_f], ld.ff)
    load(r.w_down, r.down_f.at[own_f], ld.ff)
    load(r.cot, r.cot_f.at[:, own_l, :], ld.ff)
    own_kv = [at_rows(me_h * 2 * W + k * W, W, W) for k in range(2)]
    own_w = rows_of(me_h, W)
    own_c = rows_of(me_i, RC)
    load(r.w_key.at[own_c], r.wkv_f.at[own_c, own_kv[0]], ld.kvq)
    load(r.w_value.at[own_c], r.wkv_f.at[own_c, own_kv[1]], ld.kvq)
    load(r.w_query.at[own_c], r.wq_f.at[own_c, own_w], ld.kvq)
    load(r.media.at[:, rows_of(me_h, SR), :], r.media_o, ld.mo)

    gain_m, bias_m = r.g_m[...], r.b_m[...]
    gain_l, bias_l = r.g_l[...], r.b_l[...]
    gain_f, bias_f = r.g_f[...], r.b_f[...]

    def normalize_rows(read, write, n):
        side = min(n // TILE, SIDE)

        def step(b):
            ks = [b * side + j for j in range(side)]
            mean = [jnp.sum(read(k), axis=-1, keepdims=True) * (1.0 / D) for k in ks]
            var = [
                jnp.sum(jnp.square(read(k) - m), axis=-1, keepdims=True) * (1.0 / D)
                for k, m in zip(ks, mean)
            ]
            inv = [lax.rsqrt(v + EPSILON) for v in var]
            for k, m, i in zip(ks, mean, inv):
                write(k, (read(k) - m) * i, i)

        repeat(n // TILE // side, step)

    def norm_back_rows(read, write, n, gain, k_gain):
        side = min(n // TILE, SIDE)

        def step(b):
            ks = [b * side + j for j in range(side)]
            means = []
            for k in ks:
                u, hat, _ = read(k)
                u = u * gain
                means.append(
                    [jnp.sum(v, axis=-1, keepdims=True) * (1.0 / D) for v in (u, u * hat)]
                )
            gains = biases = jnp.zeros((8, D), F32)
            for k, (one, two) in zip(ks, means):
                u, hat, inv = read(k)
                write(k, inv * (u * gain - one - hat * two))
                gains, biases = gains + fold_rows(u * hat), biases + fold_rows(u)
            r.vacc[k_gain] += gains
            r.vacc[k_gain + 1] += biases

        repeat(n // TILE // side, step)

    lane_head = lax.div(lax.broadcasted_iota(jnp.int32, (L, W), 1), HS)

    def spread(x):
        zero = jnp.zeros_like(x)
        return jnp.concatenate([jnp.where(lane_head == k, x, zero) for k in range(HN)], axis=0)

    def gather_diag(x):
        out = x[:L]
        for k in range(1, HN):
            out = jnp.where(lane_head == k, x[k * L : (k + 1) * L], out)
        return out

    loaded(ld.w, 3 * D * W * 2)
    loaded(ld.lat, G * L * D * 2)

    def row_of(g, n):
        return lax.broadcasted_iota(jnp.int32, (G, n), 0) == g

    def put_row(ref, g, x):
        ref[...] = jnp.where(row_of(g, x.shape[1]), x, ref[...])

    def to_all(ref, to):
        to_heads(lambda o: send(ref.at[me_h], ref.at[me_h], to, me_i, o))

    def kv_at(k):
        return lambda o: r.wkv_f.at[own_c, at_rows(o * 2 * W + k * W, W, W)]

    def kvq_views():
        return (
            (r.w_key, kv_at(0)), (r.w_value, kv_at(1)),
            (r.w_query, lambda o: r.wq_f.at[own_c, rows_of(o, W)]),
        )

    def att_at(g):
        return lambda o: r.att_f.at[g, :, rows_of(o, W)]

    def ga_at(b):
        return lambda o: r.ga_f.at[pl.ds(b * CG, CG), rows_of(o, LR), :]

    r.lse[me_h] = r.delta[me_h] = jnp.zeros((G, HN * L), F32)

    def relay(twins, onto, buf, n):
        arrived(twins, (NK - 1) * size(buf.at[rows_of(0, n)]))
        to_twins(
            lambda o: send(
                buf.at[rows_of(o, n)], buf.at[rows_of(o, n)], onto, mate, me_h, times=NK - 1
            )
        )

    def wout_send(o, s, to, img):
        at = r.wout_f.at[at_rows(o * W + s * QC, QC, QC)]
        send(at, at, to, img, me_h)

    def relay_wout():
        arrived(link.wout_x, (Q // 2 - 1) * (nh - 1) * QC * D * 2)
        for d in range(1, Q // 2):
            s = lax.rem(lax.div(share, 2) + d, Q // 2) * 2 + par
            to_heads(lambda o: wout_send(o, s, link.wout_y, mate))

    def share_wout():
        arrived(link.wout_z, (nh - 1) * QC * D * 2)

        for d in range(1, Q // 2):
            other = lax.rem(lax.div(share, 2) + d, Q // 2) * 2 + par
            to_heads(lambda o: wout_send(o, share, link.wout_x, first + other))
        to_heads(lambda o: wout_send(o, share, link.wout_p, mate))
        spread_rows(r.w_down, r.down_f, link.dn_x, link.dn_p)

    def image(g):
        slot = lax.rem(g, 2)
        for k, sem in enumerate((ld.m0, ld.m1)):

            @pl.when(slot == k)
            def _():
                loaded(sem, S * D * 2)

        def put_media(k, hat, _):
            r.keys[at_rows(g * T + k * TILE, TILE, TILE), :] = (hat * gain_m + bias_m).astype(BF16)

        def put_latent(k, hat, _):
            y = (hat * gain_l + bias_l).astype(BF16)
            r.keys[at_rows(g * T + S + k * TILE, TILE, TILE), :] = y
            r.lat_n[at_rows(g * L + k * TILE, TILE, TILE), :] = y

        normalize_rows(lambda k: r.media_b[slot, rows_of(k, TILE), :].astype(F32), put_media, S)
        normalize_rows(lambda k: r.lat[g, rows_of(k, TILE), :].astype(F32), put_latent, L)
        for k, sem in enumerate((ld.m0, ld.m1)):

            @pl.when((slot == k) & (g + 2 < G))
            def _():
                load(r.media.at[g + 2], r.media_b.at[k], sem)

        rows, lat_rows = rows_of(g, T), rows_of(g, L)
        kv = dot(r.keys[rows, :], r.wkv_o[...], NN).astype(BF16)
        r.kv[rows, :] = kv
        q = (dot(r.lat_n[lat_rows, :], r.wq_o[...], NN) * (HS**-0.5)).astype(BF16)
        r.q[lat_rows, :] = q
        scores = dot(kv[:, :W], spread(q), NT)
        place = lax.broadcasted_iota(jnp.int32, scores.shape, 0)
        scores = jnp.where((place < r.counts[g]) | (place >= S), scores, -1e30)
        top = jnp.max(scores, axis=0, keepdims=True)
        total = jnp.sum(jnp.exp(scores - top), axis=0, keepdims=True)
        lse = top + jnp.log(total)
        put_row(r.lse.at[me_h], g, lse)
        probs = jnp.exp(scores - lse)
        r.probs[rows, :] = probs
        att = gather_diag(dot(probs.astype(BF16), kv[:, W:], TN)).astype(BF16)
        r.att_f[g, :, own_w] = att
        head_spread(att_at(g), r.att_f.at[g, :, own_w], link.att_t, link.att_m, g, G)

        @pl.when(g >= LAG)
        def _():
            head_relay(att_at(g - LAG), link.att_t, link.att_y, g - LAG, G - LAG)

        @pl.when(g == 2)
        def _():
            share_wout()

        @pl.when(g == G - 1)
        def _():
            relay_wout()

        @pl.when(g == G // 2 + 1)
        def _():
            for w, view in kvq_views():
                head_spread(view, w.at[own_c], link.kvq_t, link.kvq_m)

        @pl.when(g == G // 2)
        def _():
            head_relay(cot_at(0), link.cot_t, link.cot_y, 0)

        @pl.when(g == G - 2)
        def _():
            relay(link.up_x, link.up_y, r.up_f, FU)

    repeat(G, image)
    for g in range(G - LAG, G):
        head_relay(att_at(g), link.att_t, link.att_y, g)
    arrived(link.kvq_t, (NH - 1) * 3 * RC * W * 2)
    for _, view in kvq_views():
        for o in twins_h:
            send(view(o), view(o), link.kvq_y, me_i, mate_h)
    to_all(r.lse, link.lse)
    cot_spread(1)
    r.vacc[...] = jnp.zeros_like(r.vacc)

    loaded(ld.ff, (W + 2 * FU + G * LR) * D * 2)
    arrived(link.wout_p, (nh - 1) * QC * D * 2)
    arrived(link.wout_y, (Q // 2 - 1) * (nh - 1) * QC * D * 2)

    def ff_forward(b):
        for k in range(CG):
            head_landed(att_at(b * CG + k), link.att_m, link.att_y, b * CG + k)
        at = rows_of(b, CR)
        imgs = pl.ds(b * CG, CG)
        att = r.att_f[imgs, :, :].reshape(CR, nh * W)
        base = r.lat[imgs, :, :].reshape(CR, D).astype(F32)
        r.tmp[:CR, :D] = dot(att, r.wout_f[...], NN) + base
        for k in range(nh):

            @pl.when(me_h == k)
            def _():
                r.mid_o[imgs] = r.tmp[:CR, :D].reshape(CG, nh, LR, D)[:, k]

        def put_norm(k, hat, inv):
            row = at_rows(b * CR + k * TILE, TILE, TILE)
            r.hat[row, :] = hat
            r.inv[row, :] = jnp.broadcast_to(inv, (TILE, LANES))
            r.ff_in[row, :] = (hat * gain_f + bias_f).astype(BF16)

        normalize_rows(lambda k: r.tmp[rows_of(k, TILE), :D], put_norm, CR)

        @pl.when(b == 0)
        def _():
            arrived(link.up_p, FU * D * 2)
            arrived(link.up_y, (NK - 1) * FU * D * 2)

        r.tmp[:CR, :FH] = dot(r.ff_in[at, :], r.up_f[...], NT)

        def gelu(k):
            row = at_rows(b * CR + k * TILE, TILE, TILE)
            value, slope = gelu_parts(r.tmp[rows_of(k, TILE), :FH])
            r.act[row, :] = value.astype(BF16)
            r.slope[row, :] = slope

        repeat(CR // TILE, gelu)

    repeat(2, ff_forward)

    def share_kvq(o, to, times):
        for buf in (r.wkv_f, r.wq_f):
            send(buf.at[own_c], buf.at[own_c], to, o, me_h, times=times)

    def relay_kvq(o):
        for buf in (r.wkv_f, r.wq_f):
            at = buf.at[rows_of(o, RC)]
            send(at, at, link.kv_y, mate, me_h, times=NK - 1)

    loaded(ld.kvq, 3 * RC * W * 2)
    arrived(link.kvq_m, 3 * RC * W * 2)
    arrived(link.kvq_y, (NH - 1) * 3 * RC * W * 2)
    to_twins(lambda o: share_kvq(o, link.kv_x, NK - 1))
    share_kvq(mate, link.kv_p, 1)

    head_relay(cot_at(1), link.cot_t, link.cot_y, 1)
    relay(link.dn_x, link.dn_y, r.down_f, FU)

    loaded(ld.mo, G * SR * D * 2)

    def keep(hats, invs):
        def put(k, hat, inv):
            hats[k] = hat
            invs[k] = jnp.broadcast_to(inv, (TILE, LANES))

        return put

    NM, NL = SR // TILE, LR // TILE
    normalize_rows(
        lambda k: r.media_o[k // NM, rows_of(k % NM, TILE), :].astype(F32),
        keep(r.hat_m, r.inv_m), G * SR,
    )
    normalize_rows(
        lambda k: r.lat[k // NL, at_rows(me_h * LR + (k % NL) * TILE, TILE, TILE), :].astype(F32),
        keep(r.hat_l, r.inv_l), G * LR,
    )
    KR = SR + LR

    def take_rows(g):
        at = at_rows(g * KR, SR, LR)
        r.keys_o[at, :] = r.keys[at_rows(g * T + me_h * SR, SR, SR), :]
        at = at_rows(g * KR + SR, LR, LR)
        r.keys_o[at, :] = r.keys[at_rows(g * T + S + me_h * LR, LR, LR), :]

    repeat(G, take_rows)
    arrived(link.dn_p, FU * D * 2)
    arrived(link.dn_y, (NK - 1) * FU * D * 2)

    def rows_pair(part, got, to, imgs, k=0, times=1):
        head_pair(
            lambda o: part.at[imgs, rows_of(o, LR), :], lambda p: got.at[p, imgs], to, k, times
        )

    def rows_twins(part, got, got2, to, to2, imgs, n, k=0):
        arrived(to, NH * n * LR * D * 2, k)
        for p, o in zip(halves_h, twins_h):
            at = rows_of(o, LR)
            both = part[imgs, at, :].astype(F32) + got[p, imgs].astype(F32)
            part[imgs, at, :] = both.astype(BF16)
            send(part.at[imgs, at, :], got2.at[half_h, imgs], to2, me_i, o, k)

    def rows_total(part, got, got2, to2, imgs, n, k=0):
        arrived(to2, (NH - 1) * n * LR * D * 2, k)
        x = part[imgs, own_l, :].astype(F32) + got[half_h, imgs].astype(F32)
        for p in halves_h:
            x = x + got2[p, imgs].astype(F32)
        return x

    def ff_out(b):
        out = dot(r.act[rows_of(b, CR), :], r.down_f[...], NN)
        r.ffo_p[pl.ds(b * CG, CG), :, :] = out.astype(BF16).reshape(CG, L, D)

    FIRST = CG // 2
    ff_out(0)
    rows_pair(r.ffo_p, r.ffo1, link.ffo1, pl.ds(0, FIRST), 0)

    def ff_backward(b):
        at, imgs = rows_of(b, CR), pl.ds(b * CG, CG)
        head_landed(cot_at(b), link.cot_m, link.cot_y, b)
        r.tmp[:CR, :FH] = dot(r.cot_f[imgs, :, :].reshape(CR, D), r.down_f[...], NT)

        def slope(k):
            row = at_rows(b * CR + k * TILE, TILE, TILE)
            r.gh[row, :] = (r.tmp[rows_of(k, TILE), :FH] * r.slope[row, :]).astype(BF16)

        repeat(CR // TILE, slope)
        r.tmp[:CR, :D] = dot(r.gh[at, :], r.up_f[...], NN)

        def read(k):
            row = at_rows(b * CR + k * TILE, TILE, TILE)
            return r.tmp[rows_of(k, TILE), :D], r.hat[row, :], r.inv[row, :1]

        def write(k, grad):
            g, part = b * CG + k * TILE // L, rows_of(k % (L // TILE), TILE)
            cot = r.cot_f[g, part, :].astype(F32) * (1.0 / nh)
            r.gm_p[g, part, :] = (grad + cot).astype(BF16)

        norm_back_rows(read, write, CR, gain_f, 4)
        rows_pair(r.gm_p, r.gm1, link.gm1, imgs, b, 2)

    repeat(2, ff_backward)

    def ffo_twins(b):
        imgs = pl.ds(b * CG, CG)
        rows_twins(r.ffo_p, r.ffo1, r.ffo2, link.ffo1, link.ffo2, imgs, CG, b)

    def gm_twins(b):
        imgs = pl.ds(b * CG, CG)
        rows_twins(r.gm_p, r.gm1, r.gm2, link.gm1, link.gm2, imgs, CG, b)

    def gm_total(b):
        imgs = pl.ds(b * CG, CG)
        gm = rows_total(r.gm_p, r.gm1, r.gm2, link.gm2, imgs, CG, b)
        r.gm_o[imgs] = gm
        ga = dot(gm.astype(BF16).reshape(CG * LR, D), r.wout_f[...], NT).astype(BF16)
        r.ga_f[imgs, own_l, :] = ga.reshape(CG, LR, nh * W)
        head_spread(ga_at(b), r.ga_f.at[imgs, own_l, :], link.ga_t, link.ga_m, b)

    ff_out(1)

    def scatter_pair(buf, got, n, to):
        repeat(
            NK,
            lambda k: send(
                buf.at[rows_of(2 * k + 1 - par, n)], got.at[rows_of(k, n)], to, mate, me_h, times=NK
            ),
        )

    def scatter_twins(buf, got, got2, n, to, to2):
        arrived(to, size(got))

        def step(d, c):
            k = lax.rem(half + d, NK)
            mine = rows_of(2 * k + par, n)
            both = buf[mine, :].astype(F32) + got[rows_of(k, n), :].astype(F32)
            buf[mine, :] = both.astype(BF16)
            send(
                buf.at[mine], got2.at[rows_of(half, n)], to2, 2 * k + par, me_h, times=NK - 1
            )
            return c

        lax.fori_loop(1, NK, step, 0)

    def scatter_sum(buf, got, got2, n, to2, total):
        arrived(to2, size(got2) // NK * (NK - 1))
        total[...] = buf[rows_of(me_i, n), :].astype(F32) + got[rows_of(half, n), :].astype(F32)

        def step(d, c):
            total[...] += got2[rows_of(lax.rem(half + d, NK), n), :].astype(F32)
            return c

        lax.fori_loop(1, NK, step, 0)

    FT = 2 * LANES

    def out_grad(t):
        at = rows_of(t, FT)
        left = r.gm_p[:, :, at].reshape(R, FT)
        r.wo[at, :] = dot(left, r.att_f[...].reshape(R, nh * W), TN).astype(BF16)

    repeat(D // FT, out_grad)
    scatter_pair(r.wo, r.wo1, RC, link.wo1)

    def down_grad(t):
        at = rows_of(t, FT)
        r.wd[at, :] = dot(r.act[:, at], r.cot_f[...].reshape(R, D), TN).astype(BF16)

    repeat(FH // FT, down_grad)
    scatter_pair(r.wd, r.wd1, FU, link.wd1)
    gm_twins(0)
    scatter_twins(r.wo, r.wo1, r.wo2, RC, link.wo1, link.wo2)

    def up_grad(t):
        at = rows_of(t, FT)
        r.wu[at, :] = dot(r.gh[:, at], r.ff_in[...], TN).astype(BF16)

    repeat(FH // FT, up_grad)
    scatter_pair(r.wu, r.wu1, FU, link.wu1)

    gm_twins(1)
    arrived(link.kv_x, (NK - 1) * 3 * nh * RC * W * 2)
    to_twins(relay_kvq)
    scatter_twins(r.wd, r.wd1, r.wd2, FU, link.wd1, link.wd2)
    gm_total(0)
    scatter_twins(r.wu, r.wu1, r.wu2, FU, link.wu1, link.wu2)

    arrived(link.lse, (nh - 1) * G * HN * L * 4)
    arrived(link.kv_p, 3 * nh * RC * W * 2)
    arrived(link.kv_y, (NK - 1) * 3 * nh * RC * W * 2)

    def heads_project(o):
        r.kv_h[o] = dot(r.keys_o[...], r.wkv_f[:, rows_of(o, 2 * W)], NN).astype(BF16)
        q_all = dot(r.lat_n[...], r.wq_f[:, rows_of(o, W)], NN) * (HS**-0.5)
        r.q_h[o] = q_all.astype(BF16)
        for g in range(G):
            rows = pl.ds(g * KR, KR)
            q = spread(r.q_h[o, g * L : (g + 1) * L, :])
            scores = dot(r.kv_h[o, rows, :W], q, NT)
            place = lax.broadcasted_iota(jnp.int32, scores.shape, 0)
            valid = (place + me_h * SR < r.counts[g]) | (place >= SR)
            scores = jnp.where(valid, scores, -1e30)
            r.probs_h[o, rows, :] = jnp.exp(scores - r.lse[o, g : g + 1, :])

    repeat(nh, heads_project)
    gm_total(1)
    head_relay(ga_at(0), link.ga_t, link.ga_y, 0)

    head_relay(ga_at(1), link.ga_t, link.ga_y, 1)
    rows_pair(r.ffo_p, r.ffo1, link.ffo1, pl.ds(FIRST, CG - FIRST), 0)

    def image_back(g):
        rows, lat_rows = rows_of(g, T), rows_of(g, L)
        ga = spread(r.ga_f[g, :, own_w])
        q = spread(r.q[lat_rows, :])
        key, value = r.kv[rows, :W], r.kv[rows, W:]
        probs = r.probs[rows, :]
        grad_probs = dot(value, ga, NT)
        delta = jnp.sum(probs * grad_probs, axis=0, keepdims=True)
        put_row(r.delta.at[me_h], g, delta)
        grad_scores = (probs * (grad_probs - delta)).astype(BF16)
        r.gkv[g, :, W:] = dot(probs.astype(BF16), ga, NN).astype(BF16)
        r.gkv[g, :, :W] = dot(grad_scores, q, NN).astype(BF16)
        grad_query = gather_diag(dot(grad_scores, key, TN)).astype(BF16)
        r.gq[g] = (grad_query.astype(F32) * (HS**-0.5)).astype(BF16)

    for b in range(2):
        head_landed(ga_at(b), link.ga_m, link.ga_y, b)
        repeat(CG, lambda k: image_back(b * CG + k))
    to_all(r.delta, link.delta)
    to_heads(
        lambda o: send(r.gq.at[:, rows_of(o, LR), :], r.gq_r.at[:, :, own_w], link.gq, me_i, o)
    )
    r.gq_r[:, :, own_w] = r.gq[:, own_l, :]
    rows_pair(r.ffo_p, r.ffo1, link.ffo1, pl.ds(CG, CG), 1)

    def proj_grad(t):
        at = rows_of(t, FT)
        left = r.gkv[...].reshape(G * T, 2 * W)
        r.wa[at, : 2 * W] = dot(r.keys[:, at], left, TN).astype(BF16)
        r.wa[at, 2 * W :] = dot(r.lat_n[:, at], r.gq[...].reshape(R, W), TN).astype(BF16)

    repeat(D // FT, proj_grad)
    scatter_pair(r.wa, r.wa1, RC, link.wa1)
    scatter_twins(r.wa, r.wa1, r.wa2, RC, link.wa1, link.wa2)
    arrived(link.delta, (nh - 1) * G * HN * L * 4)

    def heads_back(o):
        wide = rows_of(o, 2 * W)
        for g in range(G):
            rows = pl.ds(g * KR, KR)
            ga = spread(r.ga_f[g, :, rows_of(o, W)])
            q = spread(r.q_h[o, g * L : (g + 1) * L, :])
            value = r.kv_h[o, rows, W:]
            probs = r.probs_h[o, rows, :]
            grad_probs = dot(value, ga, NT)
            grad_scores = (probs * (grad_probs - r.delta[o, g : g + 1, :])).astype(BF16)
            grad_value = dot(probs.astype(BF16), ga, NN)
            grad_key = dot(grad_scores, q, NN)
            both = jnp.concatenate([grad_key, grad_value], axis=1)
            r.gkv_r[g, :, wide] = both.astype(BF16)

    ffo_twins(0)
    repeat(nh, heads_back)
    scatter_sum(r.wo, r.wo1, r.wo2, RC, link.wo2, r.tmp.at[:RC, : nh * W])
    for k in range(nh):
        r.wo_s[k] = r.tmp[:RC, k * W : (k + 1) * W].astype(BF16)
    out.wo[...] = r.tmp[:RC, own_w]
    to_heads(lambda o: send(r.wo_s.at[o], r.wo_z.at[me_h], link.wo3, me_i, o))

    arrived(link.gq, (nh - 1) * G * LR * W * 2)

    def put(k, at=slice(None)):
        name = list(outs)[k]
        a, b = getattr(out, name).at[at], getattr(dst, name).at[at]
        pltpu.make_async_copy(a, b, out_sems.at[k]).start()

    GB = min(4, G)

    def own_rows(b):
        imgs = pl.ds(GB * b, GB)
        left = r.gkv_r[imgs, :, :].reshape(GB * KR, nh * 2 * W)
        r.tmp[: GB * KR, :D] = dot(left, r.wkv_f[...], NT)
        query = dot(r.gq_r[imgs, :, :].reshape(GB * LR, nh * W), r.wq_f[...], NT)
        for k in range(GB):
            r.tmp[pl.ds(k * KR + SR, LR), :D] += query[k * LR : (k + 1) * LR]

        def read_media(j):
            k = j // NM
            u = r.tmp[at_rows(k * KR + (j % NM) * TILE, TILE, TILE), :D]
            return u, r.hat_m[b * GB * NM + j], r.inv_m[b * GB * NM + j][:, :1]

        def write_media(j, grad):
            out.mg[GB * b + j // NM, rows_of(j % NM, TILE), :] = grad.astype(BF16)

        norm_back_rows(read_media, write_media, GB * SR, gain_m, 0)

        def read_latent(j):
            at = at_rows((j // NL) * KR + SR + (j % NL) * TILE, TILE, TILE)
            return r.tmp[at, :D], r.hat_l[b * GB * NL + j], r.inv_l[b * GB * NL + j][:, :1]

        def write_latent(j, grad):
            g, part = GB * b + j // NL, rows_of(j % NL, TILE)
            out.lg[g, part, :] = (grad + r.gm_o[g, part, :]).astype(BF16)

        norm_back_rows(read_latent, write_latent, GB * LR, gain_l, 2)
        put(1, imgs)
        put(2, imgs)

    for b in range(G // GB):
        own_rows(b)
        if b == 0:
            ffo_twins(1)

    for k in range(6):
        r.vec[k : k + 1, :] = jnp.sum(r.vacc[k], axis=0, keepdims=True)
    r.vec[6:8, :] = jnp.zeros((2, D), F32)

    def block(i):
        return at_rows(lax.div(i * RC, LANES) * LANES, LANES, LANES)

    def vec_step(k):
        o = lax.rem(me_i + 1 + k, ni)
        send(r.vec.at[:, block(o)], r.vec_r.at[me_i], link.vp, o, me_h, times=ni - 1)

    repeat(ni - 1, vec_step)

    scatter_sum(r.wd, r.wd1, r.wd2, FU, link.wd2, out.dn)
    put(6)
    scatter_sum(r.wu, r.wu1, r.wu2, FU, link.wu2, out.up)
    put(5)
    scatter_sum(r.wa, r.wa1, r.wa2, RC, link.wa2, out.wa)
    put(3)
    arrived(link.vp, (ni - 1) * 8 * LANES * 4)
    r.vec_t[...] = r.vec[:, block(me_i)]

    def vec_sum(k):
        r.vec_t[...] += r.vec_r[lax.rem(me_i + 1 + k, ni)]

    repeat(ni - 1, vec_sum)
    to_heads(lambda o: send(r.vec_t, r.vec_z.at[me_h], link.vz, me_i, o))
    for b in range(2):
        imgs = pl.ds(b * CG, CG)
        total = rows_total(r.ffo_p, r.ffo1, r.ffo2, link.ffo2, imgs, CG, b)
        out.lat[imgs] = (r.mid_o[imgs] + total).astype(BF16)
    arrived(link.wo3, (nh - 1) * RC * W * 2)
    total = out.wo[...]
    for o in heads:
        total = total + r.wo_z[o].astype(F32)
    out.wo[...] = total
    arrived(link.vz, (nh - 1) * 8 * LANES * 4)
    total = r.vec_t[...]
    for o in heads:
        total = total + r.vec_z[o]
    out.vec[...] = total
    for k in (0, 4, 7):
        put(k)

    for to in vars(link).values():
        if to.bytes:
            await_bytes(send_sems.at[to.send], to.bytes)
    for k, name in enumerate(outs):
        pltpu.make_async_copy(getattr(out, name), getattr(dst, name), out_sems.at[k]).wait()


def finish(z, *refs):
    n, m = len(outputs(z)), 15
    src, dst, buf = refs[:n], refs[n : n + m], refs[n + m : 2 * n + m]
    turned, parts, in_sems, out_sems = refs[-4:]
    W = z.W
    loads = [pltpu.make_async_copy(src[k], buf[k], in_sems.at[k]) for k in range(n)]
    for copy in loads:
        copy.start()
    stores = []

    def store(ref, k):
        stores.append(pltpu.make_async_copy(ref, dst[k], out_sems.at[k]))
        stores[-1].start()

    lat, mg, lg, wa, wo, up, dn, vec = range(n)
    loads[mg].wait()
    store(buf[mg], 1)
    loads[up].wait()
    store(buf[up], 7)
    loads[dn].wait()
    store(buf[dn], 8)
    loads[lat].wait()
    store(buf[lat], 0)
    loads[lg].wait()
    store(buf[lg], 2)
    loads[wa].wait()
    store(buf[wa].at[:, pl.ds(2 * W, W)], 3)
    store(buf[wa].at[:, pl.ds(0, W)], 4)
    store(buf[wa].at[:, pl.ds(W, W)], 5)
    loads[wo].wait()
    turned[...] = buf[wo][...].T
    store(turned, 6)
    share = z.D // (z.ni * z.nh)
    place = lax.axis_index("img") * z.nh + lax.axis_index("head")
    loads[vec].wait()
    ahead = lax.rem(LANES - lax.rem(place * share, LANES), LANES)
    parts[...] = pltpu.roll(buf[vec][...], ahead, 1)[:, :share]
    for k in range(6):
        store(parts.at[pl.ds(k, 1)], 9 + k)
    for copy in stores:
        copy.wait()


def body(ni, nh, media, latents, counts, media_gain, media_bias, latent_gain, latent_bias, w_query,
         w_key, w_value, w_out, ff_gain, ff_bias, w_up, w_down, cotangent):
    z = sizes(ni, nh, media, latents, w_query, w_up)
    D, W, RC = z.D, z.W, z.RC
    vm = pl.BlockSpec(memory_space=pltpu.VMEM)
    hbm = pl.BlockSpec(memory_space=pl.ANY)
    dma = pltpu.SemaphoreType.DMA
    outs = list(outputs(z).values())
    rows = [
        v.reshape(1, D)
        for v in (media_gain, media_bias, latent_gain, latent_bias, ff_gain, ff_bias)
    ]
    counted = links(z).values()
    res = pl.pallas_call(
        functools.partial(kernel, z),
        out_shape=[jax.ShapeDtypeStruct(s, d) for s, d in outs],
        in_specs=[pl.BlockSpec(memory_space=pltpu.SMEM)] + [vm] * 6 + [hbm] * 9,
        out_specs=[hbm] * len(outs),
        scratch_shapes=[pltpu.VMEM(s, d) for s, d in (*scratch(z).values(), *outs)]
        + [
            dma((sum(a for a, _ in counted),)),
            dma((sum(b for _, b in counted),)),
            dma((len(LOADS),)),
            dma((len(outs),)),
        ],
        compiler_params=pltpu.CompilerParams(
            collective_id=0, has_side_effects=True, vmem_limit_bytes=67043328
        ),
    )(counts, *rows, media, latents, w_query, w_key, w_value, w_out, w_up, w_down, cotangent)
    share = D // (ni * nh)
    last = outs[:3] + [((RC, W), F32)] * 3 + [((W, RC), F32)] + outs[5:7] + [((1, share), F32)] * 6
    n, m = len(outs), len(last)
    res2 = pl.pallas_call(
        functools.partial(finish, z),
        out_shape=[jax.ShapeDtypeStruct(s, d) for s, d in last],
        in_specs=[hbm] * n,
        out_specs=[hbm] * m,
        scratch_shapes=[pltpu.VMEM(s, d) for s, d in outs]
        + [pltpu.VMEM((W, RC), F32), pltpu.VMEM((8, share), F32), dma((n,)), dma((m,))],
    )(*res)
    lat_out, media_grad, lat_grad, wq, wk, wv, wo, up, down = res2[:9]
    vec = [v.reshape(share) for v in res2[9:]]
    return (
        lat_out, media_grad, lat_grad, vec[0], vec[1], vec[2], vec[3], wq, wk, wv, wo, vec[4],
        vec[5], up, down,
    )


def solution(mesh):
    ni, nh = mesh.shape["img"], mesh.shape["head"]
    both = P(("img", "head"))
    rows = P("img", "head", None)
    return jax.shard_map(
        functools.partial(body, ni, nh),
        mesh=mesh,
        in_specs=(
            P("img", None, None), P("img", None, None), P("img"), P(), P(), P(), P(),
            P(None, "head"), P(None, "head"), P(None, "head"), P("head", None), P(), P(),
            P(("img", "head"), None), P(("img", "head"), None), rows,
        ),
        out_specs=(
            rows, rows, rows, both, both, both, both, P("img", "head"), P("img", "head"),
            P("img", "head"), P("head", "img"), both, both, P(("img", "head"), None),
            P(("img", "head"), None),
        ),
        check_vma=False,
    )
```
